32 devices in a mesh: bucket: 4 (over y, x), dp: 8 (over z, core).
Axes of the slice: x: 2, y: 2, z: 4, core: 2. Of those that a mesh axis runs over, the one named last changes fastest.
Arguments:
- token_ids: int32 [32, 1024], P(('bucket', 'dp')), may hold values from 0 to 11263
- segment_ids: int32 [32, 1024], P(('bucket', 'dp')), may hold values from 0 to 17, as said below
- live: int32 [32, 1024], P(('bucket', 'dp')), may hold values from 0 to 1, as said below
- timesteps: int32 [32, 1024], P(('bucket', 'dp')), may hold values from 0 to 1999, as said below
- noise: float32 [32, 1024, 128], P(('bucket', 'dp')), may hold values from -6 to 6
- embedding: float32 [11264, 128], P(('bucket', 'dp')), may hold values from -0.8 to 0.8
- embedding_moment: float32 [11264, 128], P(('bucket', 'dp')), may hold values from -2.1632466e-06 to 2.1632466e-06
- embedding_second: float32 [11264, 128], P(('bucket', 'dp')), may hold values from 1.1280114e-12 to 1.8048183e-11
- up_weight: float32 [128, 768], P(None, ('bucket', 'dp')), may hold values from -0.5 to 0.5
- up_moment: float32 [128, 768], P(None, ('bucket', 'dp')), may hold values from -2.1632466e-06 to 2.1632466e-06
- up_second: float32 [128, 768], P(None, ('bucket', 'dp')), may hold values from 1.1280114e-12 to 1.8048183e-11
- time_weight: float32 [768, 768], P(None, ('bucket', 'dp')), may hold values from -0.21875 to 0.21875
- time_moment: float32 [768, 768], P(None, ('bucket', 'dp')), may hold values from -2.1632466e-06 to 2.1632466e-06
- time_second: float32 [768, 768], P(None, ('bucket', 'dp')), may hold values from 1.1280114e-12 to 1.8048183e-11
- qkv_weight: float32 [768, 2304], P(('bucket', 'dp')), may hold values from -0.21875 to 0.21875
- qkv_moment: float32 [768, 2304], P(('bucket', 'dp')), may hold values from -2.1632466e-06 to 2.1632466e-06
- qkv_second: float32 [768, 2304], P(('bucket', 'dp')), may hold values from 1.1280114e-12 to 1.8048183e-11
- out_weight: float32 [768, 768], P(None, ('bucket', 'dp')), may hold values from -0.875 to 0.875
- out_moment: float32 [768, 768], P(None, ('bucket', 'dp')), may hold values from -2.1632466e-06 to 2.1632466e-06
- out_second: float32 [768, 768], P(None, ('bucket', 'dp')), may hold values from 1.1280114e-12 to 1.8048183e-11
- fc_weight: float32 [768, 3072], P(('bucket', 'dp')), may hold values from -0.21875 to 0.21875
- fc_moment: float32 [768, 3072], P(('bucket', 'dp')), may hold values from -2.1632466e-06 to 2.1632466e-06
- fc_second: float32 [768, 3072], P(('bucket', 'dp')), may hold values from 1.1280114e-12 to 1.8048183e-11
- proj_weight: float32 [3072, 768], P(None, ('bucket', 'dp')), may hold values from -0.109375 to 0.109375
- proj_moment: float32 [3072, 768], P(None, ('bucket', 'dp')), may hold values from -2.1632466e-06 to 2.1632466e-06
- proj_second: float32 [3072, 768], P(None, ('bucket', 'dp')), may hold values from 1.1280114e-12 to 1.8048183e-11
- down_weight: float32 [768, 128], P(('bucket', 'dp')), may hold values from -0.21875 to 0.21875
- down_moment: float32 [768, 128], P(('bucket', 'dp')), may hold values from -2.1632466e-06 to 2.1632466e-06
- down_second: float32 [768, 128], P(('bucket', 'dp')), may hold values from 1.1280114e-12 to 1.8048183e-11
- norm_gains: float32 [3, 768], P(None, ('bucket', 'dp')), may hold values from 0.35 to 2.6
- gains_moment: float32 [3, 768], P(None, ('bucket', 'dp')), may hold values from -2.1632466e-06 to 2.1632466e-06
- gains_second: float32 [3, 768], P(None, ('bucket', 'dp')), may hold values from 1.1280114e-12 to 1.8048183e-11
Outputs:
- loss: float32 [], replicated
- grad_norm: float32 [], replicated
- embedding_moment_new: float32 [11264, 128], P(('bucket', 'dp'))
- embedding_second_new: float32 [11264, 128], P(('bucket', 'dp'))
- embedding_new: float32 [11264, 128], P(('bucket', 'dp'))
- up_moment_new: float32 [128, 768], P(None, ('bucket', 'dp'))
- up_second_new: float32 [128, 768], P(None, ('bucket', 'dp'))
- up_weight_new: float32 [128, 768], P(None, ('bucket', 'dp'))
- time_moment_new: float32 [768, 768], P(None, ('bucket', 'dp'))
- time_second_new: float32 [768, 768], P(None, ('bucket', 'dp'))
- time_weight_new: float32 [768, 768], P(None, ('bucket', 'dp'))
- qkv_moment_new: float32 [768, 2304], P(('bucket', 'dp'))
- qkv_second_new: float32 [768, 2304], P(('bucket', 'dp'))
- qkv_weight_new: float32 [768, 2304], P(('bucket', 'dp'))
- out_moment_new: float32 [768, 768], P(None, ('bucket', 'dp'))
- out_second_new: float32 [768, 768], P(None, ('bucket', 'dp'))
- out_weight_new: float32 [768, 768], P(None, ('bucket', 'dp'))
- fc_moment_new: float32 [768, 3072], P(('bucket', 'dp'))
- fc_second_new: float32 [768, 3072], P(('bucket', 'dp'))
- fc_weight_new: float32 [768, 3072], P(('bucket', 'dp'))
- proj_moment_new: float32 [3072, 768], P(None, ('bucket', 'dp'))
- proj_second_new: float32 [3072, 768], P(None, ('bucket', 'dp'))
- proj_weight_new: float32 [3072, 768], P(None, ('bucket', 'dp'))
- down_moment_new: float32 [768, 128], P(('bucket', 'dp'))
- down_second_new: float32 [768, 128], P(('bucket', 'dp'))
- down_weight_new: float32 [768, 128], P(('bucket', 'dp'))
- gains_moment_new: float32 [3, 768], P(None, ('bucket', 'dp'))
- gains_second_new: float32 [3, 768], P(None, ('bucket', 'dp'))
- norm_gains_new: float32 [3, 768], P(None, ('bucket', 'dp'))
The draws below stay inside these ranges and needn't reach their ends.
Inputs may be any that keep to these rules, and one draw needn't show every extreme that they name: `segment_ids`: positions of a row that share a number form one item; a row's first item has 64 positions or more, its later items 64 or fewer; padding positions carry 1024 // 64 + 1. `live`: 1 on a row's leading positions, 0 on its padding tail; every row has 64 live positions or more. `timesteps`: equal within an item; rows held by devices whose index along bucket is b have timesteps from b * 500 up to (b+1) * 500 - 1.
All inputs are finite; a program needn't handle non-finite values.
Results may differ from the reference program's by a relative error of at most 0.003.
The reference program's roundings to bfloat16 on the way count: a program that leaves them out, or rounds other values in their place, can miss the bound.
Values may be sent and summed in bfloat16 or wider, within the bound.
No kernel may reach another device: no remote copies, remote signals or barrier semaphores. Data moves between devices by JAX's collectives and lax.ppermute only.
A program may use at most 256 MiB of HBM per device.

```python
import math
from functools import partial
import jax
import jax.numpy as jnp
import numpy as np
from jax import lax

D = 768
HEADS = 12
HEAD = 64
FF = 3072
EMB = 128
VOCAB = 11264
ROW_LEN = 1024
ITEM = 64
STEPS_T = 2000
ADAM_STEP = 10
BUCKETS = 4
ROWS = 32
PARAMS = 9308416


def packing(key):
    base_key = jax.random.fold_in(key, 11)
    key_trim, key_first, key_steps = jax.random.split(base_key, 3)
    row_index = jnp.arange(ROWS, dtype=jnp.int32)[:, None]
    places = jnp.arange(ROW_LEN, dtype=jnp.int32)[None, :]
    trim_len = jax.random.randint(key_trim, (ROWS, 1), 0, ITEM, dtype=jnp.int32)
    live_len = ROW_LEN // 3 + 2 * ROW_LEN // 3 * row_index // max(ROWS - 1, 1) - trim_len
    live_len = jnp.maximum(live_len, ITEM)
    room_len = jnp.maximum(live_len // 2 - ITEM, 0) + 1
    first_len = ITEM + jax.random.randint(key_first, (ROWS, 1), 0, room_len, dtype=jnp.int32)
    item_ids = jnp.where(places < first_len, 0, 1 + (places - first_len) // ITEM)
    pad_id = ROW_LEN // ITEM + 1
    live_mask = places < live_len
    segments = jnp.where(live_mask, item_ids, pad_id)
    step_span = STEPS_T // BUCKETS
    group_id = row_index // (ROWS // BUCKETS)
    step_table = jax.random.randint(key_steps, (ROWS, pad_id + 1), 0, step_span, dtype=jnp.int32) + group_id * step_span
    step_rows = jnp.take_along_axis(step_table, segments, 1)
    step_rows = jnp.where((row_index == 0) & (segments == 0), 0, step_rows)
    step_rows = jnp.where((row_index == ROWS - 1) & (segments == 0), STEPS_T - 1, step_rows)
    return (segments, live_mask.astype(jnp.int32), step_rows)


def draw_segment_ids(key, part):
    return packing(key)[0]


def draw_live(key, part):
    return packing(key)[1]


def draw_timesteps(key, part):
    return packing(key)[2]


def draw_norm_gains(key, part):
    own_key = jax.random.fold_in(key, 23)
    ramp = jnp.arange(D, dtype=jnp.float32) / (D - 1)
    base_level, rise_size, jitter = (0.6, 0.9, 0.2)
    factors = jax.random.uniform(own_key, (3, D), jnp.float32, 1.0 - jitter, 1.0 + jitter)
    return ((base_level + rise_size * ramp)[None, :] * factors).astype(jnp.float32)


def set_ends(drawn, stream_key, least, high):
    spot = [jax.random.randint(jax.random.fold_in(stream_key, axis), (), 0, length) for axis, length in enumerate(drawn.shape)]
    widest = drawn.shape.index(max(drawn.shape))
    beside = spot[:widest] + [(spot[widest] + 1) % drawn.shape[widest]] + spot[widest + 1:]
    return drawn.at[tuple(spot)].set(least).at[tuple(beside)].set(high)


def level_of(stream_key, shape, cuts, least, largest):
    factor_of = 1.0
    for axis_at, parts in cuts:
        steps = jax.random.uniform(jax.random.fold_in(jax.random.fold_in(stream_key, 6), axis_at), (parts,), jnp.float32, least / len(cuts), largest / len(cuts))
        factor_of = factor_of * jnp.repeat(jnp.exp(steps), shape[axis_at] // parts).reshape((-1,) + (1,) * (len(shape) - 1 - axis_at))
    return factor_of


def rank_table(count, skew):
    weights = [(1 << 20) // math.isqrt(standing ** skew) + 1 for standing in range(1, count + 1)]
    scale = 1 + sum(weights) // (1 << 30)
    return np.cumsum(np.array([max(1, weight // scale) for weight in weights]))


def ranked(rng, extent, amount, slope):
    table = rank_table(amount, slope)
    pick = jax.random.randint(jax.random.fold_in(rng, 1), extent, 0, int(table[amount - 1]))
    standing = jnp.searchsorted(jnp.asarray(table, jnp.int32), pick, side="right")
    return jax.random.permutation(jax.random.fold_in(rng, 2), amount)[standing].astype(jnp.int32)


def normal_values(rng, shape, scale, bound, pieces=(), held_as=jnp.bfloat16):
    array = scale * jax.random.normal(rng, shape, jnp.float32)
    if pieces:
        array = array * level_of(rng, shape, pieces, -0.22, 0.18)
    return jnp.clip(array, -bound, bound).astype(held_as)


def setup_inputs(seed: int = 0) -> dict:
    keys = jax.random.split(jax.random.key(seed), 33)
    token_ids = set_ends(ranked(keys[0], (ROWS, ROW_LEN), VOCAB, 2), jax.random.fold_in(keys[0], 3), 0, VOCAB - 1).astype(jnp.int32)
    segment_ids = draw_segment_ids(jax.random.fold_in(keys[32], 71), 0)
    live = draw_live(jax.random.fold_in(keys[32], 71), 0)
    timesteps = draw_timesteps(jax.random.fold_in(keys[32], 71), 0)
    noise = normal_values(keys[4], (ROWS, ROW_LEN, EMB), 1.0, 6.0, ((0, 32),), jnp.float32)
    embedding = normal_values(keys[5], (VOCAB, EMB), 0.13, 0.8, ((0, 32),), jnp.float32)
    embedding_moment = normal_values(keys[6], (VOCAB, EMB), (0.0022 / PARAMS ** 0.5), 2.163246563213761e-06, ((0, 32),), jnp.float32)
    embedding_second = jnp.clip(jnp.exp(math.log(1.8048182739982543e-11) - 2.7725887 * jax.random.uniform(keys[7], (VOCAB, EMB), jnp.float32) ** level_of(keys[7], (VOCAB, EMB), ((0, 32),), -0.2, 0.2)), 1.128011421248909e-12, 1.8048182739982543e-11)
    up_weight = normal_values(keys[8], (EMB, D), EMB ** -0.5, 0.5, ((1, 32),), jnp.float32)
    up_moment = normal_values(keys[9], (EMB, D), (0.0022 / PARAMS ** 0.5), 2.163246563213761e-06, ((1, 32),), jnp.float32)
    up_second = jnp.clip(jnp.exp(math.log(1.8048182739982543e-11) - 2.7725887 * jax.random.uniform(keys[10], (EMB, D), jnp.float32) ** level_of(keys[10], (EMB, D), ((1, 32),), -0.2, 0.2)), 1.128011421248909e-12, 1.8048182739982543e-11)
    time_weight = normal_values(keys[11], (D, D), D ** -0.5, 0.21875, ((1, 32),), jnp.float32)
    time_moment = normal_values(keys[12], (D, D), (0.0022 / PARAMS ** 0.5), 2.163246563213761e-06, ((1, 32),), jnp.float32)
    time_second = jnp.clip(jnp.exp(math.log(1.8048182739982543e-11) - 2.7725887 * jax.random.uniform(keys[13], (D, D), jnp.float32) ** level_of(keys[13], (D, D), ((1, 32),), -0.2, 0.2)), 1.128011421248909e-12, 1.8048182739982543e-11)
    qkv_weight = normal_values(keys[14], (D, 3 * D), D ** -0.5, 0.21875, ((0, 32),), jnp.float32)
    qkv_moment = normal_values(keys[15], (D, 3 * D), (0.0022 / PARAMS ** 0.5), 2.163246563213761e-06, ((0, 32),), jnp.float32)
    qkv_second = jnp.clip(jnp.exp(math.log(1.8048182739982543e-11) - 2.7725887 * jax.random.uniform(keys[16], (D, 3 * D), jnp.float32) ** level_of(keys[16], (D, 3 * D), ((0, 32),), -0.2, 0.2)), 1.128011421248909e-12, 1.8048182739982543e-11)
    out_weight = normal_values(keys[17], (D, D), (D // 16) ** -0.5, 0.875, ((1, 32),), jnp.float32)
    out_moment = normal_values(keys[18], (D, D), (0.0022 / PARAMS ** 0.5), 2.163246563213761e-06, ((1, 32),), jnp.float32)
    out_second = jnp.clip(jnp.exp(math.log(1.8048182739982543e-11) - 2.7725887 * jax.random.uniform(keys[19], (D, D), jnp.float32) ** level_of(keys[19], (D, D), ((1, 32),), -0.2, 0.2)), 1.128011421248909e-12, 1.8048182739982543e-11)
    fc_weight = normal_values(keys[20], (D, FF), D ** -0.5, 0.21875, ((0, 32),), jnp.float32)
    fc_moment = normal_values(keys[21], (D, FF), (0.0022 / PARAMS ** 0.5), 2.163246563213761e-06, ((0, 32),), jnp.float32)
    fc_second = jnp.clip(jnp.exp(math.log(1.8048182739982543e-11) - 2.7725887 * jax.random.uniform(keys[22], (D, FF), jnp.float32) ** level_of(keys[22], (D, FF), ((0, 32),), -0.2, 0.2)), 1.128011421248909e-12, 1.8048182739982543e-11)
    proj_weight = normal_values(keys[23], (FF, D), FF ** -0.5, 0.109375, ((1, 32),), jnp.float32)
    proj_moment = normal_values(keys[24], (FF, D), (0.0022 / PARAMS ** 0.5), 2.163246563213761e-06, ((1, 32),), jnp.float32)
    proj_second = jnp.clip(jnp.exp(math.log(1.8048182739982543e-11) - 2.7725887 * jax.random.uniform(keys[25], (FF, D), jnp.float32) ** level_of(keys[25], (FF, D), ((1, 32),), -0.2, 0.2)), 1.128011421248909e-12, 1.8048182739982543e-11)
    down_weight = normal_values(keys[26], (D, EMB), D ** -0.5, 0.21875, ((0, 32),), jnp.float32)
    down_moment = normal_values(keys[27], (D, EMB), (0.0022 / PARAMS ** 0.5), 2.163246563213761e-06, ((0, 32),), jnp.float32)
    down_second = jnp.clip(jnp.exp(math.log(1.8048182739982543e-11) - 2.7725887 * jax.random.uniform(keys[28], (D, EMB), jnp.float32) ** level_of(keys[28], (D, EMB), ((0, 32),), -0.2, 0.2)), 1.128011421248909e-12, 1.8048182739982543e-11)
    norm_gains = draw_norm_gains(jax.random.fold_in(keys[32], 71), 0)
    gains_moment = normal_values(keys[30], (3, D), (0.0022 / PARAMS ** 0.5), 2.163246563213761e-06, ((1, 32),), jnp.float32)
    gains_second = jnp.clip(jnp.exp(math.log(1.8048182739982543e-11) - 2.7725887 * jax.random.uniform(keys[31], (3, D), jnp.float32) ** level_of(keys[31], (3, D), ((1, 32),), -0.2, 0.2)), 1.128011421248909e-12, 1.8048182739982543e-11)
    return dict(token_ids=token_ids, segment_ids=segment_ids, live=live, timesteps=timesteps, noise=noise, embedding=embedding, embedding_moment=embedding_moment, embedding_second=embedding_second, up_weight=up_weight, up_moment=up_moment, up_second=up_second, time_weight=time_weight, time_moment=time_moment, time_second=time_second, qkv_weight=qkv_weight, qkv_moment=qkv_moment, qkv_second=qkv_second, out_weight=out_weight, out_moment=out_moment, out_second=out_second, fc_weight=fc_weight, fc_moment=fc_moment, fc_second=fc_second, proj_weight=proj_weight, proj_moment=proj_moment, proj_second=proj_second, down_weight=down_weight, down_moment=down_moment, down_second=down_second, norm_gains=norm_gains, gains_moment=gains_moment, gains_second=gains_second)


@jax.custom_vjp
def low(v):
    return lax.optimization_barrier(v.astype(jnp.bfloat16)).astype(jnp.float32)

@jax.custom_vjp
def low_back(v):
    return v

def low_keep(v):
    return (low(v), None)

def low_pass(kept, grad):
    return (grad,)

def back_keep(v):
    return (v, None)

def back_low(kept, grad):
    return (low(grad),)
low.defvjp(low_keep, low_pass)
low_back.defvjp(back_keep, back_low)
HIGH = lax.Precision.HIGHEST
NEG_BIG = -1e+30
EPS_NORM = 1e-05
BETA_ONE = 0.9
BETA_TWO = 0.95
ADAM_EPS = 1e-08
DECAY_RATE = 0.01
CLIP_NORM = 0.02
RATES = (0.05, 0.05, 0.02, 0.02, 0.02, 0.02, 0.01, 0.02, 0.3)
DECAYS = (DECAY_RATE,) * 8 + (0.0,)

def matmul(left_op, right_op):
    return jnp.dot(left_op, right_op, precision=HIGH, preferred_element_type=jnp.float32)

def layer_normalize(hidden, gain_row):
    centre = lax.optimization_barrier(jnp.mean(hidden, -1, keepdims=True))
    centred = hidden - centre
    spread = lax.optimization_barrier(jnp.mean(centred * centred, -1, keepdims=True))
    return centred * lax.rsqrt(spread + EPS_NORM) * gain_row

def sinusoid(step_row, model_width):
    half_width = model_width // 2
    freqs = jnp.exp(-math.log(10000.0) * jnp.arange(half_width, dtype=jnp.float32) / half_width)
    angles = step_row.astype(jnp.float32)[:, None] * freqs[None, :]
    return jnp.concatenate([jnp.sin(angles), jnp.cos(angles)], -1)

def row_loss(params, row_inputs):
    word_table, up_low, time_low, query_key_value_reduced, out_low, feedforward_weight_reduced, proj_low, down_weight_reduced, gains_low = [low(member) for member in params]
    tokens, segments, step_row, noise_row, token_weight = row_inputs
    length = tokens.shape[0]
    start_emb = word_table[tokens]
    fraction = step_row.astype(jnp.float32) / STEPS_T
    alpha_bar = 1.0 - jnp.sqrt(fraction + 0.0001)
    noisy_emb = jnp.sqrt(alpha_bar)[:, None] * start_emb + jnp.sqrt(1.0 - alpha_bar)[:, None] * noise_row
    feature = low(sinusoid(step_row, D))
    hidden_initial = low_back(matmul(low(noisy_emb), up_low) + matmul(feature, time_low))
    normalized_first = low(layer_normalize(hidden_initial, gains_low[0]))
    qkv_mixed = low_back(matmul(normalized_first, query_key_value_reduced))
    queries = low(qkv_mixed[:, :D]).reshape(length, HEADS, HEAD)
    key_heads = low(qkv_mixed[:, D:2 * D]).reshape(length, HEADS, HEAD)
    values = low(qkv_mixed[:, 2 * D:]).reshape(length, HEADS, HEAD)
    scores = low_back(jnp.einsum('qhd,khd->hqk', queries, key_heads, precision=HIGH) * HEAD ** (-0.5))
    allowed = (segments[:, None] == segments[None, :])[None]
    scores = jnp.where(allowed, scores, NEG_BIG)
    row_peak = lax.optimization_barrier(jnp.max(scores, -1, keepdims=True))
    exp_scores = jnp.exp(scores - row_peak)
    probs = exp_scores / lax.optimization_barrier(jnp.sum(exp_scores, -1, keepdims=True))
    attended = low_back(jnp.einsum('hqk,khd->qhd', low(probs), values, precision=HIGH)).reshape(length, D)
    hidden_after_first = hidden_initial + low_back(matmul(low(attended), out_low))
    normalized_second = low(layer_normalize(hidden_after_first, gains_low[1]))
    fc_upper = low_back(matmul(normalized_second, feedforward_weight_reduced))
    hidden_after_second = hidden_after_first + low_back(matmul(low(jax.nn.gelu(fc_upper)), proj_low))
    normalized_final = low(layer_normalize(hidden_after_second, gains_low[2]))
    prediction = low_back(matmul(normalized_final, down_weight_reduced))
    logits = low_back(matmul(low(prediction), word_table.T))
    logit_peak = lax.optimization_barrier(jnp.max(logits, -1, keepdims=True))
    log_total = logit_peak[:, 0] + jnp.log(lax.optimization_barrier(jnp.sum(jnp.exp(logits - logit_peak), -1)))
    target = jnp.take_along_axis(logits, tokens[:, None], 1)[:, 0]
    pred_gap = prediction - start_emb
    per_token = lax.optimization_barrier(jnp.mean(pred_gap * pred_gap, -1)) + log_total - target
    return jnp.sum(token_weight * per_token)

def total_loss(row_inputs, params):

    def row_step(running, row_data):
        return (running + jax.checkpoint(row_loss)(params, row_data), None)
    running, unused_rows = lax.scan(row_step, jnp.zeros((), jnp.float32), row_inputs)
    return running

def adam_update(master, moment, second, grad, rate, decay):
    moment_new = BETA_ONE * moment + (1.0 - BETA_ONE) * grad
    second_new = BETA_TWO * second + (1.0 - BETA_TWO) * grad * grad
    moment_hat = moment_new / (1.0 - BETA_ONE ** ADAM_STEP)
    second_hat = second_new / (1.0 - BETA_TWO ** ADAM_STEP)
    master_new = master - rate * (moment_hat / (jnp.sqrt(second_hat) + ADAM_EPS) + decay * master)
    return [moment_new, second_new, master_new]

def reference(token_ids, segment_ids, live, timesteps, noise, embedding, embedding_moment, embedding_second, up_weight, up_moment, up_second, time_weight, time_moment, time_second, qkv_weight, qkv_moment, qkv_second, out_weight, out_moment, out_second, fc_weight, fc_moment, fc_second, proj_weight, proj_moment, proj_second, down_weight, down_moment, down_second, norm_gains, gains_moment, gains_second):
    masters = (embedding, up_weight, time_weight, qkv_weight, out_weight, fc_weight, proj_weight, down_weight, norm_gains)
    moments = (embedding_moment, up_moment, time_moment, qkv_moment, out_moment, fc_moment, proj_moment, down_moment, gains_moment)
    seconds = (embedding_second, up_second, time_second, qkv_second, out_second, fc_second, proj_second, down_second, gains_second)
    live_float = live.astype(jnp.float32)
    step_span = STEPS_T // BUCKETS
    onehot = ((timesteps // step_span)[..., None] == jnp.arange(BUCKETS, dtype=jnp.int32)).astype(jnp.float32)
    counts = lax.optimization_barrier(jnp.sum(live_float[..., None] * onehot, (0, 1)))
    token_weight = live_float * lax.optimization_barrier(jnp.sum(onehot / counts, -1)) / BUCKETS
    row_inputs = (token_ids, segment_ids, timesteps, noise, token_weight)
    loss_sum, pullback = jax.vjp(partial(total_loss, row_inputs), masters)
    grad_list, = pullback(jnp.ones((), jnp.float32))
    squares = sum((jnp.sum(member * member) for member in grad_list))
    grad_norm = jnp.sqrt(squares)
    factor = CLIP_NORM / jnp.maximum(grad_norm, CLIP_NORM)
    results = []
    for place in range(9):
        results = results + adam_update(masters[place], moments[place], seconds[place], factor * grad_list[place], RATES[place], DECAYS[place])
    return (loss_sum, grad_norm, results[0], results[1], results[2], results[3], results[4], results[5], results[6], results[7], results[8], results[9], results[10], results[11], results[12], results[13], results[14], results[15], results[16], results[17], results[18], results[19], results[20], results[21], results[22], results[23], results[24], results[25], results[26])
```

```python
import math

import jax
import jax.numpy as jnp
from jax import lax
from jax.experimental import pallas as pl
from jax.experimental.pallas import tpu as pltpu
from jax.sharding import PartitionSpec as P

D = 768
HEAD = 64
EMB = 128
STEPS_T = 2000
ADAM_STEP = 10


NEG_BIG = -1e30
EPS_NORM = 1e-05
BETA_ONE = 0.9
BETA_TWO = 0.95
ADAM_EPS = 1e-08
DECAY_RATE = 0.01
CLIP_NORM = 0.02
RATES = (0.05, 0.05, 0.02, 0.02, 0.02, 0.02, 0.01, 0.02, 0.3)
DECAYS = (DECAY_RATE,) * 8 + (0.0,)


def matmul(left_op, right_op):
    return jnp.dot(left_op, right_op, preferred_element_type=jnp.float32)


def matmul_tn(left_op, right_op):
    return lax.dot_general(
        left_op, right_op, (((0,), (0,)), ((), ())), preferred_element_type=jnp.float32
    )


def matrix_product_transposed(left_op, right_op):
    return lax.dot_general(
        left_op, right_op, (((1,), (1,)), ((), ())), preferred_element_type=jnp.float32
    )


def layer_normalize(hidden, gain_row):
    centre = jnp.mean(hidden, -1, keepdims=True)
    centred = hidden - centre
    spread = jnp.mean(centred * centred, -1, keepdims=True)
    scale_inv = lax.rsqrt(spread + EPS_NORM)
    normed = centred * scale_inv
    return (normed * gain_row, normed, scale_inv)


def norm_back(grad_normed_out, normed, scale_inv, gain_row):
    grad_gain = jnp.sum(grad_normed_out * normed, 0)
    grad_scaled = grad_normed_out * gain_row
    grad_input = scale_inv * (
        grad_scaled
        - jnp.mean(grad_scaled, -1, keepdims=True)
        - normed * jnp.mean(grad_scaled * normed, -1, keepdims=True)
    )
    return (grad_input, grad_gain)


def sinusoid(step_row, model_width):
    half_width = model_width // 2
    freqs = jnp.exp(-math.log(10000.0) * jnp.arange(half_width, dtype=jnp.float32) / half_width)
    angles = step_row.astype(jnp.float32)[:, None] * freqs[None, :]
    return jnp.concatenate([jnp.sin(angles), jnp.cos(angles)], -1)


TILE = 128
LOG2E = math.log2(math.e)


def key_windows(segments):
    length = segments.shape[0]
    blocks = segments.reshape(-1, TILE)
    shared = jnp.any(blocks[:, :, None] == segments[None, None, :], 1)
    places = jnp.arange(length, dtype=jnp.int32)[None, :]
    first = jnp.min(jnp.where(shared, places, length), 1) // 16 * 16
    last = jnp.max(jnp.where(shared, places, -1), 1) + 1
    spans = (last - first + TILE - 1) // TILE
    starts = jnp.minimum(first, length - spans * TILE)
    return jnp.stack([starts, spans]).astype(jnp.int32)


def nt_dot(left, right):
    return lax.dot_general(
        left, right, (((1,), (1,)), ((), ())), preferred_element_type=jnp.float32
    )


def tn_dot(left, right):
    return lax.dot_general(
        left, right, (((0,), (0,)), ((), ())), preferred_element_type=jnp.float32
    )


def probs_window(query, keys, same):
    scores = jnp.where(same, nt_dot(keys, query), NEG_BIG)
    peak = jnp.max(scores, 0, keepdims=True)
    raised = jnp.exp2((scores - peak) * (HEAD ** (-0.5) * LOG2E))
    return raised * (1.0 / jnp.sum(raised, 0, keepdims=True))


def head_halves(pair):
    lanes = lax.broadcasted_iota(jnp.int32, pair.shape, 1)
    zero = jnp.zeros_like(pair)
    return [jnp.where(lanes < HEAD, pair, zero), jnp.where(lanes >= HEAD, pair, zero)]


def over_windows(windows_ref, length, visit):
    def step(block, unused):
        row_start = pl.multiple_of(block * TILE, TILE)
        key_start = pl.multiple_of(windows_ref[0, block], 16)
        for tiles in range(1, length // TILE + 1):

            @pl.when(windows_ref[1, block] == tiles)
            def _():
                visit(row_start, key_start, tiles * TILE)

        return unused

    lax.fori_loop(0, length // TILE, step, 0)


def attention_forward(mixed, seg_row, seg_col, windows):
    length, width = mixed.shape[0], mixed.shape[1] // 3
    pairs = width // TILE

    def kernel(windows_ref, q_ref, k_ref, v_ref, row_ref, col_ref, o_ref):
        def visit(row_start, key_start, span):
            rows = pl.ds(row_start, TILE)
            keys = pl.ds(key_start, span)
            key_blk, value_blk = k_ref[keys, :], v_ref[keys, :]
            same = col_ref[keys, :] == row_ref[:, rows]
            lanes = lax.broadcasted_iota(jnp.int32, (TILE, TILE), 1)
            both = [
                tn_dot(probs_window(half, key_blk, same).astype(jnp.bfloat16), value_blk)
                for half in head_halves(q_ref[rows, :])
            ]
            o_ref[rows, :] = jnp.where(lanes < HEAD, both[0], both[1]).astype(jnp.bfloat16)

        over_windows(windows_ref, length, visit)

    def column(offset):
        return pl.BlockSpec((length, TILE), lambda pair, windows: (0, pair + offset))

    return pl.pallas_call(
        kernel,
        out_shape=jax.ShapeDtypeStruct((length, width), jnp.bfloat16),
        grid_spec=pltpu.PrefetchScalarGridSpec(
            num_scalar_prefetch=1,
            grid=(pairs,),
            in_specs=[
                column(0),
                column(pairs),
                column(2 * pairs),
                pl.BlockSpec((1, length), lambda pair, windows: (0, 0)),
                pl.BlockSpec((length, 1), lambda pair, windows: (0, 0)),
            ],
            out_specs=column(0),
        ),
        compiler_params=pltpu.CompilerParams(vmem_limit_bytes=48 << 20),
        name="attention_forward",
    )(windows, mixed, mixed, mixed, seg_row, seg_col)


def attention_backward(mixed, grad_attended, seg_row, seg_col, windows):
    length, width = mixed.shape[0], mixed.shape[1] // 3
    pairs = width // TILE
    score_scale = HEAD ** (-0.5)

    def kernel(windows_ref, q_ref, k_ref, v_ref, do_ref, row_ref, col_ref, out_ref, dk_acc, dv_acc):
        pair = pl.program_id(0)
        dk_acc[...] = jnp.zeros_like(dk_acc)
        dv_acc[...] = jnp.zeros_like(dv_acc)

        def columns(third):
            return pl.ds(pl.multiple_of((third * pairs + pair) * TILE, TILE), TILE)

        def visit(row_start, key_start, span):
            rows = pl.ds(row_start, TILE)
            keys = pl.ds(key_start, span)
            key_blk, value_blk = k_ref[keys, :], v_ref[keys, :]
            same = col_ref[keys, :] == row_ref[:, rows]
            queries = head_halves(q_ref[rows, :])
            grads = head_halves(do_ref[rows, :])
            probs_low, scores_low = [], []
            for query, grad in zip(queries, grads):
                probs = probs_window(query, key_blk, same)
                grad_probs = nt_dot(value_blk, grad)
                inner = jnp.sum(probs * grad_probs, 0, keepdims=True)
                probs_low.append(probs.astype(jnp.bfloat16))
                scores_low.append((probs * (grad_probs - inner)).astype(jnp.bfloat16))
            scores_both = jnp.concatenate(scores_low, 1)
            dv_acc[keys, :] += jnp.dot(
                jnp.concatenate(probs_low, 1),
                jnp.concatenate(grads, 0),
                preferred_element_type=jnp.float32,
            )
            dk_acc[keys, :] += jnp.dot(
                scores_both,
                jnp.concatenate(queries, 0),
                preferred_element_type=jnp.float32,
            )
            lanes = lax.broadcasted_iota(jnp.int32, (TILE, TILE), 1)
            both = tn_dot(scores_both, key_blk)
            grad_query = jnp.where(lanes < HEAD, both[:TILE], both[TILE:])
            out_ref[rows, columns(0)] = (grad_query * score_scale).astype(jnp.bfloat16)

        over_windows(windows_ref, length, visit)
        out_ref[:, columns(1)] = (dk_acc[...] * score_scale).astype(jnp.bfloat16)
        out_ref[:, columns(2)] = dv_acc[...].astype(jnp.bfloat16)

    def column(offset):
        return pl.BlockSpec((length, TILE), lambda pair, windows: (0, pair + offset))

    return pl.pallas_call(
        kernel,
        out_shape=jax.ShapeDtypeStruct(mixed.shape, jnp.bfloat16),
        grid_spec=pltpu.PrefetchScalarGridSpec(
            num_scalar_prefetch=1,
            grid=(pairs,),
            in_specs=[
                column(0),
                column(pairs),
                column(2 * pairs),
                column(0),
                pl.BlockSpec((1, length), lambda pair, windows: (0, 0)),
                pl.BlockSpec((length, 1), lambda pair, windows: (0, 0)),
            ],
            out_specs=pl.BlockSpec(mixed.shape, lambda pair, windows: (0, 0)),
            scratch_shapes=[pltpu.VMEM((length, TILE), jnp.float32)] * 2,
        ),
        compiler_params=pltpu.CompilerParams(vmem_limit_bytes=48 << 20),
        name="attention_backward",
    )(windows, mixed, mixed, mixed, grad_attended, seg_row, seg_col)


def block_forward(
    hidden_initial,
    segments,
    query_key_value_reduced,
    out_low,
    feedforward_weight_reduced,
    proj_low,
    norm_gain_vector,
):
    normalized_first, centred_scaled_first, inverse_deviation_first = layer_normalize(
        hidden_initial, norm_gain_vector[0]
    )
    normed_one_low = normalized_first.astype(jnp.bfloat16)
    mixed_low = matmul(normed_one_low, query_key_value_reduced).astype(jnp.bfloat16)
    attended_low = attention_forward(mixed_low, *segments)
    hidden_after_first = hidden_initial + matrix_product_transposed(attended_low, out_low)
    normalized_second, centred_scaled_second, inverse_deviation_second = layer_normalize(
        hidden_after_first, norm_gain_vector[1]
    )
    normed_two_low = normalized_second.astype(jnp.bfloat16)
    fc_upper = matmul(normed_two_low, feedforward_weight_reduced)
    active_low = jax.nn.gelu(fc_upper).astype(jnp.bfloat16)
    hidden_after_second = hidden_after_first + matrix_product_transposed(active_low, proj_low)
    saved_acts = (
        centred_scaled_first,
        inverse_deviation_first,
        normed_one_low,
        mixed_low,
        attended_low,
        centred_scaled_second,
        inverse_deviation_second,
        normed_two_low,
        fc_upper,
        active_low,
    )
    return (saved_acts, hidden_after_second)


def block_backward(
    saved_acts,
    grad_two,
    segments,
    query_key_value_reduced,
    out_low,
    feedforward_weight_reduced,
    proj_low,
    norm_gain_vector,
):
    (
        centred_scaled_first,
        inverse_deviation_first,
        normed_one_low,
        mixed_low,
        attended_low,
        centred_scaled_second,
        inverse_deviation_second,
        normed_two_low,
        fc_upper,
        active_low,
    ) = saved_acts
    grad_mlp_low = grad_two.astype(jnp.bfloat16)
    grad_proj = matmul_tn(grad_mlp_low, active_low)
    grad_active = matmul(grad_mlp_low, proj_low)
    unused_value, gelu_pull = jax.vjp(jax.nn.gelu, fc_upper)
    (grad_upper,) = gelu_pull(grad_active)
    gradient_upper_reduced = grad_upper.astype(jnp.bfloat16)
    grad_fc = matmul_tn(normed_two_low, gradient_upper_reduced)
    grad_norm_two, grad_gain_two = norm_back(
        matrix_product_transposed(gradient_upper_reduced, feedforward_weight_reduced),
        centred_scaled_second,
        inverse_deviation_second,
        norm_gain_vector[1],
    )
    grad_one = grad_two + grad_norm_two
    grad_branch_low = grad_one.astype(jnp.bfloat16)
    grad_out = matmul_tn(grad_branch_low, attended_low)
    grad_attended = matmul(grad_branch_low, out_low).astype(jnp.bfloat16)
    gradient_mixed_reduced = attention_backward(mixed_low, grad_attended, *segments)
    grad_qkv = matmul_tn(normed_one_low, gradient_mixed_reduced)
    grad_norm_one, grad_gain_one = norm_back(
        matrix_product_transposed(gradient_mixed_reduced, query_key_value_reduced),
        centred_scaled_first,
        inverse_deviation_first,
        norm_gain_vector[0],
    )
    return (
        grad_one + grad_norm_one,
        (grad_qkv, grad_out, grad_fc, grad_proj, grad_gain_one, grad_gain_two),
    )


def head_pass(pred_low, word_table, token_weight):
    length, width = pred_low.shape
    words = word_table.shape[0]
    tile = 1024

    def kernel(pred_ref, table_ref, weight_ref, grad_table_ref, grad_pred_ref, log_ref, peak, total):
        phase, step = pl.program_id(0), pl.program_id(1)

        @pl.when((phase == 0) & (step == 0))
        def _():
            peak[...] = jnp.full_like(peak, -jnp.inf)
            total[...] = jnp.zeros_like(total)
            grad_pred_ref[...] = jnp.zeros_like(grad_pred_ref)

        table = table_ref[...]
        logits = nt_dot(table, pred_ref[...])

        @pl.when(phase == 0)
        def _():
            old = peak[...]
            new = jnp.maximum(old, jnp.max(logits, 0, keepdims=True))
            raised = jnp.sum(jnp.exp(logits - new), 0, keepdims=True)
            total[...] = total[...] * jnp.exp(old - new) + raised
            peak[...] = new

        @pl.when(phase == 1)
        def _():
            log_total = peak[...] + jnp.log(total[...])
            log_ref[...] = log_total
            grad_logits = (weight_ref[...] * jnp.exp(logits - log_total)).astype(jnp.bfloat16)
            grad_table_ref[...] = jnp.dot(
                grad_logits, pred_ref[...], preferred_element_type=jnp.float32
            )
            grad_pred_ref[...] += tn_dot(table, grad_logits)

    def whole(shape):
        return pl.BlockSpec(shape, lambda phase, step: (0, 0))

    return pl.pallas_call(
        kernel,
        out_shape=(
            jax.ShapeDtypeStruct((words, width), jnp.float32),
            jax.ShapeDtypeStruct((width, length), jnp.float32),
            jax.ShapeDtypeStruct((1, length), jnp.float32),
        ),
        grid_spec=pltpu.PrefetchScalarGridSpec(
            num_scalar_prefetch=0,
            grid=(2, words // tile),
            in_specs=[
                whole((length, width)),
                pl.BlockSpec((tile, width), lambda phase, step: (step, 0)),
                whole((1, length)),
            ],
            out_specs=[
                pl.BlockSpec((tile, width), lambda phase, step: (phase * step, 0)),
                whole((width, length)),
                whole((1, length)),
            ],
            scratch_shapes=[pltpu.VMEM((1, length), jnp.float32)] * 2,
        ),
        compiler_params=pltpu.CompilerParams(vmem_limit_bytes=48 << 20),
        name="head_pass",
    )(pred_low, word_table, token_weight)


def adam_update(master, moment, second, grad, rate, decay):
    moment_new = BETA_ONE * moment + (1.0 - BETA_ONE) * grad
    second_new = BETA_TWO * second + (1.0 - BETA_TWO) * grad * grad
    moment_hat = moment_new / (1.0 - BETA_ONE**ADAM_STEP)
    second_hat = second_new / (1.0 - BETA_TWO**ADAM_STEP)
    master_new = master - rate * (moment_hat / (jnp.sqrt(second_hat) + ADAM_EPS) + decay * master)
    return [moment_new, second_new, master_new]


AXES = ("bucket", "dp")


class Place:
    def __init__(self, buckets, columns):
        self.buckets, self.columns = buckets, columns
        self.count = buckets * columns
        self.line = columns // 2
        self.bits = [1 << place for place in range(1, columns.bit_length() - 1)]
        self.square = lax.axis_index("bucket")
        along = lax.axis_index("dp")
        self.core = along % 2
        self.along = along // 2
        self.flat = self.square * columns + along
        self.step_a = 1 + self.core
        self.step_b = 2 - self.core

    def swap(self, array, pick):
        pairs = [(member, member ^ pick(member)) for member in range(self.count)]
        return lax.ppermute(array, AXES, pairs)

    def swap_core(self, array):
        return self.swap(array, lambda member: 1)

    def swap_a(self, array):
        return self.swap(array, lambda member: self.columns * (1 + member % 2))

    def swap_b(self, array):
        return self.swap(array, lambda member: self.columns * (2 - member % 2))

    def swap_line(self, array, bit):
        return self.swap(array, lambda member: bit)

    def total(self, array):
        spans = [1] + self.bits + [self.columns, 2 * self.columns]
        for bit in spans:
            array = array + self.swap_line(array, bit)
        return array


def assemble(place, pieces):
    line, rows, cols = pieces[0].shape
    flags = jnp.stack([place.square, place.along, place.core]).astype(jnp.int32)

    def kernel(flags_ref, *refs):
        piece_refs, out_ref, held, load_sems, store_sem = refs[:8], *refs[8:]
        square, along, core = flags_ref[0], flags_ref[1], flags_ref[2]
        step_a, step_b = 1 + core, 2 - core
        spots = [
            (square, core),
            (square ^ step_a, core),
            (square ^ step_b, core),
            (square ^ 3, core),
            (square, 1 - core),
            (square ^ step_b, 1 - core),
            (square ^ step_a, 1 - core),
            (square ^ 3, 1 - core),
        ]
        loads = [
            pltpu.make_async_copy(piece_ref, held.at[at], load_sems.at[at])
            for at, piece_ref in enumerate(piece_refs)
        ]
        for load in loads:
            load.start()
        for at, (quarter, side) in enumerate(spots):
            loads[at].wait()
            for offset in range(line):
                pltpu.make_async_copy(
                    held.at[at, offset],
                    out_ref.at[quarter, along ^ offset, side],
                    store_sem,
                ).start()
        pltpu.make_async_copy(out_ref, out_ref, store_sem).wait()

    gathered = pl.pallas_call(
        kernel,
        out_shape=jax.ShapeDtypeStruct((4, line, 2, rows, cols), pieces[0].dtype),
        grid_spec=pltpu.PrefetchScalarGridSpec(
            num_scalar_prefetch=1,
            grid=(1,),
            in_specs=[pl.BlockSpec(memory_space=pl.ANY)] * 8,
            out_specs=pl.BlockSpec(memory_space=pl.ANY),
            scratch_shapes=[
                pltpu.VMEM((8, line, rows, cols), pieces[0].dtype),
                pltpu.SemaphoreType.DMA((8,)),
                pltpu.SemaphoreType.DMA(()),
            ],
        ),
        name="assemble",
    )(flags, *pieces)
    return gathered.reshape(8 * line * rows, cols)


def gather_rows(place, shard):
    own = shard[None]
    for bit in place.bits:
        own = jnp.concatenate([own, place.swap_line(own, bit)], 0)
    near_a = place.swap_a(own)
    near_b = place.swap_b(own)
    far = place.swap_b(near_a)
    mine = [own, near_a, near_b, far]
    return assemble(place, mine + [place.swap_core(piece) for piece in mine])


def scatter_sum(place, keep, send):
    rows = keep.shape[0] // place.count
    cols = keep.shape[1]
    across = place.swap_core(send)
    keep4 = keep.reshape(4, -1, cols)
    across4 = across.reshape(4, -1, cols)

    def quarter(index):
        return (
            lax.dynamic_index_in_dim(keep4, index, 0, False)
            + lax.dynamic_index_in_dim(across4, index, 0, False)
        )

    square = place.square
    first = jnp.stack([quarter(square ^ place.step_a), quarter(square ^ 3)])
    got_a = place.swap_a(first.astype(jnp.bfloat16)).astype(jnp.float32)
    second = (quarter(square ^ place.step_b) + got_a[1]).astype(jnp.bfloat16)
    got_b = place.swap_b(second).astype(jnp.float32)
    own = quarter(square) + got_a[0] + got_b
    own = own.reshape(place.line, 2, rows, cols)
    along = place.along
    for bit in place.bits:
        mine = along % 2
        own = own.reshape((own.shape[0] // 2, 2) + own.shape[1:])
        other = lax.dynamic_index_in_dim(own, 1 - mine, 1, False)
        own = lax.dynamic_index_in_dim(own, mine, 1, False) + place.swap_line(other, bit)
        along = along // 2
    own = own[0]
    other = lax.dynamic_index_in_dim(own, 1 - place.core, 0, False)
    kept = lax.dynamic_index_in_dim(own, place.core, 0, False)
    return kept, place.swap_core(other)


def in_order(place, kept, other, axis):
    return jnp.where(
        place.core == 0,
        jnp.concatenate([kept, other], axis),
        jnp.concatenate([other, kept], axis),
    )


def scatter_columns(place, grad):
    half = grad.shape[1] // 2
    keep = lax.dynamic_slice_in_dim(grad, place.core * half, half, 1)
    send = lax.dynamic_slice_in_dim(grad, (1 - place.core) * half, half, 1)
    kept, other = scatter_sum(place, keep, send)
    return in_order(place, kept, other, 1)


def scatter_table(place, grad):
    cols = grad.shape[1]
    half = grad.shape[0] // place.count // 2
    split = grad.reshape(place.count, 2, half, cols)
    keep = lax.dynamic_index_in_dim(split, place.core, 1, False).reshape(-1, cols)
    send = lax.dynamic_index_in_dim(split, 1 - place.core, 1, False).reshape(-1, cols)
    kept, other = scatter_sum(place, keep, send)
    return in_order(place, kept, other, 0)


def on_device(
    token_ids,
    segment_ids,
    live,
    timesteps,
    noise,
    embedding,
    embedding_moment,
    embedding_second,
    up_weight,
    up_moment,
    up_second,
    time_weight,
    time_moment,
    time_second,
    qkv_weight,
    qkv_moment,
    qkv_second,
    out_weight,
    out_moment,
    out_second,
    fc_weight,
    fc_moment,
    fc_second,
    proj_weight,
    proj_moment,
    proj_second,
    down_weight,
    down_moment,
    down_second,
    norm_gains,
    gains_moment,
    gains_second,
):
    masters = (
        embedding,
        up_weight,
        time_weight,
        qkv_weight,
        out_weight,
        fc_weight,
        proj_weight,
        down_weight,
        norm_gains,
    )
    moments = (
        embedding_moment,
        up_moment,
        time_moment,
        qkv_moment,
        out_moment,
        fc_moment,
        proj_moment,
        down_moment,
        gains_moment,
    )
    seconds = (
        embedding_second,
        up_second,
        time_second,
        qkv_second,
        out_second,
        fc_second,
        proj_second,
        down_second,
        gains_second,
    )
    place = Place(lax.axis_size("bucket"), lax.axis_size("dp"))
    buckets = place.buckets
    step_span = STEPS_T // buckets
    live_float = live[0].astype(jnp.float32)
    step_row = timesteps[0]
    onehot = (
        (step_row // step_span)[:, None] == jnp.arange(buckets, dtype=jnp.int32)[None, :]
    ).astype(jnp.float32)
    counts = place.total(jnp.sum(live_float[:, None] * onehot, 0))
    low = [member.astype(jnp.bfloat16) for member in masters]
    gains_pad = jnp.pad(low[8].T, ((0, 0), (0, EMB - 3)))
    word_table = gather_rows(place, low[0])
    entry_low = gather_rows(place, jnp.concatenate([low[1].T, low[2].T, gains_pad], 1))
    query_key_value_reduced = gather_rows(place, low[3])
    out_low = gather_rows(place, low[4].T)
    feedforward_weight_reduced = gather_rows(place, low[5])
    exit_low = gather_rows(place, jnp.concatenate([low[6].T, low[7]], 1))
    up_low = entry_low[:, :EMB]
    time_low = entry_low[:, EMB : EMB + D]
    gains_low = entry_low[:, EMB + D : EMB + D + 3].T
    ff_width = feedforward_weight_reduced.shape[1]
    proj_low = exit_low[:, :ff_width]
    down_weight_reduced = exit_low[:, ff_width:]
    norm_gain_vector = gains_low.astype(jnp.float32)
    tokens = token_ids[0]
    segments = (segment_ids, segment_ids.T, key_windows(segment_ids[0]))
    noise_row = noise[0]
    token_weight = live_float * jnp.sum(onehot / counts[None, :], -1) / buckets
    start_emb = word_table[tokens].astype(jnp.float32)
    fraction = step_row.astype(jnp.float32) / STEPS_T
    alpha_bar = 1.0 - jnp.sqrt(fraction + 0.0001)
    keep_root = jnp.sqrt(alpha_bar)[:, None]
    noisy_emb = keep_root * start_emb + jnp.sqrt(1.0 - alpha_bar)[:, None] * noise_row
    noisy_low = noisy_emb.astype(jnp.bfloat16)
    feature_low = sinusoid(step_row, D).astype(jnp.bfloat16)
    hidden_initial = matrix_product_transposed(
        noisy_low, up_low
    ) + matrix_product_transposed(feature_low, time_low)
    saved_acts, hidden_after_second = block_forward(
        hidden_initial,
        segments,
        query_key_value_reduced,
        out_low,
        feedforward_weight_reduced,
        proj_low,
        norm_gain_vector,
    )
    normalized_final, centred_scaled_final, inverse_deviation_final = layer_normalize(
        hidden_after_second, norm_gain_vector[2]
    )
    normed_top_low = normalized_final.astype(jnp.bfloat16)
    prediction = matmul(normed_top_low, down_weight_reduced)
    pred_low = prediction.astype(jnp.bfloat16)
    grad_table_head, grad_pred_head, log_total = head_pass(
        pred_low, word_table, token_weight[None, :]
    )
    pred_float = pred_low.astype(jnp.float32)
    target = jnp.sum(pred_float * start_emb, -1)
    cross_loss = log_total[0] - target
    target_prob = jnp.exp(target - log_total[0])
    target_shift = (token_weight * (target_prob - 1.0)).astype(jnp.bfloat16).astype(jnp.float32) - (
        token_weight * target_prob
    ).astype(jnp.bfloat16).astype(jnp.float32)
    target_shift = target_shift[:, None]
    pred_gap = prediction - start_emb
    loss_local = jnp.sum(token_weight * (jnp.mean(pred_gap * pred_gap, -1) + cross_loss))
    grad_mse = token_weight[:, None] * 2.0 * pred_gap / EMB
    gradient_prediction_reduced = (
        grad_mse + grad_pred_head.T + target_shift * start_emb
    ).astype(jnp.bfloat16)
    grad_down = matmul_tn(normed_top_low, gradient_prediction_reduced)
    grad_top, grad_gain_top = norm_back(
        matrix_product_transposed(gradient_prediction_reduced, down_weight_reduced),
        centred_scaled_final,
        inverse_deviation_final,
        norm_gain_vector[2],
    )
    grad_zero, block_grads = block_backward(
        saved_acts,
        grad_top,
        segments,
        query_key_value_reduced,
        out_low,
        feedforward_weight_reduced,
        proj_low,
        norm_gain_vector,
    )
    grad_qkv, grad_out, grad_fc, grad_proj, grad_gain_one, grad_gain_two = block_grads
    grad_zero_low = grad_zero.astype(jnp.bfloat16)
    grad_up = matmul_tn(grad_zero_low, noisy_low)
    grad_time = matmul_tn(grad_zero_low, feature_low)
    grad_start = keep_root * matmul(grad_zero_low, up_low) - grad_mse + target_shift * pred_float
    grad_table = grad_table_head + jax.ops.segment_sum(
        grad_start, tokens, num_segments=word_table.shape[0]
    )
    grad_gains = jnp.stack([grad_gain_one, grad_gain_two, grad_gain_top], 0)
    small = jnp.concatenate([grad_gains.reshape(-1, EMB), jnp.full((1, EMB), loss_local)], 0)
    small = place.total(small)
    loss_sum = small[-1, 0]
    own_cols = D // place.count
    shard_gains = lax.dynamic_slice_in_dim(
        small[:-1].reshape(3, D), place.flat * own_cols, own_cols, 1
    )
    shard_proj = scatter_columns(place, grad_proj)
    shard_fc = scatter_columns(place, grad_fc)
    shard_out = scatter_columns(place, grad_out)
    shard_qkv = scatter_columns(place, grad_qkv)
    shard_rest = scatter_columns(place, jnp.concatenate([grad_up, grad_time, grad_down], 1))
    shard_table = scatter_table(place, grad_table)
    shards = (
        shard_table,
        shard_rest[:, :EMB].T,
        shard_rest[:, EMB : EMB + D].T,
        shard_qkv,
        shard_out.T,
        shard_fc,
        shard_proj.T,
        shard_rest[:, EMB + D :],
        shard_gains,
    )
    squares_local = jnp.zeros((), jnp.float32)
    for member in shards:
        squares_local = squares_local + jnp.sum(member * member)
    squares = place.total(jnp.full((8, EMB), squares_local))[0, 0]
    grad_norm = jnp.sqrt(squares)
    factor = CLIP_NORM / jnp.maximum(grad_norm, CLIP_NORM)
    results = []
    for place in range(9):
        results = results + adam_update(
            masters[place],
            moments[place],
            seconds[place],
            factor * shards[place],
            RATES[place],
            DECAYS[place],
        )
    return (
        loss_sum,
        grad_norm,
        results[0],
        results[1],
        results[2],
        results[3],
        results[4],
        results[5],
        results[6],
        results[7],
        results[8],
        results[9],
        results[10],
        results[11],
        results[12],
        results[13],
        results[14],
        results[15],
        results[16],
        results[17],
        results[18],
        results[19],
        results[20],
        results[21],
        results[22],
        results[23],
        results[24],
        results[25],
        results[26],
    )


def solution(mesh):
    return jax.shard_map(
        on_device,
        mesh=mesh,
        in_specs=(
            P(("bucket", "dp"), None),
            P(("bucket", "dp"), None),
            P(("bucket", "dp"), None),
            P(("bucket", "dp"), None),
            P(("bucket", "dp"), None, None),
            P(("bucket", "dp"), None),
            P(("bucket", "dp"), None),
            P(("bucket", "dp"), None),
            P(None, ("bucket", "dp")),
            P(None, ("bucket", "dp")),
            P(None, ("bucket", "dp")),
            P(None, ("bucket", "dp")),
            P(None, ("bucket", "dp")),
            P(None, ("bucket", "dp")),
            P(("bucket", "dp"), None),
            P(("bucket", "dp"), None),
            P(("bucket", "dp"), None),
            P(None, ("bucket", "dp")),
            P(None, ("bucket", "dp")),
            P(None, ("bucket", "dp")),
            P(("bucket", "dp"), None),
            P(("bucket", "dp"), None),
            P(("bucket", "dp"), None),
            P(None, ("bucket", "dp")),
            P(None, ("bucket", "dp")),
            P(None, ("bucket", "dp")),
            P(("bucket", "dp"), None),
            P(("bucket", "dp"), None),
            P(("bucket", "dp"), None),
            P(None, ("bucket", "dp")),
            P(None, ("bucket", "dp")),
            P(None, ("bucket", "dp")),
        ),
        out_specs=(
            P(),
            P(),
            P(("bucket", "dp"), None),
            P(("bucket", "dp"), None),
            P(("bucket", "dp"), None),
            P(None, ("bucket", "dp")),
            P(None, ("bucket", "dp")),
            P(None, ("bucket", "dp")),
            P(None, ("bucket", "dp")),
            P(None, ("bucket", "dp")),
            P(None, ("bucket", "dp")),
            P(("bucket", "dp"), None),
            P(("bucket", "dp"), None),
            P(("bucket", "dp"), None),
            P(None, ("bucket", "dp")),
            P(None, ("bucket", "dp")),
            P(None, ("bucket", "dp")),
            P(("bucket", "dp"), None),
            P(("bucket", "dp"), None),
            P(("bucket", "dp"), None),
            P(None, ("bucket", "dp")),
            P(None, ("bucket", "dp")),
            P(None, ("bucket", "dp")),
            P(("bucket", "dp"), None),
            P(("bucket", "dp"), None),
            P(("bucket", "dp"), None),
            P(None, ("bucket", "dp")),
            P(None, ("bucket", "dp")),
            P(None, ("bucket", "dp")),
        ),
        check_vma=False,
    )
```

```python
import math

import jax
import jax.numpy as jnp
from jax import lax
from jax.experimental import pallas as pl
from jax.experimental.pallas import tpu as pltpu
from jax.sharding import PartitionSpec as P

D = 768
HEAD = 64
EMB = 128
STEPS_T = 2000
ADAM_STEP = 10


NEG_BIG = -1e30
EPS_NORM = 1e-05
BETA_ONE = 0.9
BETA_TWO = 0.95
ADAM_EPS = 1e-08
DECAY_RATE = 0.01
CLIP_NORM = 0.02
RATES = (0.05, 0.05, 0.02, 0.02, 0.02, 0.02, 0.01, 0.02, 0.3)
DECAYS = (DECAY_RATE,) * 8 + (0.0,)


def matmul(left_op, right_op):
    return jnp.dot(left_op, right_op, preferred_element_type=jnp.float32)


def matmul_tn(left_op, right_op):
    return lax.dot_general(
        left_op, right_op, (((0,), (0,)), ((), ())), preferred_element_type=jnp.float32
    )


def matrix_product_transposed(left_op, right_op):
    return lax.dot_general(
        left_op, right_op, (((1,), (1,)), ((), ())), preferred_element_type=jnp.float32
    )


def layer_normalize(hidden, gain_row):
    centre = jnp.mean(hidden, -1, keepdims=True)
    centred = hidden - centre
    spread = jnp.mean(centred * centred, -1, keepdims=True)
    scale_inv = lax.rsqrt(spread + EPS_NORM)
    normed = centred * scale_inv
    return (normed * gain_row, normed, scale_inv)


def norm_back(grad_normed_out, normed, scale_inv, gain_row):
    grad_gain = jnp.sum(grad_normed_out * normed, 0)
    grad_scaled = grad_normed_out * gain_row
    grad_input = scale_inv * (
        grad_scaled
        - jnp.mean(grad_scaled, -1, keepdims=True)
        - normed * jnp.mean(grad_scaled * normed, -1, keepdims=True)
    )
    return (grad_input, grad_gain)


def sinusoid(step_row, model_width):
    half_width = model_width // 2
    freqs = jnp.exp(-math.log(10000.0) * jnp.arange(half_width, dtype=jnp.float32) / half_width)
    angles = step_row.astype(jnp.float32)[:, None] * freqs[None, :]
    return jnp.concatenate([jnp.sin(angles), jnp.cos(angles)], -1)


TILE = 128
LOG2E = math.log2(math.e)
VMEM_LIMIT = 48 << 20


def tie(*arrays):
    return lax.optimization_barrier(arrays)


def key_windows(segments):
    length = segments.shape[0]
    blocks = segments.reshape(-1, TILE)
    shared = jnp.any(blocks[:, :, None] == segments[None, None, :], 1)
    places = jnp.arange(length, dtype=jnp.int32)[None, :]
    first = jnp.min(jnp.where(shared, places, length), 1) // TILE * TILE
    last = jnp.max(jnp.where(shared, places, -1), 1) + 1
    spans = (last - first + TILE - 1) // TILE
    return jnp.stack([first, spans]).astype(jnp.int32)


def nt_dot(left, right):
    return lax.dot_general(
        left, right, (((1,), (1,)), ((), ())), preferred_element_type=jnp.float32
    )


def tn_dot(left, right):
    return lax.dot_general(
        left, right, (((0,), (0,)), ((), ())), preferred_element_type=jnp.float32
    )


def head_stack(pair):
    lanes = lax.broadcasted_iota(jnp.int32, pair.shape, 1)
    zero = jnp.zeros_like(pair)
    return jnp.concatenate(
        [jnp.where(lanes < HEAD, pair, zero), jnp.where(lanes >= HEAD, pair, zero)], 0
    )


def fold(array):
    return array.reshape(-1, 8, array.shape[-1])


PAIRS = D // TILE
WIDE = PAIRS * TILE
LOG_ROWS = -(-2 * PAIRS // 8) * 8


def attention_forward(mixed, seg_row, seg_col, windows):
    length, width = mixed.shape[0], mixed.shape[1] // 3
    groups = width // WIDE
    factor = HEAD ** (-0.5) * LOG2E

    def kernel(windows_ref, q_ref, k_ref, v_ref, row_ref, col_ref, o_ref, log_ref, held, out, flip):
        flip[...] = v_ref[...].T

        def step(block, unused):
            rows = pl.ds(pl.multiple_of(block * TILE, TILE), TILE)
            start, count = windows_ref[0, block], windows_ref[1, block]
            row = row_ref[:, rows]
            queries = [head_stack(q_ref[rows, pl.ds(pair * TILE, TILE)]) for pair in range(PAIRS)]

            def keys_at(at):
                return pl.ds(pl.multiple_of(start + at * TILE, TILE), TILE)

            def held_at(at):
                return pl.ds(pl.multiple_of(at * TILE, TILE), TILE)

            def score(at, state):
                keys = keys_at(at)
                same = col_ref[keys, :] == row
                same = jnp.concatenate([same, same], 1)
                found = []
                for pair in range(PAIRS):
                    old, total = state[pair]
                    scores = nt_dot(k_ref[keys, pl.ds(pair * TILE, TILE)], queries[pair])
                    scores = jnp.where(same, scores * factor, NEG_BIG)
                    held[pair, held_at(at), :] = scores
                    scores = fold(scores)
                    new = jnp.maximum(old, jnp.max(scores, 0))
                    raised = jnp.sum(jnp.exp2(scores - new[None]), 0)
                    found.append((new, total * jnp.exp2(old - new) + raised))
                return tuple(found)

            low = jnp.full((8, 2 * TILE), NEG_BIG, jnp.float32)
            state = lax.fori_loop(0, count, score, ((low, jnp.zeros_like(low)),) * PAIRS)
            logs = []
            for peak, total in state:
                top = jnp.max(peak, 0, keepdims=True)
                total = jnp.sum(total * jnp.exp2(peak - top), 0, keepdims=True)
                logs.append(top + jnp.log2(total))
            out[...] = jnp.zeros_like(out)

            def spread(at, unused):
                for pair in range(PAIRS):
                    probs = jnp.exp2(held[pair, held_at(at), :] - logs[pair]).astype(jnp.bfloat16)
                    out[pair] += jnp.dot(
                        flip[pl.ds(pair * TILE, TILE), keys_at(at)],
                        probs,
                        preferred_element_type=jnp.float32,
                    )
                return unused

            lax.fori_loop(0, count, spread, 0)
            dims = lax.broadcasted_iota(jnp.int32, (TILE, TILE), 0)
            for pair in range(PAIRS):
                both = out[pair]
                chosen = jnp.where(dims < HEAD, both[:, :TILE], both[:, TILE:])
                o_ref[rows, pl.ds(pair * TILE, TILE)] = chosen.T.astype(jnp.bfloat16)
                log_ref[2 * pair : 2 * pair + 1, rows] = logs[pair][:, :TILE]
                log_ref[2 * pair + 1 : 2 * pair + 2, rows] = logs[pair][:, TILE:]
            return unused

        lax.fori_loop(0, length // TILE, step, 0)

    def column(place):
        return pl.BlockSpec((length, WIDE), lambda group, windows: (0, 3 * group + place))

    return pl.pallas_call(
        kernel,
        out_shape=(
            jax.ShapeDtypeStruct((length, width), jnp.bfloat16),
            jax.ShapeDtypeStruct((LOG_ROWS * groups, length), jnp.float32),
        ),
        grid_spec=pltpu.PrefetchScalarGridSpec(
            num_scalar_prefetch=1,
            grid=(groups,),
            in_specs=[
                column(0),
                column(1),
                column(2),
                pl.BlockSpec((1, length), lambda group, windows: (0, 0)),
                pl.BlockSpec((length, TILE), lambda group, windows: (0, 0)),
            ],
            out_specs=[
                pl.BlockSpec((length, WIDE), lambda group, windows: (0, group)),
                pl.BlockSpec((LOG_ROWS, length), lambda group, windows: (group, 0)),
            ],
            scratch_shapes=[
                pltpu.VMEM((PAIRS, length, 2 * TILE), jnp.float32),
                pltpu.VMEM((PAIRS, TILE, 2 * TILE), jnp.float32),
                pltpu.VMEM((WIDE, length), jnp.bfloat16),
            ],
        ),
        compiler_params=pltpu.CompilerParams(vmem_limit_bytes=VMEM_LIMIT),
        name="attention_forward",
    )(windows, mixed, mixed, mixed, seg_row, seg_col)


def attention_backward(mixed, grad_attended, log_sums, seg_row, seg_col, windows):
    length = mixed.shape[0]
    score_scale = HEAD ** (-0.5)
    factor = score_scale * LOG2E

    def kernel(windows_ref, q_ref, k_ref, v_ref, do_ref, log_ref, row_ref, col_ref, *refs):
        out_ref, held, pulled, dq_flip, dq_acc, dk_acc, dv_acc, key_flip = refs
        third = pl.program_id(0)

        def step(block, unused):
            rows = pl.ds(pl.multiple_of(block * TILE, TILE), TILE)
            start, count = windows_ref[0, block], windows_ref[1, block]
            row = row_ref[:, rows]
            pairs = [pl.ds(pair * TILE, TILE) for pair in range(PAIRS)]
            queries = [head_stack(q_ref[rows, cols]) for cols in pairs]
            grads = [head_stack(do_ref[rows, cols]) for cols in pairs]
            logs = [
                jnp.concatenate(
                    [
                        log_ref[2 * pair : 2 * pair + 1, rows],
                        log_ref[2 * pair + 1 : 2 * pair + 2, rows],
                    ],
                    1,
                )
                for pair in range(PAIRS)
            ]

            def keys_at(at):
                return pl.ds(pl.multiple_of(start + at * TILE, TILE), TILE)

            def held_at(at):
                return pl.ds(pl.multiple_of(at * TILE, TILE), TILE)

            def weigh(at, inners):
                keys = keys_at(at)
                same = col_ref[keys, :] == row
                same = jnp.concatenate([same, same], 1)
                found = []
                for pair, cols in enumerate(pairs):
                    scores = nt_dot(k_ref[keys, cols], queries[pair])
                    probs = jnp.where(same, jnp.exp2(scores * factor - logs[pair]), 0.0)
                    grad_probs = nt_dot(v_ref[keys, cols], grads[pair])
                    held[pair, held_at(at), :] = probs
                    pulled[pair, held_at(at), :] = grad_probs
                    found.append(inners[pair] + jnp.sum(fold(probs * grad_probs), 0))
                return tuple(found)

            zero = jnp.zeros((8, 2 * TILE), jnp.float32)
            inners = lax.fori_loop(0, count, weigh, (zero,) * PAIRS)
            inners = [jnp.sum(inner, 0, keepdims=True) for inner in inners]
            dq_flip[...] = jnp.zeros_like(dq_flip)

            def spread(at, unused):
                keys = keys_at(at)
                for pair, cols in enumerate(pairs):
                    probs = held[pair, held_at(at), :]
                    scores = probs * (pulled[pair, held_at(at), :] - inners[pair])
                    scores_low = scores.astype(jnp.bfloat16)
                    dv_acc[keys, cols] += jnp.dot(
                        probs.astype(jnp.bfloat16), grads[pair], preferred_element_type=jnp.float32
                    )
                    dk_acc[keys, cols] += jnp.dot(
                        scores_low, queries[pair], preferred_element_type=jnp.float32
                    )
                    dq_flip[pair] += jnp.dot(
                        key_flip[cols, keys], scores_low, preferred_element_type=jnp.float32
                    )
                return unused

            lax.fori_loop(0, count, spread, 0)
            dims = lax.broadcasted_iota(jnp.int32, (TILE, TILE), 0)
            for pair, cols in enumerate(pairs):
                both = dq_flip[pair]
                dq_acc[rows, cols] = jnp.where(dims < HEAD, both[:, :TILE], both[:, TILE:]).T
            return unused

        @pl.when(third == 0)
        def _():
            dk_acc[...] = jnp.zeros_like(dk_acc)
            dv_acc[...] = jnp.zeros_like(dv_acc)
            key_flip[...] = k_ref[...].T
            lax.fori_loop(0, length // TILE, step, 0)
            out_ref[...] = (dq_acc[...] * score_scale).astype(jnp.bfloat16)

        @pl.when(third == 1)
        def _():
            out_ref[...] = (dk_acc[...] * score_scale).astype(jnp.bfloat16)

        @pl.when(third == 2)
        def _():
            out_ref[...] = dv_acc[...].astype(jnp.bfloat16)

    def column(place):
        return pl.BlockSpec((length, WIDE), lambda third, windows: (0, place))

    return pl.pallas_call(
        kernel,
        out_shape=jax.ShapeDtypeStruct(mixed.shape, jnp.bfloat16),
        grid_spec=pltpu.PrefetchScalarGridSpec(
            num_scalar_prefetch=1,
            grid=(3,),
            in_specs=[
                column(0),
                column(1),
                column(2),
                column(0),
                pl.BlockSpec((LOG_ROWS, length), lambda third, windows: (0, 0)),
                pl.BlockSpec((1, length), lambda third, windows: (0, 0)),
                pl.BlockSpec((length, TILE), lambda third, windows: (0, 0)),
            ],
            out_specs=pl.BlockSpec((length, WIDE), lambda third, windows: (0, third)),
            scratch_shapes=[pltpu.VMEM((PAIRS, length, 2 * TILE), jnp.float32)] * 2
            + [pltpu.VMEM((PAIRS, TILE, 2 * TILE), jnp.float32)]
            + [pltpu.VMEM((length, WIDE), jnp.float32)] * 3
            + [pltpu.VMEM((WIDE, length), jnp.bfloat16)],
        ),
        compiler_params=pltpu.CompilerParams(vmem_limit_bytes=VMEM_LIMIT),
        name="attention_backward",
    )(windows, mixed, mixed, mixed, grad_attended, log_sums, seg_row, seg_col)


def head_pass(pred_low, word_table, token_weight):
    length, width = pred_low.shape
    words = word_table.shape[0]
    tile, across = 1024, 256

    def kernel(
        pred_ref, table_ref, weight_ref, grad_table_ref, grad_pred_ref, log_ref, peak, total, grads
    ):
        phase, step = pl.program_id(0), pl.program_id(1)
        blocks = [
            (pl.ds(row, TILE), pl.ds(col, across))
            for col in range(0, length, across)
            for row in range(0, tile, TILE)
        ]

        @pl.when((phase == 0) & (step == 0))
        def _():
            peak[...] = jnp.full_like(peak, -1e30)
            total[...] = jnp.zeros_like(total)
            grad_pred_ref[...] = jnp.zeros_like(grad_pred_ref)

        @pl.when(phase == 0)
        def _():
            for rows, cols in blocks:
                logits = fold(nt_dot(table_ref[rows, :], pred_ref[cols, :]) * LOG2E)
                old = peak[:, cols]
                new = jnp.maximum(old, jnp.max(logits, 0))
                raised = jnp.sum(jnp.exp2(logits - new[None]), 0)
                total[:, cols] = total[:, cols] * jnp.exp2(old - new) + raised
                peak[:, cols] = new

        @pl.when((phase == 1) & (step == 0))
        def _():
            top = jnp.max(peak[...], 0, keepdims=True)
            sums = jnp.sum(total[...] * jnp.exp2(peak[...] - top), 0, keepdims=True)
            logs = top + jnp.log2(sums)
            log_ref[...] = logs / LOG2E
            weight = weight_ref[...]
            down = jnp.where(weight > 0.0, jnp.log2(weight), -1e30)
            peak[...] = jnp.broadcast_to(logs - down, peak.shape)

        @pl.when(phase == 1)
        def _():
            for rows, cols in blocks:
                logits = nt_dot(table_ref[rows, :], pred_ref[cols, :])
                lowered = fold(logits * LOG2E) - peak[:, cols][None]
                grads[rows, cols] = (
                    jnp.exp2(lowered).reshape(TILE, across).astype(jnp.bfloat16)
                )
            grad_table_ref[...] = jnp.dot(
                grads[...], pred_ref[...], preferred_element_type=jnp.float32
            )
            grad_pred_ref[...] += tn_dot(table_ref[...], grads[...])

    def whole(shape):
        return pl.BlockSpec(shape, lambda phase, step: (0, 0))

    return pl.pallas_call(
        kernel,
        out_shape=(
            jax.ShapeDtypeStruct((words, width), jnp.float32),
            jax.ShapeDtypeStruct((width, length), jnp.float32),
            jax.ShapeDtypeStruct((1, length), jnp.float32),
        ),
        grid_spec=pltpu.PrefetchScalarGridSpec(
            num_scalar_prefetch=0,
            grid=(2, words // tile),
            in_specs=[
                whole((length, width)),
                pl.BlockSpec((tile, width), lambda phase, step: (step, 0)),
                whole((1, length)),
            ],
            out_specs=[
                pl.BlockSpec((tile, width), lambda phase, step: (phase * step, 0)),
                whole((width, length)),
                whole((1, length)),
            ],
            scratch_shapes=[pltpu.VMEM((8, length), jnp.float32)] * 2
            + [pltpu.VMEM((tile, length), jnp.bfloat16)],
        ),
        compiler_params=pltpu.CompilerParams(vmem_limit_bytes=VMEM_LIMIT),
        name="head_pass",
    )(pred_low, word_table, token_weight)


def adam_rule(master, moment, second, grad, rate, decay):
    moment_new = BETA_ONE * moment + (1.0 - BETA_ONE) * grad
    second_new = BETA_TWO * second + (1.0 - BETA_TWO) * grad * grad
    moment_hat = moment_new / (1.0 - BETA_ONE**ADAM_STEP)
    second_hat = second_new / (1.0 - BETA_TWO**ADAM_STEP)
    master_new = master - rate * (moment_hat / (jnp.sqrt(second_hat) + ADAM_EPS) + decay * master)
    return [moment_new, second_new, master_new]


def adam_update(factor, masters, moments, seconds, grads):
    count = len(masters) - 1
    shapes = [member.shape for member in masters[:count]]

    def kernel(factor_ref, *refs):
        small, refs = refs[:4], refs[4:]
        sources, targets = refs[: 4 * count], refs[4 * count : 7 * count]
        small_out, refs = refs[7 * count : 7 * count + 3], refs[7 * count + 3 :]
        held, load_sems, store_sems = refs[:count], refs[count], refs[count + 1]
        loads = []
        for at in range(count):
            for kind in range(4):
                loads.append(
                    pltpu.make_async_copy(
                        sources[kind * count + at], held[at].at[kind], load_sems.at[at, kind]
                    )
                )
                loads[-1].start()
        scale = factor_ref[0]
        values = [ref[...] for ref in small]
        values[3] = scale * values[3]
        for kind, value in enumerate(adam_rule(*values, RATES[count], DECAYS[count])):
            small_out[kind][...] = value
        stores = []
        for at in range(count):
            for kind in range(4):
                loads[4 * at + kind].wait()
            values = [held[at][kind] for kind in range(4)]
            values[3] = scale * values[3]
            for kind, value in enumerate(adam_rule(*values, RATES[at], DECAYS[at])):
                held[at][4 + kind] = value
                stores.append(
                    pltpu.make_async_copy(
                        held[at].at[4 + kind], targets[3 * at + kind], store_sems.at[at, kind]
                    )
                )
                stores[-1].start()
        for store in stores:
            store.wait()

    kinds = (masters, moments, seconds, grads)
    return pl.pallas_call(
        kernel,
        out_shape=[
            jax.ShapeDtypeStruct(member.shape, jnp.float32) for member in masters for kind in range(3)
        ],
        in_specs=[pl.BlockSpec(memory_space=pltpu.SMEM)]
        + [pl.BlockSpec(memory_space=pltpu.VMEM)] * 4
        + [pl.BlockSpec(memory_space=pltpu.HBM)] * (4 * count),
        out_specs=[pl.BlockSpec(memory_space=pltpu.HBM)] * (3 * count)
        + [pl.BlockSpec(memory_space=pltpu.VMEM)] * 3,
        scratch_shapes=[pltpu.VMEM((7,) + shape, jnp.float32) for shape in shapes]
        + [pltpu.SemaphoreType.DMA((count, 4)), pltpu.SemaphoreType.DMA((count, 3))],
        compiler_params=pltpu.CompilerParams(vmem_limit_bytes=60 << 20),
        name="adam_update",
    )(
        factor.reshape(1),
        *[members[count] for members in kinds],
        *[member for members in kinds for member in members[:count]],
    )


AXES = ("bucket", "dp")


class Place:
    def __init__(self, buckets, columns):
        self.buckets, self.columns = buckets, columns
        self.count = buckets * columns
        self.line = columns // 2
        self.bits = [1 << place for place in range(1, columns.bit_length() - 1)]
        self.offsets = [0]
        for bit in reversed(self.bits):
            self.offsets += [offset ^ (bit >> 1) for offset in self.offsets]
        self.square = lax.axis_index("bucket")
        along = lax.axis_index("dp")
        self.core = along % 2
        self.along = along // 2
        self.flat = self.square * columns + along
        self.step_a = 1 + self.core
        self.step_b = 2 - self.core

    def swap(self, array, pick):
        pairs = [(member, member ^ pick(member)) for member in range(self.count)]
        return lax.ppermute(array, AXES, pairs)

    def swap_core(self, array):
        return self.swap(array, lambda member: 1)

    def swap_a(self, array):
        return self.swap(array, lambda member: self.columns * (1 + member % 2))

    def swap_b(self, array):
        return self.swap(array, lambda member: self.columns * (2 - member % 2))

    def swap_line(self, array, bit):
        return self.swap(array, lambda member: bit)

    def total(self, array):
        array = array + self.swap_core(array)
        spans = [self.columns, 2 * self.columns] + self.bits
        for at in range(0, len(spans), 2):
            near, *more = spans[at : at + 2]
            parts = [self.swap_line(array, near)]
            for far in more:
                parts += [self.swap_line(array, far), self.swap_line(array, near ^ far)]
            array = array + sum(parts)
        return array


def assemble(place, pieces):
    twice, rows, cols = pieces[0].shape
    line = twice // 2
    flags = jnp.stack([place.square, place.along, place.core]).astype(jnp.int32)

    def kernel(flags_ref, *refs):
        piece_refs, out_ref, held, load_sems, store_sem = refs[:4], *refs[4:]
        square, along, core = flags_ref[0], flags_ref[1], flags_ref[2]
        step_a, step_b = 1 + core, 2 - core
        spots = [
            (0, (square, square ^ step_a), core),
            (2, (square, square ^ step_b), 1 - core),
            (1, (square ^ step_b, square ^ 3), core),
            (3, (square ^ step_a, square ^ 3), 1 - core),
        ]
        loads = [
            pltpu.make_async_copy(piece_ref, held.at[at], load_sems.at[at])
            for at, piece_ref in enumerate(piece_refs)
        ]
        for load in loads:
            load.start()
        for at, quarters, side in spots:
            loads[at].wait()
            for half, quarter in enumerate(quarters):
                for order, offset in enumerate(place.offsets):
                    pltpu.make_async_copy(
                        held.at[at, half * line + order],
                        out_ref.at[quarter, along ^ offset, side],
                        store_sem,
                    ).start()
        pltpu.make_async_copy(out_ref, out_ref, store_sem).wait()

    gathered = pl.pallas_call(
        kernel,
        out_shape=jax.ShapeDtypeStruct((4, line, 2, rows, cols), pieces[0].dtype),
        grid_spec=pltpu.PrefetchScalarGridSpec(
            num_scalar_prefetch=1,
            grid=(1,),
            in_specs=[pl.BlockSpec(memory_space=pltpu.HBM)] * 4,
            out_specs=pl.BlockSpec(memory_space=pltpu.HBM),
            scratch_shapes=[
                pltpu.VMEM((4, twice, rows, cols), pieces[0].dtype),
                pltpu.SemaphoreType.DMA((4,)),
                pltpu.SemaphoreType.DMA(()),
            ],
        ),
        compiler_params=pltpu.CompilerParams(vmem_limit_bytes=VMEM_LIMIT),
        name="assemble",
    )(flags, *pieces)
    return gathered.reshape(8 * line * rows, cols)


def product_half(left, right):
    half = right.shape[1] // 2

    def half_of(side):
        return matmul_tn(left, lax.dynamic_slice_in_dim(right, side * half, half, 1))

    return half_of


def column_half(array):
    half = array.shape[1] // 2
    return lambda side: lax.dynamic_slice_in_dim(array, side * half, half, 1)


def scatter_halves(place, table, spots, rows):
    words, width = table.shape
    half = words // 2
    each = half // place.count
    length = rows.shape[0]
    flag = place.core.astype(jnp.int32).reshape(1)

    def kernel(spots_ref, flag_ref, table_ref, rows_ref, send_ref, keep_ref, held, load_sem, sems):
        for owner in range(place.count):
            for side in range(2):
                pltpu.make_async_copy(
                    table_ref.at[pl.ds((2 * owner + side) * each, each)],
                    held.at[pl.ds(side * half + owner * each, each)],
                    load_sem,
                ).start()
        pltpu.make_async_copy(table_ref, held, load_sem).wait()

        def step(at, unused):
            for more in range(16):
                place_at = pl.ds(spots_ref[at * 16 + more], 1)
                held[place_at, :] += rows_ref[pl.ds(at * 16 + more, 1), :]
            return unused

        lax.fori_loop(0, length // 16, step, 0)
        core = flag_ref[0]
        first = pltpu.make_async_copy(held.at[pl.ds((1 - core) * half, half)], send_ref, sems.at[0])
        second = pltpu.make_async_copy(held.at[pl.ds(core * half, half)], keep_ref, sems.at[1])
        first.start()
        second.start()
        first.wait()
        second.wait()

    return pl.pallas_call(
        kernel,
        out_shape=[jax.ShapeDtypeStruct((half, width), jnp.float32)] * 2,
        grid_spec=pltpu.PrefetchScalarGridSpec(
            num_scalar_prefetch=2,
            grid=(1,),
            in_specs=[
                pl.BlockSpec(memory_space=pltpu.HBM),
                pl.BlockSpec((length, width), lambda step, spots, flag: (0, 0)),
            ],
            out_specs=[pl.BlockSpec(memory_space=pltpu.HBM)] * 2,
            scratch_shapes=[
                pltpu.VMEM((words, width), jnp.float32),
                pltpu.SemaphoreType.DMA(()),
                pltpu.SemaphoreType.DMA((2,)),
            ],
        ),
        compiler_params=pltpu.CompilerParams(vmem_limit_bytes=VMEM_LIMIT),
        name="scatter_halves",
    )(spots, flag, table, rows)


def join(held, arrived):
    return jnp.concatenate([held, arrived], 0)


class Reduction:
    def __init__(self, place, half_of, stack=False, exact=False, short=False):
        self.place, self.half_of = place, half_of
        self.stack, self.exact, self.short = stack, exact, short

    def whole(self, pieces):
        return pieces[0] if len(pieces) == 1 else jnp.concatenate(pieces, 1)

    def to_core(self):
        return self.half_of(1 - self.place.core)

    def keep(self, pieces=None):
        self.kept_pieces = self.half_of(self.place.core) if pieces is None else pieces
        self.halves = [piece.shape[1] for piece in self.kept_pieces]
        self.quarter_rows = self.kept_pieces[0].shape[0] // 4
        self.rows = self.kept_pieces[0].shape[0] // self.place.count

    def quarter(self, index):
        start = index * self.quarter_rows

        def rows(piece):
            return lax.dynamic_slice_in_dim(piece, start, self.quarter_rows, 0)

        return self.whole(
            [rows(kept) + rows(came) for kept, came in zip(self.kept_pieces, self.across)]
        )

    def lower(self, array):
        if not self.exact:
            return array.astype(jnp.bfloat16)
        last = array[..., -TILE:][..., : TILE // 2]
        rounded = lax.reduce_precision(last, 8, 7)
        both = jnp.concatenate([rounded, last - rounded], -1)
        return jnp.concatenate([array[..., :-TILE], both], -1).astype(jnp.bfloat16)

    def lift(self, array):
        array = array.astype(jnp.float32)
        if not self.exact:
            return array
        rounded, rest = array[..., -TILE : -TILE // 2], array[..., -TILE // 2 :]
        both = jnp.concatenate([rounded + rest, jnp.zeros_like(rest)], -1)
        return jnp.concatenate([array[..., :-TILE], both], -1)

    def to_a(self, across):
        self.across = across
        square = self.place.square
        pair = [self.quarter(square ^ self.place.step_a), self.quarter(square ^ 3)]
        return jnp.stack([self.lower(member) for member in pair])

    def to_b(self, from_a):
        self.from_a = from_a
        mixed = self.quarter(self.place.square ^ self.place.step_b)
        return self.lower(mixed + self.lift(from_a[1]))

    def from_b(self, from_b):
        own = self.quarter(self.place.square)
        own = own + self.lift(self.from_a[0]) + self.lift(from_b)
        self.own = own.reshape(self.place.line, 2, self.rows, own.shape[-1])
        self.along = self.place.along

    def to_line(self):
        split = self.own.reshape((self.own.shape[0] // 2, 2) + self.own.shape[1:])
        mine = self.along % 2
        self.along = self.along // 2
        self.own = lax.dynamic_index_in_dim(split, mine, 1, False)
        other = lax.dynamic_index_in_dim(split, 1 - mine, 1, False)
        return other.astype(jnp.bfloat16) if self.short else other

    def from_line(self, arrived):
        self.own = self.own + arrived.astype(jnp.float32)

    def to_end(self):
        own = self.own[0]
        self.kept = lax.dynamic_index_in_dim(own, self.place.core, 0, False)
        return lax.dynamic_index_in_dim(own, 1 - self.place.core, 0, False)

    def finish(self, other):
        results, start = [], 0
        for half in self.halves:
            kept, came = self.kept[:, start : start + half], other[:, start : start + half]
            start += half
            axis = 0 if self.stack else 1
            results.append(
                jnp.where(
                    self.place.core == 0,
                    jnp.concatenate([kept, came], axis),
                    jnp.concatenate([came, kept], axis),
                )
            )
        return results


def on_device(
    token_ids,
    segment_ids,
    live,
    timesteps,
    noise,
    embedding,
    embedding_moment,
    embedding_second,
    up_weight,
    up_moment,
    up_second,
    time_weight,
    time_moment,
    time_second,
    qkv_weight,
    qkv_moment,
    qkv_second,
    out_weight,
    out_moment,
    out_second,
    fc_weight,
    fc_moment,
    fc_second,
    proj_weight,
    proj_moment,
    proj_second,
    down_weight,
    down_moment,
    down_second,
    norm_gains,
    gains_moment,
    gains_second,
):
    masters = (
        embedding,
        up_weight,
        time_weight,
        qkv_weight,
        out_weight,
        fc_weight,
        proj_weight,
        down_weight,
        norm_gains,
    )
    moments = (
        embedding_moment,
        up_moment,
        time_moment,
        qkv_moment,
        out_moment,
        fc_moment,
        proj_moment,
        down_moment,
        gains_moment,
    )
    seconds = (
        embedding_second,
        up_second,
        time_second,
        qkv_second,
        out_second,
        fc_second,
        proj_second,
        down_second,
        gains_second,
    )
    place = Place(lax.axis_size("bucket"), lax.axis_size("dp"))
    buckets = place.buckets
    step_span = STEPS_T // buckets
    tokens = token_ids[0]
    step_row = timesteps[0]
    live_float = live[0].astype(jnp.float32)
    onehot = (
        (step_row // step_span)[:, None] == jnp.arange(buckets, dtype=jnp.int32)[None, :]
    ).astype(jnp.float32)
    count_own = jnp.sum(live_float[:, None] * onehot, 0)
    count_high = jnp.floor(count_own / 32.0)
    aside = jnp.concatenate([count_high, count_own - 32.0 * count_high]).astype(jnp.bfloat16)
    low = [member.astype(jnp.bfloat16) for member in masters]
    own_rows = low[3].shape[0]
    gains_pad = jnp.concatenate(
        [
            low[8].T,
            jnp.broadcast_to(aside[None, :], (own_rows, 2 * buckets)),
            jnp.zeros((own_rows, EMB - 3 - 2 * buckets), jnp.bfloat16),
        ],
        1,
    )
    model_width = low[3].shape[1] // 3
    ff_width = low[5].shape[1]

    table = low[0][None]
    entry = jnp.concatenate([low[1].T, low[2].T, gains_pad], 1)[None]
    qkv = low[3][None]
    leave = jnp.concatenate([low[4].T, low[5], low[6].T, low[7]], 1)[None]
    fraction = step_row.astype(jnp.float32) / STEPS_T
    alpha_bar = 1.0 - jnp.sqrt(fraction + 0.0001)
    keep_root = jnp.sqrt(alpha_bar)[:, None]
    seg_col = jnp.broadcast_to(segment_ids.T, (segment_ids.shape[1], TILE))
    windows = key_windows(segment_ids[0])
    down_bits = place.bits[::-1]

    for bit in down_bits[:-1]:
        table = join(table, place.swap_line(table, bit))
        entry = join(entry, place.swap_line(entry, bit))
        table, entry, windows = tie(table, entry, windows)
    table = join(table, place.swap_line(table, down_bits[-1]))
    entry = join(entry, place.swap_line(entry, down_bits[-1]))
    for bit in down_bits[:-1]:
        entry, qkv = tie(entry, qkv)
        qkv = join(qkv, place.swap_line(qkv, bit))
    table, entry, qkv, leave, step_row = tie(table, entry, qkv, leave, step_row)
    feature_low = sinusoid(step_row, D).astype(jnp.bfloat16)
    table = join(table, place.swap_a(table))
    entry = join(entry, place.swap_a(entry))
    qkv = join(qkv, place.swap_line(qkv, down_bits[-1]))
    for bit in down_bits[:-1]:
        leave = join(leave, place.swap_line(leave, bit))
    table, entry, qkv = tie(table, entry, qkv)
    table_pieces = [table, place.swap_b(table), place.swap_core(table)]
    entry_pieces = [entry, place.swap_b(entry), place.swap_core(entry)]
    *both, qkv, leave, feature_low = tie(*table_pieces, *entry_pieces, qkv, leave, feature_low)
    table_pieces, entry_pieces = both[:3], both[3:]
    table_pieces.append(place.swap_core(table_pieces[1]))
    entry_pieces.append(place.swap_core(entry_pieces[1]))
    qkv_a = place.swap_a(qkv)
    leave = join(leave, place.swap_line(leave, down_bits[-1]))
    entry_low = assemble(place, entry_pieces)
    word_table = assemble(place, table_pieces)
    word_table, qkv_a, qkv = tie(word_table, qkv_a, qkv)
    qkv_half = join(qkv, qkv_a)
    qkv_pieces = [qkv_half, place.swap_b(qkv_half), place.swap_core(qkv_half)]
    up_low = entry_low[:, :EMB]
    time_low = entry_low[:, EMB : EMB + model_width]
    aside_low = entry_low[:, EMB + model_width :]
    gain_rows = aside_low[:, :3].T.astype(jnp.float32)
    shares = aside_low.reshape(place.count, own_rows, EMB)[:, 0, 3 : 3 + 2 * buckets]
    count_sums = jnp.sum(shares.astype(jnp.float32), 0)
    counts = 32.0 * count_sums[:buckets] + count_sums[buckets:]
    token_weight = live_float * jnp.sum(onehot / counts[None, :], -1) / buckets

    start_emb = word_table[tokens].astype(jnp.float32)
    noisy_emb = keep_root * start_emb + jnp.sqrt(1.0 - alpha_bar)[:, None] * noise[0]
    noisy_low = noisy_emb.astype(jnp.bfloat16)
    hidden_zero = matrix_product_transposed(noisy_low, up_low) + matrix_product_transposed(
        feature_low, time_low
    )
    normed, scaled_one, inverse_one = layer_normalize(hidden_zero, gain_rows[0])
    normed_one_low = normed.astype(jnp.bfloat16)
    *qkv_pieces, normed_one_low, leave = tie(*qkv_pieces, normed_one_low, leave)
    leave_a = place.swap_a(leave)
    qkv_pieces.append(place.swap_core(qkv_pieces[1]))
    qkv_low = assemble(place, qkv_pieces)
    mixed_low = matmul(normed_one_low, qkv_low).astype(jnp.bfloat16)
    segments = (segment_ids, seg_col, windows)
    leave_a, leave, mixed_low = tie(leave_a, leave, mixed_low)
    leave_half, mixed_low = tie(join(leave, leave_a), mixed_low)
    leave_pieces = [leave_half, place.swap_b(leave_half), place.swap_core(leave_half)]
    attended_low, log_sums = attention_forward(mixed_low, *segments)
    *leave_pieces, attended_low = tie(*leave_pieces, attended_low)
    leave_pieces.append(place.swap_core(leave_pieces[1]))
    leave_low = assemble(place, leave_pieces)
    out_low = leave_low[:, :model_width]
    fc_low = leave_low[:, model_width : model_width + ff_width]
    proj_low = leave_low[:, model_width + ff_width : model_width + 2 * ff_width]
    down_low = leave_low[:, model_width + 2 * ff_width :]
    hidden_one = hidden_zero + matrix_product_transposed(attended_low, out_low)
    normed, scaled_two, inverse_two = layer_normalize(hidden_one, gain_rows[1])
    normed_two_low = normed.astype(jnp.bfloat16)
    fc_upper = matmul(normed_two_low, fc_low)
    active_low = jax.nn.gelu(fc_upper).astype(jnp.bfloat16)
    hidden_two = hidden_one + matrix_product_transposed(active_low, proj_low)
    normed, scaled_top, inverse_top = layer_normalize(hidden_two, gain_rows[2])
    normed_top_low = normed.astype(jnp.bfloat16)
    prediction = matmul(normed_top_low, down_low)
    pred_low = prediction.astype(jnp.bfloat16)
    grad_table_head, grad_pred_head, log_total = head_pass(
        pred_low, word_table, token_weight[None, :]
    )

    pred_float = pred_low.astype(jnp.float32)
    target = jnp.sum(pred_float * start_emb, -1)
    cross_loss = log_total[0] - target
    target_prob = jnp.exp(target - log_total[0])
    target_shift = lax.reduce_precision(
        token_weight * (target_prob - 1.0), 8, 7
    ) - lax.reduce_precision(token_weight * target_prob, 8, 7)
    target_shift = target_shift[:, None]
    pred_gap = prediction - start_emb
    loss_local = jnp.sum(token_weight * (jnp.mean(pred_gap * pred_gap, -1) + cross_loss))
    grad_mse = token_weight[:, None] * 2.0 * pred_gap / EMB
    grad_pred_low = (grad_mse + grad_pred_head.T + target_shift * start_emb).astype(jnp.bfloat16)
    grad_down = matmul_tn(normed_top_low, grad_pred_low)
    grad_two, grad_gain_top = norm_back(
        matrix_product_transposed(grad_pred_low, down_low), scaled_top, inverse_top, gain_rows[2]
    )

    bits = list(place.bits)
    grad_two_low = grad_two.astype(jnp.bfloat16)
    proj_half = product_half(grad_two_low, active_low)
    proj = Reduction(place, lambda side: [proj_half(side)], short=True)
    proj_send, grad_two_low = tie(*proj.to_core(), grad_two_low)
    proj_came = place.swap_core(proj_send)
    proj.keep()
    unused_value, gelu_pull = jax.vjp(jax.nn.gelu, fc_upper)
    (grad_upper,) = gelu_pull(matmul(grad_two_low, proj_low))
    grad_upper_low = grad_upper.astype(jnp.bfloat16)
    proj_came, grad_upper_low = tie(proj_came, grad_upper_low)
    proj_send, grad_upper_low = tie(proj.to_a([proj_came]), grad_upper_low)
    proj_came = place.swap_a(proj_send)
    fc_half = product_half(normed_two_low, grad_upper_low)
    fc = Reduction(place, lambda side: [fc_half(side)], short=True)
    fc_send, grad_upper_low = tie(*fc.to_core(), grad_upper_low)
    fc_came = place.swap_core(fc_send)
    fc.keep()
    grad_normed_two = matrix_product_transposed(grad_upper_low, fc_low)
    back_two, grad_gain_two = norm_back(grad_normed_two, scaled_two, inverse_two, gain_rows[1])
    grad_one = grad_two + back_two
    grad_one_low = grad_one.astype(jnp.bfloat16)
    proj_came, fc_came, grad_one_low = tie(proj_came, fc_came, grad_one_low)
    proj_send, fc_send, grad_one_low = tie(
        proj.to_b(proj_came), fc.to_a([fc_came]), grad_one_low
    )
    proj_came, fc_came = place.swap_b(proj_send), place.swap_a(fc_send)
    grad_out = matmul_tn(grad_one_low, attended_low)
    grad_attended = matmul(grad_one_low, out_low).astype(jnp.bfloat16)
    lanes = lax.broadcasted_iota(jnp.int32, (model_width, 2 * TILE), 1)
    exact = jnp.where(lanes == 1, grad_gain_two[:, None], 0.0)
    exact = jnp.where(lanes == 2, grad_gain_top[:, None], exact)
    exact = jnp.where(lanes == 3, loss_local, exact)
    grad_out, exact, grad_attended, proj_came = tie(grad_out, exact, grad_attended, proj_came)
    proj.from_b(proj_came)
    proj_send, grad_attended = tie(proj.to_line(), grad_attended)
    proj_came = place.swap_line(proj_send, bits[0])
    grad_mixed = attention_backward(mixed_low, grad_attended, log_sums, *segments)

    proj_came, fc_came, grad_mixed = tie(proj_came, fc_came, grad_mixed)
    proj.from_line(proj_came)
    proj_send, fc_send, grad_mixed = tie(proj.to_line(), fc.to_b(fc_came), grad_mixed)
    proj_came, fc_came = place.swap_line(proj_send, bits[1]), place.swap_b(fc_send)
    out_half, qkv_half = column_half(grad_out), product_half(normed_one_low, grad_mixed)
    mix = Reduction(place, lambda side: [out_half(side), qkv_half(side)])
    *mix_send, grad_mixed = tie(*mix.to_core(), grad_mixed)
    mix_came = [place.swap_core(piece) for piece in mix_send]
    grad_normed_one = matrix_product_transposed(grad_mixed, qkv_low)
    back_one, grad_gain_one = norm_back(grad_normed_one, scaled_one, inverse_one, gain_rows[0])
    grad_zero = grad_one + back_one
    proj_came, fc_came, grad_zero = tie(proj_came, fc_came, grad_zero)
    proj.from_line(proj_came)
    fc.from_b(fc_came)
    fc_send, grad_zero = tie(fc.to_line(), grad_zero)
    fc_came = place.swap_line(fc_send, bits[0])
    grad_zero_low = grad_zero.astype(jnp.bfloat16)
    grad_start = matmul(grad_zero_low, up_low)
    grad_start = keep_root * grad_start - grad_mse + target_shift * pred_float
    mix.keep()
    *mix_came, grad_start = tie(*mix_came, grad_start)
    mix_send, grad_start = tie(mix.to_a(mix_came), grad_start)
    mix_came = place.swap_a(mix_send)

    own_words = word_table.shape[0] // place.count // 2
    if own_words % 8 == 0:
        owner, spot = tokens // (2 * own_words), tokens % (2 * own_words)
        spot = (spot // own_words * place.count + owner) * own_words + spot % own_words
        words_send, words_kept = scatter_halves(place, grad_table_head, spot, grad_start)
    else:
        grad_table = grad_table_head.at[tokens].add(grad_start)
        split = grad_table.reshape(place.count, 2, own_words, EMB)
        words_send, words_kept = [
            lax.dynamic_index_in_dim(split, side, 1, False).reshape(-1, EMB)
            for side in (1 - place.core, place.core)
        ]
    words = Reduction(place, None, stack=True)
    words.keep([words_kept])
    words_send, fc_came, grad_zero_low = tie(words_send, fc_came, grad_zero_low)
    words_came = place.swap_core(words_send)
    fc.from_line(fc_came)
    time_half = product_half(grad_zero_low, feature_low)
    pair_half = column_half(jnp.concatenate([matmul_tn(grad_zero_low, noisy_low), grad_down], 1))
    exact_half = column_half(jnp.where(lanes == 0, grad_gain_one[:, None], exact))
    rest = Reduction(
        place, lambda side: [time_half(side), pair_half(side), exact_half(side)], exact=True
    )
    *rest_send, mix_came, words_came = tie(*rest.to_core(), mix_came, words_came)
    rest_came = [place.swap_core(piece) for piece in rest_send]
    words_send = words.to_a([words_came])
    words_send, mix_came = tie(words_send, mix_came)
    words_came = place.swap_a(words_send)
    fc_send, mix_send = tie(fc.to_line(), mix.to_b(mix_came))
    fc_came, mix_came = place.swap_line(fc_send, bits[1]), place.swap_b(mix_send)
    rest.keep()
    *rest_came, words_came = tie(*rest_came, words_came)
    words_send, rest_send = tie(words.to_b(words_came), rest.to_a(rest_came))
    words_came, rest_came = place.swap_b(words_send), place.swap_a(rest_send)
    mix_came, words_came = tie(mix_came, words_came)
    mix.from_b(mix_came)
    words.from_b(words_came)
    words_send, mix_send = tie(words.to_line(), mix.to_line())
    words_came = place.swap_line(words_send, bits[0])
    mix_came = place.swap_line(mix_send, bits[0])
    rest_came, fc_came, words_came = tie(rest_came, fc_came, words_came)
    words.from_line(words_came)
    fc.from_line(fc_came)
    words_send, rest_send = tie(words.to_line(), rest.to_b(rest_came))
    words_came, rest_came = place.swap_line(words_send, bits[1]), place.swap_b(rest_send)
    mix_came, rest_came = tie(mix_came, rest_came)
    mix.from_line(mix_came)
    rest.from_b(rest_came)
    rest_send, mix_send = tie(rest.to_line(), mix.to_line())
    rest_came = place.swap_line(rest_send, bits[0])
    mix_came = place.swap_line(mix_send, bits[1])
    words_came, rest_came = tie(words_came, rest_came)
    words.from_line(words_came)
    rest.from_line(rest_came)
    rest_came = place.swap_line(rest.to_line(), bits[1])
    mix_came, rest_came = tie(mix_came, rest_came)
    mix.from_line(mix_came)
    rest.from_line(rest_came)
    members = (proj, fc, mix, rest, words)
    for bit in bits[2:]:
        for member in members:
            member.from_line(place.swap_line(member.to_line(), bit))
    squares_local = jnp.zeros((), jnp.float32)
    for member in members:
        own = member.own[0]
        if member.exact:
            lanes = lax.broadcasted_iota(jnp.int32, own.shape, own.ndim - 1)
            aside = (place.core == 0) & (lanes == own.shape[-1] - TILE + 3)
            own = jnp.where(aside, 0.0, own)
        squares_local = squares_local + jnp.sum(own * own)
    ends = [member.finish(place.swap_core(member.to_end())) for member in members]
    (shard_proj,), (shard_fc,), (shard_out, shard_qkv), rest_ends, (shard_table,) = ends
    shard_time, shard_pair, shard_exact = rest_ends
    loss_sum = shard_exact[0, 3]
    shards = (
        shard_table,
        shard_pair[:, :EMB],
        shard_time,
        shard_qkv,
        shard_out,
        shard_fc,
        shard_proj,
        shard_pair[:, EMB:],
        shard_exact[:, :3].T,
    )
    squares = place.total(jnp.full((8, EMB), squares_local))[0, 0]
    grad_norm = jnp.sqrt(squares)
    factor = CLIP_NORM / jnp.maximum(grad_norm, CLIP_NORM)
    flips = (False, True, True, False, True, False, True, False, False)

    def lay(members):
        return [member.T if flip else member for member, flip in zip(members, flips)]

    results = adam_update(factor, lay(masters), lay(moments), lay(seconds), shards)
    results = [result.T if flips[at // 3] else result for at, result in enumerate(results)]
    return (
        loss_sum,
        grad_norm,
        results[0],
        results[1],
        results[2],
        results[3],
        results[4],
        results[5],
        results[6],
        results[7],
        results[8],
        results[9],
        results[10],
        results[11],
        results[12],
        results[13],
        results[14],
        results[15],
        results[16],
        results[17],
        results[18],
        results[19],
        results[20],
        results[21],
        results[22],
        results[23],
        results[24],
        results[25],
        results[26],
    )


def solution(mesh):
    return jax.shard_map(
        on_device,
        mesh=mesh,
        in_specs=(
            P(("bucket", "dp"), None),
            P(("bucket", "dp"), None),
            P(("bucket", "dp"), None),
            P(("bucket", "dp"), None),
            P(("bucket", "dp"), None, None),
            P(("bucket", "dp"), None),
            P(("bucket", "dp"), None),
            P(("bucket", "dp"), None),
            P(None, ("bucket", "dp")),
            P(None, ("bucket", "dp")),
            P(None, ("bucket", "dp")),
            P(None, ("bucket", "dp")),
            P(None, ("bucket", "dp")),
            P(None, ("bucket", "dp")),
            P(("bucket", "dp"), None),
            P(("bucket", "dp"), None),
            P(("bucket", "dp"), None),
            P(None, ("bucket", "dp")),
            P(None, ("bucket", "dp")),
            P(None, ("bucket", "dp")),
            P(("bucket", "dp"), None),
            P(("bucket", "dp"), None),
            P(("bucket", "dp"), None),
            P(None, ("bucket", "dp")),
            P(None, ("bucket", "dp")),
            P(None, ("bucket", "dp")),
            P(("bucket", "dp"), None),
            P(("bucket", "dp"), None),
            P(("bucket", "dp"), None),
            P(None, ("bucket", "dp")),
            P(None, ("bucket", "dp")),
            P(None, ("bucket", "dp")),
        ),
        out_specs=(
            P(),
            P(),
            P(("bucket", "dp"), None),
            P(("bucket", "dp"), None),
            P(("bucket", "dp"), None),
            P(None, ("bucket", "dp")),
            P(None, ("bucket", "dp")),
            P(None, ("bucket", "dp")),
            P(None, ("bucket", "dp")),
            P(None, ("bucket", "dp")),
            P(None, ("bucket", "dp")),
            P(("bucket", "dp"), None),
            P(("bucket", "dp"), None),
            P(("bucket", "dp"), None),
            P(None, ("bucket", "dp")),
            P(None, ("bucket", "dp")),
            P(None, ("bucket", "dp")),
            P(("bucket", "dp"), None),
            P(("bucket", "dp"), None),
            P(("bucket", "dp"), None),
            P(None, ("bucket", "dp")),
            P(None, ("bucket", "dp")),
            P(None, ("bucket", "dp")),
            P(("bucket", "dp"), None),
            P(("bucket", "dp"), None),
            P(("bucket", "dp"), None),
            P(None, ("bucket", "dp")),
            P(None, ("bucket", "dp")),
            P(None, ("bucket", "dp")),
        ),
        check_vma=False,
    )
```

```python
import math

import jax
import jax.numpy as jnp
from jax import lax
from jax.experimental import pallas as pl
from jax.experimental.pallas import tpu as pltpu
from jax.sharding import PartitionSpec as P

D = 768
HEAD = 64
EMB = 128
STEPS_T = 2000
ADAM_STEP = 10


NEG_BIG = -1e30
EPS_NORM = 1e-05
BETA_ONE = 0.9
BETA_TWO = 0.95
ADAM_EPS = 1e-08
DECAY_RATE = 0.01
CLIP_NORM = 0.02
RATES = (0.05, 0.05, 0.02, 0.02, 0.02, 0.02, 0.01, 0.02, 0.3)
DECAYS = (DECAY_RATE,) * 8 + (0.0,)


def matmul(left_op, right_op):
    return jnp.dot(left_op, right_op, preferred_element_type=jnp.float32)


def matmul_tn(left_op, right_op):
    return lax.dot_general(
        left_op, right_op, (((0,), (0,)), ((), ())), preferred_element_type=jnp.float32
    )


def matrix_product_transposed(left_op, right_op):
    return lax.dot_general(
        left_op, right_op, (((1,), (1,)), ((), ())), preferred_element_type=jnp.float32
    )


def layer_normalize(hidden, gain_row):
    centre = jnp.mean(hidden, -1, keepdims=True)
    centred = hidden - centre
    spread = jnp.mean(centred * centred, -1, keepdims=True)
    scale_inv = lax.rsqrt(spread + EPS_NORM)
    normed = centred * scale_inv
    return (normed * gain_row, normed, scale_inv)


def gelu_and_slope(upper):
    root, cube = math.sqrt(2.0 / math.pi), 0.044715
    square = upper * upper
    bend = jnp.tanh(upper * (root + root * cube * square))
    half = 0.5 + 0.5 * bend
    steep = root + 3.0 * root * cube * square
    return upper * half, half + 0.5 * upper * (1.0 - bend * bend) * steep


def norm_back(grad_normed_out, normed, scale_inv, gain_row):
    grad_gain = jnp.sum(grad_normed_out * normed, 0)
    grad_scaled = grad_normed_out * gain_row
    grad_input = scale_inv * (
        grad_scaled
        - jnp.mean(grad_scaled, -1, keepdims=True)
        - normed * jnp.mean(grad_scaled * normed, -1, keepdims=True)
    )
    return (grad_input, grad_gain)


def sinusoid(step_row, model_width):
    half_width = model_width // 2
    freqs = jnp.exp(-math.log(10000.0) * jnp.arange(half_width, dtype=jnp.float32) / half_width)
    angles = step_row.astype(jnp.float32)[:, None] * freqs[None, :]
    return jnp.concatenate([jnp.sin(angles), jnp.cos(angles)], -1)


TILE = 128
LOG2E = math.log2(math.e)


def tie(*arrays):
    return lax.optimization_barrier(arrays)


def key_windows(segments):
    length = segments.shape[0]
    blocks = segments.reshape(-1, TILE)
    shared = jnp.any(blocks[:, :, None] == segments[None, None, :], 1)
    places = jnp.arange(length, dtype=jnp.int32)[None, :]
    first = jnp.min(jnp.where(shared, places, length), 1) // TILE * TILE
    last = jnp.max(jnp.where(shared, places, -1), 1) + 1
    spans = (last - first + KEYS - 1) // KEYS
    first = jnp.minimum(first, length - spans * KEYS)
    return jnp.stack([first, spans]).astype(jnp.int32)


def nt_dot(left, right):
    return lax.dot_general(
        left, right, (((1,), (1,)), ((), ())), preferred_element_type=jnp.float32
    )


def tn_dot(left, right):
    return lax.dot_general(
        left, right, (((0,), (0,)), ((), ())), preferred_element_type=jnp.float32
    )


def head_stack(pair):
    lanes = lax.broadcasted_iota(jnp.int32, pair.shape, 1)
    zero = jnp.zeros_like(pair)
    return jnp.concatenate(
        [jnp.where(lanes < HEAD, pair, zero), jnp.where(lanes >= HEAD, pair, zero)], 0
    )


def fold(array):
    return array.reshape(-1, 8, array.shape[-1])


PAIRS = D // TILE
WIDE = PAIRS * TILE
KEYS = 256
LOG_ROWS = -(-2 * PAIRS // 8) * 8


def attention_forward(mixed, seg_row, seg_col, windows):
    length, width = mixed.shape[0], mixed.shape[1] // 3
    groups = width // WIDE
    factor = HEAD ** (-0.5) * LOG2E

    def kernel(windows_ref, q_ref, k_ref, v_ref, row_ref, col_ref, o_ref, log_ref, held, out, flip):
        flip[...] = v_ref[...].T

        def step(block, unused):
            rows = pl.ds(pl.multiple_of(block * TILE, TILE), TILE)
            start, count = windows_ref[0, block], windows_ref[1, block]
            row = row_ref[:, rows]
            queries = [head_stack(q_ref[rows, pl.ds(pair * TILE, TILE)]) for pair in range(PAIRS)]

            def keys_at(at):
                return pl.ds(pl.multiple_of(start + at * KEYS, TILE), KEYS)

            def held_at(at):
                return pl.ds(pl.multiple_of(at * KEYS, KEYS), KEYS)

            def score(at, state):
                keys = keys_at(at)
                same = col_ref[keys, :] == row
                same = jnp.concatenate([same, same], 1)
                found = []
                for pair in range(PAIRS):
                    old, total = state[pair]
                    scores = nt_dot(k_ref[keys, pl.ds(pair * TILE, TILE)], queries[pair])
                    scores = jnp.where(same, scores * factor, NEG_BIG)
                    held[pair, held_at(at), :] = scores
                    scores = fold(scores)
                    new = jnp.maximum(old, jnp.max(scores, 0))
                    raised = jnp.sum(jnp.exp2(scores - new[None]), 0)
                    found.append((new, total * jnp.exp2(old - new) + raised))
                return tuple(found)

            low = jnp.full((8, 2 * TILE), NEG_BIG, jnp.float32)
            state = lax.fori_loop(0, count, score, ((low, jnp.zeros_like(low)),) * PAIRS)
            logs = []
            for peak, total in state:
                top = jnp.max(peak, 0, keepdims=True)
                total = jnp.sum(total * jnp.exp2(peak - top), 0, keepdims=True)
                logs.append(top + jnp.log2(total))
            out[...] = jnp.zeros_like(out)

            def spread(at, unused):
                for pair in range(PAIRS):
                    probs = jnp.exp2(held[pair, held_at(at), :] - logs[pair]).astype(jnp.bfloat16)
                    out[pair] += jnp.dot(
                        flip[pl.ds(pair * TILE, TILE), keys_at(at)],
                        probs,
                        preferred_element_type=jnp.float32,
                    )
                return unused

            lax.fori_loop(0, count, spread, 0)
            dims = lax.broadcasted_iota(jnp.int32, (TILE, TILE), 0)
            for pair in range(PAIRS):
                both = out[pair]
                chosen = jnp.where(dims < HEAD, both[:, :TILE], both[:, TILE:])
                o_ref[rows, pl.ds(pair * TILE, TILE)] = chosen.T.astype(jnp.bfloat16)
                log_ref[2 * pair : 2 * pair + 1, rows] = logs[pair][:, :TILE]
                log_ref[2 * pair + 1 : 2 * pair + 2, rows] = logs[pair][:, TILE:]
            return unused

        lax.fori_loop(0, length // TILE, step, 0)

    def column(place):
        return pl.BlockSpec((length, WIDE), lambda group, windows: (0, 3 * group + place))

    return pl.pallas_call(
        kernel,
        out_shape=(
            jax.ShapeDtypeStruct((length, width), jnp.bfloat16),
            jax.ShapeDtypeStruct((LOG_ROWS * groups, length), jnp.float32),
        ),
        grid_spec=pltpu.PrefetchScalarGridSpec(
            num_scalar_prefetch=1,
            grid=(groups,),
            in_specs=[
                column(0),
                column(1),
                column(2),
                pl.BlockSpec((1, length), lambda group, windows: (0, 0)),
                pl.BlockSpec((length, TILE), lambda group, windows: (0, 0)),
            ],
            out_specs=[
                pl.BlockSpec((length, WIDE), lambda group, windows: (0, group)),
                pl.BlockSpec((LOG_ROWS, length), lambda group, windows: (group, 0)),
            ],
            scratch_shapes=[
                pltpu.VMEM((PAIRS, length, 2 * TILE), jnp.float32),
                pltpu.VMEM((PAIRS, TILE, 2 * TILE), jnp.float32),
                pltpu.VMEM((WIDE, length), jnp.bfloat16),
            ],
        ),
        compiler_params=pltpu.CompilerParams(vmem_limit_bytes=28 << 20),
        name="attention_forward",
    )(windows, mixed, mixed, mixed, seg_row, seg_col)


def attention_backward(mixed, grad_attended, log_sums, seg_row, seg_col, windows):
    length = mixed.shape[0]
    score_scale = HEAD ** (-0.5)
    factor = score_scale * LOG2E

    def kernel(windows_ref, q_ref, k_ref, v_ref, do_ref, log_ref, row_ref, col_ref, *refs):
        out_ref, held, pulled, dq_flip, dq_acc, dk_acc, dv_acc, key_flip = refs
        third = pl.program_id(0)

        def step(block, unused):
            rows = pl.ds(pl.multiple_of(block * TILE, TILE), TILE)
            start, count = windows_ref[0, block], windows_ref[1, block]
            row = row_ref[:, rows]
            pairs = [pl.ds(pair * TILE, TILE) for pair in range(PAIRS)]
            queries = [head_stack(q_ref[rows, cols]) for cols in pairs]
            grads = [head_stack(do_ref[rows, cols]) for cols in pairs]
            logs = [
                jnp.concatenate(
                    [
                        log_ref[2 * pair : 2 * pair + 1, rows],
                        log_ref[2 * pair + 1 : 2 * pair + 2, rows],
                    ],
                    1,
                )
                for pair in range(PAIRS)
            ]

            def keys_at(at):
                return pl.ds(pl.multiple_of(start + at * KEYS, TILE), KEYS)

            def held_at(at):
                return pl.ds(pl.multiple_of(at * KEYS, KEYS), KEYS)

            def weigh(at, inners):
                keys = keys_at(at)
                same = col_ref[keys, :] == row
                same = jnp.concatenate([same, same], 1)
                found = []
                for pair, cols in enumerate(pairs):
                    scores = nt_dot(k_ref[keys, cols], queries[pair])
                    probs = jnp.where(same, jnp.exp2(scores * factor - logs[pair]), 0.0)
                    grad_probs = nt_dot(v_ref[keys, cols], grads[pair])
                    held[pair, held_at(at), :] = probs
                    pulled[pair, held_at(at), :] = grad_probs
                    found.append(inners[pair] + jnp.sum(fold(probs * grad_probs), 0))
                return tuple(found)

            zero = jnp.zeros((8, 2 * TILE), jnp.float32)
            inners = lax.fori_loop(0, count, weigh, (zero,) * PAIRS)
            inners = [jnp.sum(inner, 0, keepdims=True) for inner in inners]
            dq_flip[...] = jnp.zeros_like(dq_flip)

            def spread(at, unused):
                keys = keys_at(at)
                for pair, cols in enumerate(pairs):
                    probs = held[pair, held_at(at), :]
                    scores = probs * (pulled[pair, held_at(at), :] - inners[pair])
                    scores_low = scores.astype(jnp.bfloat16)
                    dv_acc[keys, cols] += jnp.dot(
                        probs.astype(jnp.bfloat16), grads[pair], preferred_element_type=jnp.float32
                    )
                    dk_acc[keys, cols] += jnp.dot(
                        scores_low, queries[pair], preferred_element_type=jnp.float32
                    )
                    dq_flip[pair] += jnp.dot(
                        key_flip[cols, keys], scores_low, preferred_element_type=jnp.float32
                    )
                return unused

            lax.fori_loop(0, count, spread, 0)
            dims = lax.broadcasted_iota(jnp.int32, (TILE, TILE), 0)
            for pair, cols in enumerate(pairs):
                both = dq_flip[pair]
                dq_acc[rows, cols] = jnp.where(dims < HEAD, both[:, :TILE], both[:, TILE:]).T
            return unused

        @pl.when(third == 0)
        def _():
            dk_acc[...] = jnp.zeros_like(dk_acc)
            dv_acc[...] = jnp.zeros_like(dv_acc)
            key_flip[...] = k_ref[...].T
            lax.fori_loop(0, length // TILE, step, 0)
            out_ref[...] = (dq_acc[...] * score_scale).astype(jnp.bfloat16)

        @pl.when(third == 1)
        def _():
            out_ref[...] = (dk_acc[...] * score_scale).astype(jnp.bfloat16)

        @pl.when(third == 2)
        def _():
            out_ref[...] = dv_acc[...].astype(jnp.bfloat16)

    def column(place):
        return pl.BlockSpec((length, WIDE), lambda third, windows: (0, place))

    return pl.pallas_call(
        kernel,
        out_shape=jax.ShapeDtypeStruct(mixed.shape, jnp.bfloat16),
        grid_spec=pltpu.PrefetchScalarGridSpec(
            num_scalar_prefetch=1,
            grid=(3,),
            in_specs=[
                column(0),
                column(1),
                column(2),
                column(0),
                pl.BlockSpec((LOG_ROWS, length), lambda third, windows: (0, 0)),
                pl.BlockSpec((1, length), lambda third, windows: (0, 0)),
                pl.BlockSpec((length, TILE), lambda third, windows: (0, 0)),
            ],
            out_specs=pl.BlockSpec((length, WIDE), lambda third, windows: (0, third)),
            scratch_shapes=[pltpu.VMEM((PAIRS, length, 2 * TILE), jnp.float32)] * 2
            + [pltpu.VMEM((PAIRS, TILE, 2 * TILE), jnp.float32)]
            + [pltpu.VMEM((length, WIDE), jnp.float32)] * 3
            + [pltpu.VMEM((WIDE, length), jnp.bfloat16)],
        ),
        compiler_params=pltpu.CompilerParams(vmem_limit_bytes=44 << 20),
        name="attention_backward",
    )(windows, mixed, mixed, mixed, grad_attended, log_sums, seg_row, seg_col)


def head_pass(pred_low, word_table, token_weight):
    length, width = pred_low.shape
    words = word_table.shape[0]
    tile, across = 1024, 256

    def kernel(
        pred_ref, table_ref, weight_ref, grad_table_ref, grad_pred_ref, log_ref, peak, total, grads
    ):
        phase, step = pl.program_id(0), pl.program_id(1)
        blocks = [
            (pl.ds(row, TILE), pl.ds(col, across))
            for col in range(0, length, across)
            for row in range(0, tile, TILE)
        ]

        @pl.when((phase == 0) & (step == 0))
        def _():
            peak[...] = jnp.full_like(peak, -1e30)
            total[...] = jnp.zeros_like(total)
            grad_pred_ref[...] = jnp.zeros_like(grad_pred_ref)

        @pl.when(phase == 0)
        def _():
            for rows, cols in blocks:
                logits = fold(nt_dot(table_ref[rows, :], pred_ref[cols, :]) * LOG2E)
                old = peak[:, cols]
                new = jnp.maximum(old, jnp.max(logits, 0))
                raised = jnp.sum(jnp.exp2(logits - new[None]), 0)
                total[:, cols] = total[:, cols] * jnp.exp2(old - new) + raised
                peak[:, cols] = new

        @pl.when((phase == 1) & (step == 0))
        def _():
            top = jnp.max(peak[...], 0, keepdims=True)
            sums = jnp.sum(total[...] * jnp.exp2(peak[...] - top), 0, keepdims=True)
            logs = top + jnp.log2(sums)
            log_ref[...] = logs / LOG2E
            weight = weight_ref[...]
            down = jnp.where(weight > 0.0, jnp.log2(weight), -1e30)
            peak[...] = jnp.broadcast_to(logs - down, peak.shape)

        @pl.when(phase == 1)
        def _():
            for rows, cols in blocks:
                logits = nt_dot(table_ref[rows, :], pred_ref[cols, :])
                lowered = fold(logits * LOG2E) - peak[:, cols][None]
                grads[rows, cols] = (
                    jnp.exp2(lowered).reshape(TILE, across).astype(jnp.bfloat16)
                )
            grad_table_ref[...] = jnp.dot(
                grads[...], pred_ref[...], preferred_element_type=jnp.float32
            )
            grad_pred_ref[...] += tn_dot(table_ref[...], grads[...])

    def whole(shape):
        return pl.BlockSpec(shape, lambda phase, step: (0, 0))

    return pl.pallas_call(
        kernel,
        out_shape=(
            jax.ShapeDtypeStruct((words, width), jnp.float32),
            jax.ShapeDtypeStruct((width, length), jnp.float32),
            jax.ShapeDtypeStruct((1, length), jnp.float32),
        ),
        grid_spec=pltpu.PrefetchScalarGridSpec(
            num_scalar_prefetch=0,
            grid=(2, words // tile),
            in_specs=[
                whole((length, width)),
                pl.BlockSpec((tile, width), lambda phase, step: (step, 0)),
                whole((1, length)),
            ],
            out_specs=[
                pl.BlockSpec((tile, width), lambda phase, step: (phase * step, 0)),
                whole((width, length)),
                whole((1, length)),
            ],
            scratch_shapes=[pltpu.VMEM((8, length), jnp.float32)] * 2
            + [pltpu.VMEM((tile, length), jnp.bfloat16)],
        ),
        compiler_params=pltpu.CompilerParams(vmem_limit_bytes=18 << 20),
        name="head_pass",
    )(pred_low, word_table, token_weight)


def adam_rule(master, moment, second, grad, rate, decay):
    moment_new = BETA_ONE * moment + (1.0 - BETA_ONE) * grad
    second_new = BETA_TWO * second + (1.0 - BETA_TWO) * grad * grad
    moment_hat = moment_new / (1.0 - BETA_ONE**ADAM_STEP)
    second_hat = second_new / (1.0 - BETA_TWO**ADAM_STEP)
    master_new = master - rate * (moment_hat / (jnp.sqrt(second_hat) + ADAM_EPS) + decay * master)
    return [moment_new, second_new, master_new]


def adam_update(factor, masters, moments, seconds, grads):
    count = len(masters) - 1
    shapes = [member.shape for member in masters[:count]]

    def kernel(factor_ref, *refs):
        small, refs = refs[:4], refs[4:]
        sources, targets = refs[: 4 * count], refs[4 * count : 7 * count]
        small_out, refs = refs[7 * count : 7 * count + 3], refs[7 * count + 3 :]
        held, load_sems, store_sems = refs[:count], refs[count], refs[count + 1]
        loads = []
        for at in range(count):
            for kind in range(4):
                loads.append(
                    pltpu.make_async_copy(
                        sources[kind * count + at], held[at].at[kind], load_sems.at[at, kind]
                    )
                )
                loads[-1].start()
        scale = factor_ref[0]
        values = [ref[...] for ref in small]
        values[3] = scale * values[3]
        for kind, value in enumerate(adam_rule(*values, RATES[count], DECAYS[count])):
            small_out[kind][...] = value
        stores = []
        for at in range(count):
            for kind in range(4):
                loads[4 * at + kind].wait()
            values = [held[at][kind] for kind in range(4)]
            values[3] = scale * values[3]
            for kind, value in enumerate(adam_rule(*values, RATES[at], DECAYS[at])):
                held[at][4 + kind] = value
                stores.append(
                    pltpu.make_async_copy(
                        held[at].at[4 + kind], targets[3 * at + kind], store_sems.at[at, kind]
                    )
                )
                stores[-1].start()
        for store in stores:
            store.wait()

    kinds = (masters, moments, seconds, grads)
    return pl.pallas_call(
        kernel,
        out_shape=[
            jax.ShapeDtypeStruct(member.shape, jnp.float32) for member in masters for kind in range(3)
        ],
        in_specs=[pl.BlockSpec(memory_space=pltpu.SMEM)]
        + [pl.BlockSpec(memory_space=pltpu.VMEM)] * 4
        + [pl.BlockSpec(memory_space=pltpu.HBM)] * (4 * count),
        out_specs=[pl.BlockSpec(memory_space=pltpu.HBM)] * (3 * count)
        + [pl.BlockSpec(memory_space=pltpu.VMEM)] * 3,
        scratch_shapes=[pltpu.VMEM((7,) + shape, jnp.float32) for shape in shapes]
        + [pltpu.SemaphoreType.DMA((count, 4)), pltpu.SemaphoreType.DMA((count, 3))],
        compiler_params=pltpu.CompilerParams(vmem_limit_bytes=60 << 20),
        name="adam_update",
    )(
        factor.reshape(1),
        *[members[count] for members in kinds],
        *[member for members in kinds for member in members[:count]],
    )


AXES = ("bucket", "dp")


class Place:
    def __init__(self, buckets, columns):
        self.buckets, self.columns = buckets, columns
        self.count = buckets * columns
        self.line = columns // 2
        self.bits = [1 << place for place in range(1, columns.bit_length() - 1)]
        self.offsets = [0]
        for bit in reversed(self.bits):
            self.offsets += [offset ^ (bit >> 1) for offset in self.offsets]
        self.square = lax.axis_index("bucket")
        along = lax.axis_index("dp")
        self.core = along % 2
        self.along = along // 2
        self.flat = self.square * columns + along
        self.step_a = 1 + self.core
        self.step_b = 2 - self.core

    def swap(self, array, pick):
        pairs = [(member, member ^ pick(member)) for member in range(self.count)]
        return lax.ppermute(array, AXES, pairs)

    def swap_core(self, array):
        return self.swap(array, lambda member: 1)

    def swap_a(self, array):
        return self.swap(array, lambda member: self.columns * (1 + member % 2))

    def swap_b(self, array):
        return self.swap(array, lambda member: self.columns * (2 - member % 2))

    def swap_line(self, array, bit):
        return self.swap(array, lambda member: bit)

    def total(self, array):
        array = array + self.swap_core(array)
        spans = [self.columns, 2 * self.columns] + self.bits
        for at in range(0, len(spans), 2):
            near, *more = spans[at : at + 2]
            parts = [self.swap_line(array, near)]
            for far in more:
                parts += [self.swap_line(array, far), self.swap_line(array, near ^ far)]
            array = array + sum(parts)
        return array


def assemble(place, pieces):
    twice, rows, cols = pieces[0].shape
    line = twice // 2
    flags = jnp.stack([place.square, place.along, place.core]).astype(jnp.int32)

    def kernel(flags_ref, *refs):
        piece_refs, out_ref, held, load_sems, store_sem = refs[:4], *refs[4:]
        square, along, core = flags_ref[0], flags_ref[1], flags_ref[2]
        step_a, step_b = 1 + core, 2 - core
        spots = [
            (0, (square, square ^ step_a), core),
            (2, (square, square ^ step_b), 1 - core),
            (1, (square ^ step_b, square ^ 3), core),
            (3, (square ^ step_a, square ^ 3), 1 - core),
        ]
        loads = [
            pltpu.make_async_copy(piece_ref, held.at[at], load_sems.at[at])
            for at, piece_ref in enumerate(piece_refs)
        ]
        for load in loads:
            load.start()
        for at, quarters, side in spots:
            loads[at].wait()
            for half, quarter in enumerate(quarters):
                for order, offset in enumerate(place.offsets):
                    pltpu.make_async_copy(
                        held.at[at, half * line + order],
                        out_ref.at[quarter, along ^ offset, side],
                        store_sem,
                    ).start()
        pltpu.make_async_copy(out_ref, out_ref, store_sem).wait()

    gathered = pl.pallas_call(
        kernel,
        out_shape=jax.ShapeDtypeStruct((4, line, 2, rows, cols), pieces[0].dtype),
        grid_spec=pltpu.PrefetchScalarGridSpec(
            num_scalar_prefetch=1,
            grid=(1,),
            in_specs=[pl.BlockSpec(memory_space=pltpu.HBM)] * 4,
            out_specs=pl.BlockSpec(memory_space=pltpu.HBM),
            scratch_shapes=[
                pltpu.VMEM((4, twice, rows, cols), pieces[0].dtype),
                pltpu.SemaphoreType.DMA((4,)),
                pltpu.SemaphoreType.DMA(()),
            ],
        ),
        compiler_params=pltpu.CompilerParams(vmem_limit_bytes=(2 << 20) + 8 * twice * cols * (-(-rows // 8) * 8)),
        name="assemble",
    )(flags, *pieces)
    return gathered.reshape(8 * line * rows, cols)


def product_half(left, right):
    half = right.shape[1] // 2

    def half_of(side):
        return matmul_tn(left, lax.dynamic_slice_in_dim(right, side * half, half, 1))

    return half_of


def column_half(array):
    half = array.shape[1] // 2
    return lambda side: lax.dynamic_slice_in_dim(array, side * half, half, 1)


def scatter_halves(place, table, spots, rows):
    words, width = table.shape
    half = words // 2
    each = half // place.count
    length = rows.shape[0]
    flag = place.core.astype(jnp.int32).reshape(1)

    def kernel(spots_ref, flag_ref, table_ref, rows_ref, send_ref, keep_ref, held, load_sem, sems):
        for owner in range(place.count):
            for side in range(2):
                pltpu.make_async_copy(
                    table_ref.at[pl.ds((2 * owner + side) * each, each)],
                    held.at[pl.ds(side * half + owner * each, each)],
                    load_sem,
                ).start()
        pltpu.make_async_copy(table_ref, held, load_sem).wait()

        def step(at, unused):
            for more in range(16):
                place_at = pl.ds(spots_ref[at * 16 + more], 1)
                held[place_at, :] += rows_ref[pl.ds(at * 16 + more, 1), :]
            return unused

        lax.fori_loop(0, length // 16, step, 0)
        core = flag_ref[0]
        first = pltpu.make_async_copy(held.at[pl.ds((1 - core) * half, half)], send_ref, sems.at[0])
        second = pltpu.make_async_copy(held.at[pl.ds(core * half, half)], keep_ref, sems.at[1])
        first.start()
        second.start()
        first.wait()
        second.wait()

    return pl.pallas_call(
        kernel,
        out_shape=[jax.ShapeDtypeStruct((half, width), jnp.float32)] * 2,
        grid_spec=pltpu.PrefetchScalarGridSpec(
            num_scalar_prefetch=2,
            grid=(1,),
            in_specs=[
                pl.BlockSpec(memory_space=pltpu.HBM),
                pl.BlockSpec((length, width), lambda step, spots, flag: (0, 0)),
            ],
            out_specs=[pl.BlockSpec(memory_space=pltpu.HBM)] * 2,
            scratch_shapes=[
                pltpu.VMEM((words, width), jnp.float32),
                pltpu.SemaphoreType.DMA(()),
                pltpu.SemaphoreType.DMA((2,)),
            ],
        ),
        compiler_params=pltpu.CompilerParams(vmem_limit_bytes=9 << 20),
        name="scatter_halves",
    )(spots, flag, table, rows)


def join(held, arrived):
    return jnp.concatenate([held, arrived], 0)


class Reduction:
    def __init__(self, place, kept, across, axis=1, exact=False, short=0):
        self.place, self.axis, self.exact, self.short = place, axis, exact, short
        self.rows = [piece.shape[0] // place.count for piece in kept]
        shapes = [
            (4, place.line // 2, 2, 2 * rows, piece.shape[1]) for rows, piece in zip(self.rows, kept)
        ]
        kept = [piece.reshape(shape) for piece, shape in zip(kept, shapes)]
        across = [piece.reshape(shape) for piece, shape in zip(across, shapes)]
        if axis == 1:
            self.parts = [(own, came, own.shape[4], 0) for own, came in zip(kept, across)]
        else:
            self.parts = [
                (own, came, TILE, block)
                for own, came in zip(kept, across)
                for block in range(own.shape[4] // TILE)
            ]
            self.rows = [own.shape[3] // 2 for own, unused, cols, block in self.parts]
        self.cols = [part[2] for part in self.parts]
        if axis == 1:
            self.span = (2 * self.rows[0], sum(self.cols))
        else:
            self.span = (2 * sum(self.rows), self.cols[0])
        self.level = 0

    def where(self, at):
        if self.axis == 1:
            start = sum(self.cols[:at])
            return slice(0, self.span[0]), slice(start, start + self.cols[at])
        start = 2 * sum(self.rows[:at])
        return slice(start, start + 2 * self.rows[at]), slice(0, self.span[1])

    def lower(self, at, value):
        if self.exact and at == len(self.cols) - 1:
            last = value[..., : TILE // 2]
            rounded = last.astype(jnp.bfloat16).astype(jnp.float32)
            value = jnp.concatenate([rounded, last - rounded], -1)
        return value.astype(jnp.bfloat16)

    def lift(self, at, value):
        value = value.astype(jnp.float32)
        if self.exact and at == len(self.cols) - 1:
            rounded, rest = value[..., : TILE // 2], value[..., TILE // 2 :]
            value = jnp.concatenate([rounded + rest, jnp.zeros_like(rest)], -1)
        return value

    def cast(self, at, value, ref):
        return self.lower(at, value) if ref.dtype == jnp.bfloat16 else value

    def took(self, at, value):
        return self.lift(at, value) if value.dtype == jnp.bfloat16 else value

    def call(self, name, kernel, steps, flags, inputs, outputs):
        return pl.pallas_call(
            kernel,
            out_shape=[entry for entry, unused, index in outputs],
            grid_spec=pltpu.PrefetchScalarGridSpec(
                num_scalar_prefetch=1,
                grid=(steps,),
                in_specs=[pl.BlockSpec(block, index) for unused, block, index in inputs],
                out_specs=[pl.BlockSpec(block, index) for unused, block, index in outputs],
            ),
            compiler_params=pltpu.CompilerParams(vmem_limit_bytes=40 << 20),
            name=name,
        )(jnp.stack(flags).astype(jnp.int32), *[array for array, unused, index in inputs])

    def pieces(self, block, index):
        entries = []
        for kept, across, cols, place in self.parts:

            def at_place(step, flags, place=place):
                return index(step, flags) + (place,)

            for array in (kept, across):
                entries.append((array, block + (array.shape[3], cols), at_place))
        return entries

    def to_a(self):
        square, line = self.place.square, self.place.line
        count = len(self.cols)

        def kernel(flags_ref, *refs):
            out_ref = refs[-1]
            for at in range(count):
                rows, cols = self.where(at)
                value = refs[2 * at][0] + refs[2 * at + 1][0]
                out_ref[0, :, :, rows, cols] = self.lower(at, value)

        shape = (2, line // 2, 2) + self.span
        (result,) = self.call(
            "reduce_first",
            kernel,
            2,
            [square ^ self.place.step_a, square ^ 3],
            self.pieces((1, line // 2, 2), lambda step, flags: (flags[step], 0, 0, 0)),
            [
                (
                    jax.ShapeDtypeStruct(shape, jnp.bfloat16),
                    (1,) + shape[1:],
                    lambda step, flags: (step, 0, 0, 0, 0),
                )
            ],
        )
        return result

    def came_a(self, refs, at, index):
        rows, cols = self.where(at)
        if len(self.from_a) > 1:
            return self.lift(at, refs[at][index + (slice(None), slice(None))])
        return self.lift(at, refs[0][index + (rows, cols)])

    def to_b(self, from_a):
        self.from_a = from_a
        line, count = self.place.line, len(self.cols)

        def kernel(flags_ref, *refs):
            out_ref, firsts = refs[-1], refs[2 * count : -1]
            for at in range(count):
                rows, cols = self.where(at)
                value = refs[2 * at][0] + refs[2 * at + 1][0]
                value = value + self.came_a(firsts, at, (0, slice(None), slice(None)))
                out_ref[:, :, rows, cols] = self.lower(at, value)

        shape = (line // 2, 2) + self.span
        (result,) = self.call(
            "reduce_second",
            kernel,
            1,
            [self.place.square ^ self.place.step_b],
            self.pieces((1, line // 2, 2), lambda step, flags: (flags[0], 0, 0, 0))
            + [
                (array, (1,) + array.shape[1:], lambda step, flags: (1, 0, 0, 0, 0))
                for array in from_a
            ],
            [(jax.ShapeDtypeStruct(shape, jnp.bfloat16), shape, lambda step, flags: (0, 0, 0, 0))],
        )
        return result

    def halves(self, lines):
        self.level += 1
        kinds = (jnp.bfloat16 if self.level <= self.short else jnp.float32, jnp.float32)
        shape = (lines,) + self.span
        return [
            (jax.ShapeDtypeStruct(shape, kind), shape, lambda step, flags: (0, 0, 0))
            for kind in kinds
        ]

    def to_line(self, from_b):
        line, count = self.place.line, len(self.cols)
        mine = self.place.along % 2
        self.along = self.place.along // 2

        def kernel(flags_ref, *refs):
            firsts, second_ref = refs[2 * count : -3], refs[-3]
            for step, out_ref in enumerate(refs[-2:]):

                @pl.when(pl.program_id(0) == step)
                def _():
                    for at in range(count):
                        rows, cols = self.where(at)
                        value = refs[2 * at][0, :, 0] + refs[2 * at + 1][0, :, 0]
                        value = value + self.came_a(firsts, at, (0, slice(None), 0))
                        value = value + self.lift(at, second_ref[:, 0, rows, cols])
                        out_ref[:, rows, cols] = self.cast(at, value, out_ref)

        send, self.own = self.call(
            "reduce_third",
            kernel,
            2,
            [self.place.square, 1 - mine, mine],
            self.pieces((1, line // 2, 1), lambda step, flags: (flags[0], 0, flags[1 + step], 0))
            + [
                (
                    array,
                    (1, line // 2, 1) + array.shape[3:],
                    lambda step, flags: (0, 0, flags[1 + step], 0, 0),
                )
                for array in self.from_a
            ]
            + [
                (
                    from_b,
                    (line // 2, 1) + self.span,
                    lambda step, flags: (0, flags[1 + step], 0, 0),
                )
            ],
            self.halves(line // 2),
        )
        return send

    def next_line(self, came):
        lines, count = self.own.shape[0] // 2, len(self.cols)
        mine = self.along % 2
        self.along = self.along // 2
        entries = [
            (
                array.reshape((lines, 2) + self.span),
                (lines, 1) + self.span,
                lambda step, flags: (0, flags[step], 0, 0),
            )
            for array in (self.own, came)
        ]

        def kernel(flags_ref, own_ref, came_ref, *out_refs):
            for step, out_ref in enumerate(out_refs):

                @pl.when(pl.program_id(0) == step)
                def _():
                    for at in range(count):
                        rows, cols = self.where(at)
                        value = own_ref[:, 0, rows, cols] + self.took(at, came_ref[:, 0, rows, cols])
                        out_ref[:, rows, cols] = self.cast(at, value, out_ref)

        send, self.own = self.call(
            "reduce_line", kernel, 2, [1 - mine, mine], entries, self.halves(lines)
        )
        return send

    def to_end(self, came):
        half, count = (self.span[0] // 2, self.span[1]), len(self.cols)

        def kernel(flags_ref, own_ref, came_ref, send_ref, keep_ref, squares_ref):
            first = flags_ref[0] == 0
            if came_ref.dtype == jnp.bfloat16 and self.exact:
                pieces = [self.took(at, came_ref[(0,) + self.where(at)]) for at in range(count)]
                came = jnp.concatenate(pieces, self.axis)
            else:
                came = came_ref[0].astype(jnp.float32)
            value = own_ref[0] + came
            squared = value * value
            if self.exact:
                spot_row = lax.broadcasted_iota(jnp.int32, squared.shape, 0)
                spot_lane = lax.broadcasted_iota(jnp.int32, squared.shape, 1)
                aside = (spot_lane == 3) & (spot_row >= self.span[0] - 2 * self.rows[-1])
                squared = jnp.where(aside & first, 0.0, squared)
            squares_ref[...] = jnp.full(squares_ref.shape, jnp.sum(squared), jnp.float32)
            groups = [self.rows[0]] if self.axis == 1 else self.rows
            start = 0
            for rows in groups:
                low, high = value[2 * start : 2 * start + rows], value[2 * start + rows : 2 * start + 2 * rows]
                send_ref[start : start + rows] = jnp.where(first, high, low)
                keep_ref[start : start + rows] = jnp.where(first, low, high)
                start += rows

        whole = (1,) + self.span
        send, self.last, self.squares = self.call(
            "reduce_last",
            kernel,
            1,
            [self.place.core],
            [(array, whole, lambda step, flags: (0, 0, 0)) for array in (self.own, came)],
            [
                (jax.ShapeDtypeStruct(shape, jnp.float32), shape, lambda step, flags: (0, 0))
                for shape in (half, half, (8, TILE))
            ],
        )
        return send

    def unpack(self, array):
        results, start = [], 0
        for size in self.cols if self.axis == 1 else self.rows:
            results.append(lax.slice_in_dim(array, start, start + size, axis=self.axis))
            start += size
        return results

    def finish(self, came):
        return self.unpack(self.last), self.unpack(came)


def in_order(place, kept, came, axis):
    return jnp.where(
        place.core == 0,
        jnp.concatenate([kept, came], axis),
        jnp.concatenate([came, kept], axis),
    )


def on_device(
    token_ids,
    segment_ids,
    live,
    timesteps,
    noise,
    embedding,
    embedding_moment,
    embedding_second,
    up_weight,
    up_moment,
    up_second,
    time_weight,
    time_moment,
    time_second,
    qkv_weight,
    qkv_moment,
    qkv_second,
    out_weight,
    out_moment,
    out_second,
    fc_weight,
    fc_moment,
    fc_second,
    proj_weight,
    proj_moment,
    proj_second,
    down_weight,
    down_moment,
    down_second,
    norm_gains,
    gains_moment,
    gains_second,
):
    masters = (
        embedding,
        up_weight,
        time_weight,
        qkv_weight,
        out_weight,
        fc_weight,
        proj_weight,
        down_weight,
        norm_gains,
    )
    moments = (
        embedding_moment,
        up_moment,
        time_moment,
        qkv_moment,
        out_moment,
        fc_moment,
        proj_moment,
        down_moment,
        gains_moment,
    )
    seconds = (
        embedding_second,
        up_second,
        time_second,
        qkv_second,
        out_second,
        fc_second,
        proj_second,
        down_second,
        gains_second,
    )
    place = Place(lax.axis_size("bucket"), lax.axis_size("dp"))
    buckets = place.buckets
    step_span = STEPS_T // buckets
    tokens = token_ids[0]
    step_row = timesteps[0]
    live_float = live[0].astype(jnp.float32)
    onehot = (
        (step_row // step_span)[:, None] == jnp.arange(buckets, dtype=jnp.int32)[None, :]
    ).astype(jnp.float32)
    count_own = jnp.sum(live_float[:, None] * onehot, 0)
    count_high = jnp.floor(count_own / 32.0)
    aside = jnp.concatenate([count_high, count_own - 32.0 * count_high]).astype(jnp.bfloat16)
    low = [member.astype(jnp.bfloat16) for member in masters]
    own_rows = low[3].shape[0]
    gains_pad = jnp.concatenate(
        [
            low[8].T,
            jnp.broadcast_to(aside[None, :], (own_rows, 2 * buckets)),
            jnp.zeros((own_rows, EMB - 3 - 2 * buckets), jnp.bfloat16),
        ],
        1,
    )
    model_width = low[3].shape[1] // 3
    ff_width = low[5].shape[1]

    table = low[0][None]
    entry = jnp.concatenate([low[1].T, low[2].T, gains_pad], 1)[None]
    qkv = low[3][None]
    leave = jnp.concatenate([low[4].T, low[5], low[6].T, low[7]], 1)[None]
    fraction = step_row.astype(jnp.float32) / STEPS_T
    alpha_bar = 1.0 - jnp.sqrt(fraction + 0.0001)
    keep_root = jnp.sqrt(alpha_bar)[:, None]
    seg_col = jnp.broadcast_to(segment_ids.T, (segment_ids.shape[1], TILE))
    windows = key_windows(segment_ids[0])
    down_bits = place.bits[::-1]

    for bit in down_bits[:-1]:
        table = join(table, place.swap_line(table, bit))
        entry = join(entry, place.swap_line(entry, bit))
        table, entry, windows = tie(table, entry, windows)
    table = join(table, place.swap_line(table, down_bits[-1]))
    entry = join(entry, place.swap_line(entry, down_bits[-1]))
    for bit in down_bits[:-1]:
        entry, qkv = tie(entry, qkv)
        qkv = join(qkv, place.swap_line(qkv, bit))
    table, entry, qkv, leave = tie(table, entry, qkv, leave)
    table_came, entry_came = place.swap_a(table), place.swap_a(entry)
    qkv_came = place.swap_line(qkv, down_bits[-1])
    for bit in down_bits[:-1]:
        leave = join(leave, place.swap_line(leave, bit))
    table_came, entry_came, qkv_came, step_row = tie(table_came, entry_came, qkv_came, step_row)
    feature_low = sinusoid(step_row, D).astype(jnp.bfloat16)
    table, entry, qkv = join(table, table_came), join(entry, entry_came), join(qkv, qkv_came)
    table_pieces = [table, place.swap_b(table), place.swap_core(table)]
    entry_pieces = [entry, place.swap_b(entry), place.swap_core(entry)]
    leave_came = place.swap_line(leave, down_bits[-1])
    *both, qkv, feature_low = tie(*table_pieces, *entry_pieces, qkv, feature_low)
    table_pieces, entry_pieces = both[:3], both[3:]
    table_pieces.append(place.swap_core(table_pieces[1]))
    entry_pieces.append(place.swap_core(entry_pieces[1]))
    qkv_came = place.swap_a(qkv)
    entry_low = assemble(place, entry_pieces)
    entry_low, qkv_came = tie(entry_low, qkv_came)
    qkv = join(qkv, qkv_came)
    qkv_pieces = [qkv, place.swap_b(qkv), place.swap_core(qkv)]
    qkv, table_pieces[0] = tie(qkv, table_pieces[0])
    word_table = assemble(place, table_pieces)
    word_table, leave_came = tie(word_table, leave_came)
    leave = join(leave, leave_came)
    leave_came = place.swap_a(leave)
    up_low = entry_low[:, :EMB]
    time_low = entry_low[:, EMB : EMB + model_width]
    aside_low = entry_low[:, EMB + model_width :]
    gain_rows = aside_low[:, :3].T.astype(jnp.float32)
    shares = aside_low.reshape(place.count, own_rows, EMB)[:, 0, 3 : 3 + 2 * buckets]
    count_sums = jnp.sum(shares.astype(jnp.float32), 0)
    counts = 32.0 * count_sums[:buckets] + count_sums[buckets:]
    token_weight = live_float * jnp.sum(onehot / counts[None, :], -1) / buckets

    start_emb = word_table[tokens].astype(jnp.float32)
    noisy_emb = keep_root * start_emb + jnp.sqrt(1.0 - alpha_bar)[:, None] * noise[0]
    noisy_low = noisy_emb.astype(jnp.bfloat16)
    hidden_zero = matrix_product_transposed(noisy_low, up_low) + matrix_product_transposed(
        feature_low, time_low
    )
    normed, scaled_one, inverse_one = layer_normalize(hidden_zero, gain_rows[0])
    normed_one_low = normed.astype(jnp.bfloat16)
    *qkv_pieces, normed_one_low = tie(*qkv_pieces, normed_one_low)
    qkv_pieces.append(place.swap_core(qkv_pieces[1]))
    qkv_low = assemble(place, qkv_pieces)
    leave_came, qkv_low = tie(leave_came, qkv_low)
    leave = join(leave, leave_came)
    leave_pieces = [leave, place.swap_b(leave), place.swap_core(leave)]
    mixed_low = matmul(normed_one_low, qkv_low).astype(jnp.bfloat16)
    segments = (segment_ids, seg_col, windows)
    attended_low, log_sums = attention_forward(mixed_low, *segments)
    *leave_pieces, attended_low = tie(*leave_pieces, attended_low)
    leave_pieces.append(place.swap_core(leave_pieces[1]))
    leave_low = assemble(place, leave_pieces)
    out_low = leave_low[:, :model_width]
    fc_low = leave_low[:, model_width : model_width + ff_width]
    proj_low = leave_low[:, model_width + ff_width : model_width + 2 * ff_width]
    down_low = leave_low[:, model_width + 2 * ff_width :]
    hidden_one = hidden_zero + matrix_product_transposed(attended_low, out_low)
    normed, scaled_two, inverse_two = layer_normalize(hidden_one, gain_rows[1])
    normed_two_low = normed.astype(jnp.bfloat16)
    active, slope = gelu_and_slope(matmul(normed_two_low, fc_low))
    active_low, slope = tie(active.astype(jnp.bfloat16), slope)
    hidden_two = hidden_one + matrix_product_transposed(active_low, proj_low)
    normed, scaled_top, inverse_top = layer_normalize(hidden_two, gain_rows[2])
    normed_top_low = normed.astype(jnp.bfloat16)
    prediction = matmul(normed_top_low, down_low)
    pred_low = prediction.astype(jnp.bfloat16)
    grad_table_head, grad_pred_head, log_total = head_pass(
        pred_low, word_table, token_weight[None, :]
    )

    pred_float = pred_low.astype(jnp.float32)
    target = jnp.sum(pred_float * start_emb, -1)
    cross_loss = log_total[0] - target
    target_prob = jnp.exp(target - log_total[0])
    target_shift = lax.reduce_precision(
        token_weight * (target_prob - 1.0), 8, 7
    ) - lax.reduce_precision(token_weight * target_prob, 8, 7)
    target_shift = target_shift[:, None]
    pred_gap = prediction - start_emb
    loss_local = jnp.sum(token_weight * (jnp.mean(pred_gap * pred_gap, -1) + cross_loss))
    grad_mse = token_weight[:, None] * 2.0 * pred_gap / EMB
    grad_pred_low = (grad_mse + grad_pred_head.T + target_shift * start_emb).astype(jnp.bfloat16)
    grad_down = matmul_tn(normed_top_low, grad_pred_low)
    grad_two, grad_gain_top = norm_back(
        matrix_product_transposed(grad_pred_low, down_low), scaled_top, inverse_top, gain_rows[2]
    )

    bits = list(place.bits)
    core = place.core
    grad_two_low = grad_two.astype(jnp.bfloat16)
    proj_half = product_half(grad_two_low, active_low)
    proj_send, grad_two_low = tie(proj_half(1 - core), grad_two_low)
    proj_came = place.swap_core(proj_send)
    proj_kept = proj_half(core)
    grad_upper_low = (slope * matmul(grad_two_low, proj_low)).astype(jnp.bfloat16)
    proj_came, grad_upper_low = tie(proj_came, grad_upper_low)
    proj = Reduction(place, [proj_kept], [proj_came])
    proj_send, grad_upper_low = tie(proj.to_a(), grad_upper_low)
    proj_a = place.swap_a(proj_send)
    fc_half = product_half(normed_two_low, grad_upper_low)
    fc_send, grad_upper_low = tie(fc_half(1 - core), grad_upper_low)
    fc_came = place.swap_core(fc_send)
    fc_kept = fc_half(core)
    grad_normed_two = matrix_product_transposed(grad_upper_low, fc_low)
    back_two, grad_gain_two = norm_back(grad_normed_two, scaled_two, inverse_two, gain_rows[1])
    grad_one = grad_two + back_two
    grad_one_low = grad_one.astype(jnp.bfloat16)
    proj_a, fc_came, grad_one_low = tie(proj_a, fc_came, grad_one_low)
    fc = Reduction(place, [fc_kept], [fc_came])
    fc_send, grad_one_low = tie(fc.to_a(), grad_one_low)
    fc_a = place.swap_a(fc_send)
    out_half = product_half(grad_one_low, attended_low)
    out_send, out_kept = out_half(1 - core), out_half(core)
    grad_attended = matmul(grad_one_low, out_low).astype(jnp.bfloat16)
    lanes = lax.broadcasted_iota(jnp.int32, (model_width, 2 * TILE), 1)
    exact = jnp.where(lanes == 1, grad_gain_two[:, None], 0.0)
    exact = jnp.where(lanes == 2, grad_gain_top[:, None], exact)
    exact = jnp.where(lanes == 3, loss_local, exact)
    out_send, out_kept, exact, grad_attended = tie(out_send, out_kept, exact, grad_attended)
    out_came = place.swap_core(out_send)
    grad_mixed = attention_backward(mixed_low, grad_attended, log_sums, *segments)

    fc_a, out_came, grad_mixed = tie(fc_a, out_came, grad_mixed)
    feed = Reduction(place, [proj_kept, fc_kept], [proj_came, fc_came], short=len(bits))
    feed_send, grad_mixed = tie(feed.to_b([proj_a, fc_a]), grad_mixed)
    feed_came = place.swap_b(feed_send)
    qkv_half = product_half(normed_one_low, grad_mixed)
    qkv_send, grad_mixed = tie(qkv_half(1 - core), grad_mixed)
    qkv_came = place.swap_core(qkv_send)
    grad_normed_one = matrix_product_transposed(grad_mixed, qkv_low)
    back_one, grad_gain_one = norm_back(grad_normed_one, scaled_one, inverse_one, gain_rows[0])
    grad_zero = grad_one + back_one
    feed_came, grad_zero = tie(feed_came, grad_zero)
    feed_send, grad_zero = tie(feed.to_line(feed_came), grad_zero)
    feed_came = place.swap_line(feed_send, bits[0])
    grad_zero_low = grad_zero.astype(jnp.bfloat16)
    grad_start = matmul(grad_zero_low, up_low)
    grad_start = keep_root * grad_start - grad_mse + target_shift * pred_float
    qkv_kept, qkv_came, grad_start = tie(qkv_half(core), qkv_came, grad_start)
    mix = Reduction(place, [out_kept, qkv_kept], [out_came, qkv_came], short=1)
    mix_send, grad_start = tie(mix.to_a(), grad_start)
    mix_came = place.swap_a(mix_send)

    own_words = word_table.shape[0] // place.count // 2
    if own_words % 8 == 0:
        owner, spot = tokens // (2 * own_words), tokens % (2 * own_words)
        spot = (spot // own_words * place.count + owner) * own_words + spot % own_words
        words_send, words_kept = scatter_halves(place, grad_table_head, spot, grad_start)
    else:
        grad_table = grad_table_head.at[tokens].add(grad_start)
        split = grad_table.reshape(place.count, 2, own_words, EMB)
        words_send, words_kept = [
            lax.dynamic_index_in_dim(split, side, 1, False).reshape(-1, EMB)
            for side in (1 - core, core)
        ]
    words_send, mix_came, feed_came, grad_zero_low = tie(
        words_send, mix_came, feed_came, grad_zero_low
    )
    words_came = place.swap_core(words_send)
    feed_send, mix_send, grad_zero_low = tie(
        feed.next_line(feed_came), mix.to_b([mix_came]), grad_zero_low
    )
    feed_came, mix_came = place.swap_line(feed_send, bits[1]), place.swap_b(mix_send)
    time_half = product_half(grad_zero_low, feature_low)
    pair_half = column_half(jnp.concatenate([matmul_tn(grad_zero_low, noisy_low), grad_down], 1))
    exact_half = column_half(jnp.where(lanes == 0, grad_gain_one[:, None], exact))

    def rest_half(side):
        return time_half(side), jnp.concatenate([pair_half(side), exact_half(side)], 1)

    rest_send = tie(*rest_half(1 - core))
    rest_came = [place.swap_core(piece) for piece in rest_send]
    rest_kept = rest_half(core)
    words_came, *rest_came = tie(words_came, *rest_came)
    late = Reduction(
        place, [words_kept, *rest_kept], [words_came, *rest_came], axis=0, exact=True
    )
    late_send, mix_came = tie(late.to_a(), mix_came)
    late_came = place.swap_a(late_send)
    mix_came = place.swap_line(mix.to_line(mix_came), bits[0])
    late_came, mix_came, feed_came = tie(late_came, mix_came, feed_came)
    late_send, mix_send = tie(late.to_b([late_came]), mix.next_line(mix_came))
    late_came, mix_came = place.swap_b(late_send), place.swap_line(mix_send, bits[1])
    (late_came,) = tie(late_came)
    late_came = place.swap_line(late.to_line(late_came), bits[0])
    late_came, mix_came = tie(late_came, mix_came)
    late_came = place.swap_line(late.next_line(late_came), bits[1])
    members, arrived = (feed, mix, late), [feed_came, mix_came, late_came]
    for bit in bits[2:]:
        arrived = [
            place.swap_line(member.next_line(came), bit) for member, came in zip(members, arrived)
        ]
    ends = [
        member.finish(place.swap_core(member.to_end(came))) for member, came in zip(members, arrived)
    ]
    squares_local = feed.squares + mix.squares + late.squares
    (proj_end, fc_end), (out_end, qkv_end), (words_end, *rest_ends) = [
        list(zip(*end)) for end in ends
    ]
    time_end = [jnp.concatenate(sides[:-2], 1) for sides in zip(*rest_ends)]
    pair_end, exact_end = rest_ends[-2:]
    shard_pair = in_order(place, *pair_end, 1)
    shard_exact = jnp.where(core == 0, *exact_end)
    loss_sum = shard_exact[0, 3]
    shards = (
        in_order(place, *words_end, 0),
        shard_pair[:, :EMB],
        in_order(place, *time_end, 1),
        in_order(place, *qkv_end, 1),
        in_order(place, *out_end, 1),
        in_order(place, *fc_end, 1),
        in_order(place, *proj_end, 1),
        shard_pair[:, EMB:],
        shard_exact[:, :3].T,
    )
    squares = place.total(squares_local)[0, 0]
    grad_norm = jnp.sqrt(squares)
    factor = CLIP_NORM / jnp.maximum(grad_norm, CLIP_NORM)
    flips = (False, True, True, False, True, False, True, False, False)

    def lay(members):
        return [member.T if flip else member for member, flip in zip(members, flips)]

    results = adam_update(factor, lay(masters), lay(moments), lay(seconds), shards)
    results = [result.T if flips[at // 3] else result for at, result in enumerate(results)]
    return (
        loss_sum,
        grad_norm,
        results[0],
        results[1],
        results[2],
        results[3],
        results[4],
        results[5],
        results[6],
        results[7],
        results[8],
        results[9],
        results[10],
        results[11],
        results[12],
        results[13],
        results[14],
        results[15],
        results[16],
        results[17],
        results[18],
        results[19],
        results[20],
        results[21],
        results[22],
        results[23],
        results[24],
        results[25],
        results[26],
    )


def solution(mesh):
    return jax.shard_map(
        on_device,
        mesh=mesh,
        in_specs=(
            P(("bucket", "dp"), None),
            P(("bucket", "dp"), None),
            P(("bucket", "dp"), None),
            P(("bucket", "dp"), None),
            P(("bucket", "dp"), None, None),
            P(("bucket", "dp"), None),
            P(("bucket", "dp"), None),
            P(("bucket", "dp"), None),
            P(None, ("bucket", "dp")),
            P(None, ("bucket", "dp")),
            P(None, ("bucket", "dp")),
            P(None, ("bucket", "dp")),
            P(None, ("bucket", "dp")),
            P(None, ("bucket", "dp")),
            P(("bucket", "dp"), None),
            P(("bucket", "dp"), None),
            P(("bucket", "dp"), None),
            P(None, ("bucket", "dp")),
            P(None, ("bucket", "dp")),
            P(None, ("bucket", "dp")),
            P(("bucket", "dp"), None),
            P(("bucket", "dp"), None),
            P(("bucket", "dp"), None),
            P(None, ("bucket", "dp")),
            P(None, ("bucket", "dp")),
            P(None, ("bucket", "dp")),
            P(("bucket", "dp"), None),
            P(("bucket", "dp"), None),
            P(("bucket", "dp"), None),
            P(None, ("bucket", "dp")),
            P(None, ("bucket", "dp")),
            P(None, ("bucket", "dp")),
        ),
        out_specs=(
            P(),
            P(),
            P(("bucket", "dp"), None),
            P(("bucket", "dp"), None),
            P(("bucket", "dp"), None),
            P(None, ("bucket", "dp")),
            P(None, ("bucket", "dp")),
            P(None, ("bucket", "dp")),
            P(None, ("bucket", "dp")),
            P(None, ("bucket", "dp")),
            P(None, ("bucket", "dp")),
            P(("bucket", "dp"), None),
            P(("bucket", "dp"), None),
            P(("bucket", "dp"), None),
            P(None, ("bucket", "dp")),
            P(None, ("bucket", "dp")),
            P(None, ("bucket", "dp")),
            P(("bucket", "dp"), None),
            P(("bucket", "dp"), None),
            P(("bucket", "dp"), None),
            P(None, ("bucket", "dp")),
            P(None, ("bucket", "dp")),
            P(None, ("bucket", "dp")),
            P(("bucket", "dp"), None),
            P(("bucket", "dp"), None),
            P(("bucket", "dp"), None),
            P(None, ("bucket", "dp")),
            P(None, ("bucket", "dp")),
            P(None, ("bucket", "dp")),
        ),
        check_vma=False,
    )
```

```python
import math

import jax
import jax.numpy as jnp
from jax import lax
from jax.experimental import pallas as pl
from jax.experimental.pallas import tpu as pltpu
from jax.sharding import PartitionSpec as P

D = 768
HEAD = 64
EMB = 128
STEPS_T = 2000
ADAM_STEP = 10


NEG_BIG = -1e30
EPS_NORM = 1e-05
BETA_ONE = 0.9
BETA_TWO = 0.95
ADAM_EPS = 1e-08
DECAY_RATE = 0.01
CLIP_NORM = 0.02
RATES = (0.05, 0.05, 0.02, 0.02, 0.02, 0.02, 0.01, 0.02, 0.3)
DECAYS = (DECAY_RATE,) * 8 + (0.0,)


def matmul(left_op, right_op):
    return jnp.dot(left_op, right_op, preferred_element_type=jnp.float32)


def matmul_tn(left_op, right_op):
    return lax.dot_general(
        left_op, right_op, (((0,), (0,)), ((), ())), preferred_element_type=jnp.float32
    )


def matrix_product_transposed(left_op, right_op):
    return lax.dot_general(
        left_op, right_op, (((1,), (1,)), ((), ())), preferred_element_type=jnp.float32
    )


def layer_normalize(hidden, gain_row):
    centre = jnp.mean(hidden, -1, keepdims=True)
    centred = hidden - centre
    spread = jnp.mean(centred * centred, -1, keepdims=True)
    scale_inv = lax.rsqrt(spread + EPS_NORM)
    normed = centred * scale_inv
    return (normed * gain_row, normed, scale_inv)


def gelu_and_slope(upper):
    root, cube = math.sqrt(2.0 / math.pi), 0.044715
    square = upper * upper
    bend = jnp.tanh(upper * (root + root * cube * square))
    half = 0.5 + 0.5 * bend
    steep = root + 3.0 * root * cube * square
    return upper * half, half + 0.5 * upper * (1.0 - bend * bend) * steep


def norm_back(grad_normed_out, normed, scale_inv, gain_row):
    grad_gain = jnp.sum(grad_normed_out * normed, 0)
    grad_scaled = grad_normed_out * gain_row
    grad_input = scale_inv * (
        grad_scaled
        - jnp.mean(grad_scaled, -1, keepdims=True)
        - normed * jnp.mean(grad_scaled * normed, -1, keepdims=True)
    )
    return (grad_input, grad_gain)


def sinusoid(step_row, model_width):
    half_width = model_width // 2
    freqs = jnp.exp(-math.log(10000.0) * jnp.arange(half_width, dtype=jnp.float32) / half_width)
    angles = step_row.astype(jnp.float32)[:, None] * freqs[None, :]
    return jnp.concatenate([jnp.sin(angles), jnp.cos(angles)], -1)


TILE = 128
LOG2E = math.log2(math.e)


def tie(*arrays):
    return lax.optimization_barrier(arrays)


def key_windows(segments):
    length = segments.shape[0]
    blocks = segments.reshape(-1, TILE)
    shared = jnp.any(blocks[:, :, None] == segments[None, None, :], 1)
    places = jnp.arange(length, dtype=jnp.int32)[None, :]
    first = jnp.min(jnp.where(shared, places, length), 1) // TILE * TILE
    last = jnp.max(jnp.where(shared, places, -1), 1) + 1
    spans = (last - first + KEYS - 1) // KEYS
    first = jnp.minimum(first, length - spans * KEYS)
    return jnp.stack([first, spans]).astype(jnp.int32)


def nt_dot(left, right):
    return lax.dot_general(
        left, right, (((1,), (1,)), ((), ())), preferred_element_type=jnp.float32
    )


def tn_dot(left, right):
    return lax.dot_general(
        left, right, (((0,), (0,)), ((), ())), preferred_element_type=jnp.float32
    )


def head_stack(pair):
    lanes = lax.broadcasted_iota(jnp.int32, pair.shape, 1)
    zero = jnp.zeros_like(pair)
    return jnp.concatenate(
        [jnp.where(lanes < HEAD, pair, zero), jnp.where(lanes >= HEAD, pair, zero)], 0
    )


def fold(array):
    return array.reshape(-1, 8, array.shape[-1])


PAIRS = D // TILE
WIDE = PAIRS * TILE
KEYS = 256
LOG_ROWS = -(-2 * PAIRS // 8) * 8


def attention_forward(mixed, seg_row, seg_col, windows):
    length, width = mixed.shape[0], mixed.shape[1] // 3
    groups = width // WIDE
    factor = HEAD ** (-0.5) * LOG2E

    def kernel(windows_ref, q_ref, k_ref, v_ref, row_ref, col_ref, o_ref, log_ref, held, out, flip):
        flip[...] = v_ref[...].T

        def step(block, unused):
            rows = pl.ds(pl.multiple_of(block * TILE, TILE), TILE)
            start, count = windows_ref[0, block], windows_ref[1, block]
            row = row_ref[:, rows]
            queries = [head_stack(q_ref[rows, pl.ds(pair * TILE, TILE)]) for pair in range(PAIRS)]

            def keys_at(at):
                return pl.ds(pl.multiple_of(start + at * KEYS, TILE), KEYS)

            def held_at(at):
                return pl.ds(pl.multiple_of(at * KEYS, KEYS), KEYS)

            def score(at, state):
                keys = keys_at(at)
                same = col_ref[keys, :] == row
                same = jnp.concatenate([same, same], 1)
                found = []
                for pair in range(PAIRS):
                    old, total = state[pair]
                    scores = nt_dot(k_ref[keys, pl.ds(pair * TILE, TILE)], queries[pair])
                    scores = jnp.where(same, scores * factor, NEG_BIG)
                    held[pair, held_at(at), :] = scores
                    scores = fold(scores)
                    new = jnp.maximum(old, jnp.max(scores, 0))
                    raised = jnp.sum(jnp.exp2(scores - new[None]), 0)
                    found.append((new, total * jnp.exp2(old - new) + raised))
                return tuple(found)

            low = jnp.full((8, 2 * TILE), NEG_BIG, jnp.float32)
            state = lax.fori_loop(0, count, score, ((low, jnp.zeros_like(low)),) * PAIRS)
            logs = []
            for peak, total in state:
                top = jnp.max(peak, 0, keepdims=True)
                total = jnp.sum(total * jnp.exp2(peak - top), 0, keepdims=True)
                logs.append(top + jnp.log2(total))
            out[...] = jnp.zeros_like(out)

            def spread(at, unused):
                for pair in range(PAIRS):
                    probs = jnp.exp2(held[pair, held_at(at), :] - logs[pair]).astype(jnp.bfloat16)
                    out[pair] += jnp.dot(
                        flip[pl.ds(pair * TILE, TILE), keys_at(at)],
                        probs,
                        preferred_element_type=jnp.float32,
                    )
                return unused

            lax.fori_loop(0, count, spread, 0)
            dims = lax.broadcasted_iota(jnp.int32, (TILE, TILE), 0)
            for pair in range(PAIRS):
                both = out[pair]
                chosen = jnp.where(dims < HEAD, both[:, :TILE], both[:, TILE:])
                o_ref[rows, pl.ds(pair * TILE, TILE)] = chosen.T.astype(jnp.bfloat16)
                log_ref[2 * pair : 2 * pair + 1, rows] = logs[pair][:, :TILE]
                log_ref[2 * pair + 1 : 2 * pair + 2, rows] = logs[pair][:, TILE:]
            return unused

        lax.fori_loop(0, length // TILE, step, 0)

    def column(place):
        return pl.BlockSpec((length, WIDE), lambda group, windows: (0, 3 * group + place))

    return pl.pallas_call(
        kernel,
        out_shape=(
            jax.ShapeDtypeStruct((length, width), jnp.bfloat16),
            jax.ShapeDtypeStruct((LOG_ROWS * groups, length), jnp.float32),
        ),
        grid_spec=pltpu.PrefetchScalarGridSpec(
            num_scalar_prefetch=1,
            grid=(groups,),
            in_specs=[
                column(0),
                column(1),
                column(2),
                pl.BlockSpec((1, length), lambda group, windows: (0, 0)),
                pl.BlockSpec((length, TILE), lambda group, windows: (0, 0)),
            ],
            out_specs=[
                pl.BlockSpec((length, WIDE), lambda group, windows: (0, group)),
                pl.BlockSpec((LOG_ROWS, length), lambda group, windows: (group, 0)),
            ],
            scratch_shapes=[
                pltpu.VMEM((PAIRS, length, 2 * TILE), jnp.float32),
                pltpu.VMEM((PAIRS, TILE, 2 * TILE), jnp.float32),
                pltpu.VMEM((WIDE, length), jnp.bfloat16),
            ],
        ),
        compiler_params=pltpu.CompilerParams(vmem_limit_bytes=28 << 20),
        name="attention_forward",
    )(windows, mixed, mixed, mixed, seg_row, seg_col)


def attention_backward(mixed, grad_attended, log_sums, seg_row, seg_col, windows):
    length = mixed.shape[0]
    score_scale = HEAD ** (-0.5)
    factor = score_scale * LOG2E

    def kernel(windows_ref, q_ref, k_ref, v_ref, do_ref, log_ref, row_ref, col_ref, *refs):
        out_ref, held, pulled, dq_flip, dq_acc, dk_acc, dv_acc, key_flip = refs
        third = pl.program_id(0)

        def step(block, unused):
            rows = pl.ds(pl.multiple_of(block * TILE, TILE), TILE)
            start, count = windows_ref[0, block], windows_ref[1, block]
            row = row_ref[:, rows]
            pairs = [pl.ds(pair * TILE, TILE) for pair in range(PAIRS)]
            queries = [head_stack(q_ref[rows, cols]) for cols in pairs]
            grads = [head_stack(do_ref[rows, cols]) for cols in pairs]
            logs = [
                jnp.concatenate(
                    [
                        log_ref[2 * pair : 2 * pair + 1, rows],
                        log_ref[2 * pair + 1 : 2 * pair + 2, rows],
                    ],
                    1,
                )
                for pair in range(PAIRS)
            ]

            def keys_at(at):
                return pl.ds(pl.multiple_of(start + at * KEYS, TILE), KEYS)

            def held_at(at):
                return pl.ds(pl.multiple_of(at * KEYS, KEYS), KEYS)

            def weigh(at, inners):
                keys = keys_at(at)
                same = col_ref[keys, :] == row
                same = jnp.concatenate([same, same], 1)
                found = []
                for pair, cols in enumerate(pairs):
                    scores = nt_dot(k_ref[keys, cols], queries[pair])
                    probs = jnp.where(same, jnp.exp2(scores * factor - logs[pair]), 0.0)
                    grad_probs = nt_dot(v_ref[keys, cols], grads[pair])
                    held[pair, held_at(at), :] = probs
                    pulled[pair, held_at(at), :] = grad_probs
                    found.append(inners[pair] + jnp.sum(fold(probs * grad_probs), 0))
                return tuple(found)

            zero = jnp.zeros((8, 2 * TILE), jnp.float32)
            inners = lax.fori_loop(0, count, weigh, (zero,) * PAIRS)
            inners = [jnp.sum(inner, 0, keepdims=True) for inner in inners]
            dq_flip[...] = jnp.zeros_like(dq_flip)

            def spread(at, unused):
                keys = keys_at(at)
                for pair, cols in enumerate(pairs):
                    probs = held[pair, held_at(at), :]
                    scores = probs * (pulled[pair, held_at(at), :] - inners[pair])
                    scores_low = scores.astype(jnp.bfloat16)
                    dv_acc[keys, cols] += jnp.dot(
                        probs.astype(jnp.bfloat16), grads[pair], preferred_element_type=jnp.float32
                    )
                    dk_acc[keys, cols] += jnp.dot(
                        scores_low, queries[pair], preferred_element_type=jnp.float32
                    )
                    dq_flip[pair] += jnp.dot(
                        key_flip[cols, keys], scores_low, preferred_element_type=jnp.float32
                    )
                return unused

            lax.fori_loop(0, count, spread, 0)
            dims = lax.broadcasted_iota(jnp.int32, (TILE, TILE), 0)
            for pair, cols in enumerate(pairs):
                both = dq_flip[pair]
                dq_acc[rows, cols] = jnp.where(dims < HEAD, both[:, :TILE], both[:, TILE:]).T
            return unused

        @pl.when(third == 0)
        def _():
            dk_acc[...] = jnp.zeros_like(dk_acc)
            dv_acc[...] = jnp.zeros_like(dv_acc)
            key_flip[...] = k_ref[...].T
            lax.fori_loop(0, length // TILE, step, 0)
            out_ref[...] = (dq_acc[...] * score_scale).astype(jnp.bfloat16)

        @pl.when(third == 1)
        def _():
            out_ref[...] = (dk_acc[...] * score_scale).astype(jnp.bfloat16)

        @pl.when(third == 2)
        def _():
            out_ref[...] = dv_acc[...].astype(jnp.bfloat16)

    def column(place):
        return pl.BlockSpec(
            (length, WIDE), lambda third, windows: (0, place), pipeline_mode=pl.Buffered(1)
        )

    return pl.pallas_call(
        kernel,
        out_shape=jax.ShapeDtypeStruct(mixed.shape, jnp.bfloat16),
        grid_spec=pltpu.PrefetchScalarGridSpec(
            num_scalar_prefetch=1,
            grid=(3,),
            in_specs=[
                column(0),
                column(1),
                column(2),
                column(0),
                pl.BlockSpec((LOG_ROWS, length), lambda third, windows: (0, 0)),
                pl.BlockSpec((1, length), lambda third, windows: (0, 0)),
                pl.BlockSpec((length, TILE), lambda third, windows: (0, 0)),
            ],
            out_specs=pl.BlockSpec((length, WIDE), lambda third, windows: (0, third)),
            scratch_shapes=[pltpu.VMEM((PAIRS, length, 2 * TILE), jnp.float32)] * 2
            + [pltpu.VMEM((PAIRS, TILE, 2 * TILE), jnp.float32)]
            + [pltpu.VMEM((length, WIDE), jnp.float32)] * 3
            + [pltpu.VMEM((WIDE, length), jnp.bfloat16)],
        ),
        compiler_params=pltpu.CompilerParams(vmem_limit_bytes=38 << 20),
        name="attention_backward",
    )(windows, mixed, mixed, mixed, grad_attended, log_sums, seg_row, seg_col)


def head_pass(pred_low, word_table, token_weight, small):
    length, width = pred_low.shape
    words = word_table.shape[0]
    tile, across = 1024, 256

    def kernel(
        small_ref, pred_ref, table_ref, weight_ref, grad_table_ref, grad_pred_ref, log_ref, peak, total, grads
    ):
        phase, step = pl.program_id(0), pl.program_id(1)
        blocks = [
            (pl.ds(row, TILE), pl.ds(col, across))
            for col in range(0, length, across)
            for row in range(0, tile, TILE)
        ]

        @pl.when((phase == 0) & (step == 0))
        def _():
            peak[...] = jnp.full_like(peak, jnp.where(small_ref[0] == 1, 0.0, -1e30))
            total[...] = jnp.zeros_like(total)
            grad_pred_ref[...] = jnp.zeros_like(grad_pred_ref)

        @pl.when((phase == 0) & (small_ref[0] == 1))
        def _():
            for rows, cols in blocks:
                logits = fold(nt_dot(table_ref[rows, :], pred_ref[cols, :]) * LOG2E)
                total[:, cols] += jnp.sum(jnp.exp2(logits), 0)

        @pl.when((phase == 0) & (small_ref[0] == 0))
        def _():
            for rows, cols in blocks:
                logits = fold(nt_dot(table_ref[rows, :], pred_ref[cols, :]) * LOG2E)
                old = peak[:, cols]
                new = jnp.maximum(old, jnp.max(logits, 0))
                raised = jnp.sum(jnp.exp2(logits - new[None]), 0)
                total[:, cols] = total[:, cols] * jnp.exp2(old - new) + raised
                peak[:, cols] = new

        @pl.when((phase == 1) & (step == 0))
        def _():
            top = jnp.max(peak[...], 0, keepdims=True)
            sums = jnp.sum(total[...] * jnp.exp2(peak[...] - top), 0, keepdims=True)
            logs = top + jnp.log2(sums)
            log_ref[...] = logs / LOG2E
            weight = weight_ref[...]
            down = jnp.where(weight > 0.0, jnp.log2(weight), -1e30)
            peak[...] = jnp.broadcast_to(logs - down, peak.shape)

        @pl.when(phase == 1)
        def _():
            for rows, cols in blocks:
                logits = nt_dot(table_ref[rows, :], pred_ref[cols, :])
                lowered = fold(logits * LOG2E) - peak[:, cols][None]
                grads[rows, cols] = (
                    jnp.exp2(lowered).reshape(TILE, across).astype(jnp.bfloat16)
                )
            grad_table_ref[...] = jnp.dot(
                grads[...], pred_ref[...], preferred_element_type=jnp.float32
            )
            grad_pred_ref[...] += tn_dot(table_ref[...], grads[...])

    def whole(shape):
        return pl.BlockSpec(shape, lambda phase, step, small: (0, 0))

    return pl.pallas_call(
        kernel,
        out_shape=(
            jax.ShapeDtypeStruct((words, width), jnp.float32),
            jax.ShapeDtypeStruct((width, length), jnp.float32),
            jax.ShapeDtypeStruct((1, length), jnp.float32),
        ),
        grid_spec=pltpu.PrefetchScalarGridSpec(
            num_scalar_prefetch=1,
            grid=(2, words // tile),
            in_specs=[
                whole((length, width)),
                pl.BlockSpec((tile, width), lambda phase, step, small: (step, 0)),
                whole((1, length)),
            ],
            out_specs=[
                pl.BlockSpec((tile, width), lambda phase, step, small: (phase * step, 0)),
                whole((width, length)),
                whole((1, length)),
            ],
            scratch_shapes=[pltpu.VMEM((8, length), jnp.float32)] * 2
            + [pltpu.VMEM((tile, length), jnp.bfloat16)],
        ),
        compiler_params=pltpu.CompilerParams(vmem_limit_bytes=60 << 20),
        name="head_pass",
    )(small, pred_low, word_table, token_weight)


def adam_rule(master, moment, second, grad, rate, decay):
    moment_new = BETA_ONE * moment + (1.0 - BETA_ONE) * grad
    second_new = BETA_TWO * second + (1.0 - BETA_TWO) * grad * grad
    moment_hat = moment_new / (1.0 - BETA_ONE**ADAM_STEP)
    second_hat = second_new / (1.0 - BETA_TWO**ADAM_STEP)
    master_new = master - rate * (moment_hat / (jnp.sqrt(second_hat) + ADAM_EPS) + decay * master)
    return [moment_new, second_new, master_new]


def adam_update(factor, masters, moments, seconds, grads):
    count = len(masters) - 1
    shapes = [member.shape for member in masters[:count]]

    def kernel(factor_ref, *refs):
        small, refs = refs[:4], refs[4:]
        sources, targets = refs[: 4 * count], refs[4 * count : 7 * count]
        small_out, refs = refs[7 * count : 7 * count + 3], refs[7 * count + 3 :]
        held, load_sems, store_sems = refs[:count], refs[count], refs[count + 1]
        loads = []
        for at in range(count):
            for kind in range(4):
                loads.append(
                    pltpu.make_async_copy(
                        sources[kind * count + at], held[at].at[kind], load_sems.at[at, kind]
                    )
                )
                loads[-1].start()
        scale = factor_ref[0]
        values = [ref[...] for ref in small]
        values[3] = scale * values[3]
        for kind, value in enumerate(adam_rule(*values, RATES[count], DECAYS[count])):
            small_out[kind][...] = value
        stores = []
        for at in range(count):
            for kind in range(4):
                loads[4 * at + kind].wait()
            values = [held[at][kind] for kind in range(4)]
            values[3] = scale * values[3]
            for kind, value in enumerate(adam_rule(*values, RATES[at], DECAYS[at])):
                held[at][4 + kind] = value
                stores.append(
                    pltpu.make_async_copy(
                        held[at].at[4 + kind], targets[3 * at + kind], store_sems.at[at, kind]
                    )
                )
                stores[-1].start()
        for store in stores:
            store.wait()

    kinds = (masters, moments, seconds, grads)
    return pl.pallas_call(
        kernel,
        out_shape=[
            jax.ShapeDtypeStruct(member.shape, jnp.float32) for member in masters for kind in range(3)
        ],
        in_specs=[pl.BlockSpec(memory_space=pltpu.SMEM)]
        + [pl.BlockSpec(memory_space=pltpu.VMEM)] * 4
        + [pl.BlockSpec(memory_space=pltpu.HBM)] * (4 * count),
        out_specs=[pl.BlockSpec(memory_space=pltpu.HBM)] * (3 * count)
        + [pl.BlockSpec(memory_space=pltpu.VMEM)] * 3,
        scratch_shapes=[pltpu.VMEM((7,) + shape, jnp.float32) for shape in shapes]
        + [pltpu.SemaphoreType.DMA((count, 4)), pltpu.SemaphoreType.DMA((count, 3))],
        compiler_params=pltpu.CompilerParams(vmem_limit_bytes=60 << 20),
        name="adam_update",
    )(
        factor.reshape(1),
        *[members[count] for members in kinds],
        *[member for members in kinds for member in members[:count]],
    )


AXES = ("bucket", "dp")


class Place:
    def __init__(self, buckets, columns):
        self.buckets, self.columns = buckets, columns
        self.count = buckets * columns
        self.line = columns // 2
        self.bits = [1 << place for place in range(1, columns.bit_length() - 1)]
        self.offsets = [0]
        for bit in reversed(self.bits):
            self.offsets += [offset ^ (bit >> 1) for offset in self.offsets]
        self.square = lax.axis_index("bucket")
        along = lax.axis_index("dp")
        self.core = along % 2
        self.along = along // 2
        self.flat = self.square * columns + along
        self.step_a = 1 + self.core
        self.step_b = 2 - self.core

    def swap(self, array, pick):
        pairs = [(member, member ^ pick(member)) for member in range(self.count)]
        return lax.ppermute(array, AXES, pairs)

    def swap_core(self, array):
        return self.swap(array, lambda member: 1)

    def swap_a(self, array):
        return self.swap(array, lambda member: self.columns * (1 + member % 2))

    def swap_b(self, array):
        return self.swap(array, lambda member: self.columns * (2 - member % 2))

    def swap_line(self, array, bit):
        return self.swap(array, lambda member: bit)

    def total(self, array, beside):
        array = array + self.swap_core(array)
        spans = [self.columns, 2 * self.columns] + self.bits
        for at in range(0, len(spans), 2):
            near, *more = spans[at : at + 2]
            parts = [self.swap_line(array, near)]
            for far in more:
                parts += [self.swap_line(array, far), self.swap_line(array, near ^ far)]
            array = array + sum(parts)
            if at == 0:
                array, *beside = tie(array, *beside)
        return array, beside


def assemble(place, pieces):
    twice, rows, cols = pieces[0].shape
    line = twice // 2
    flags = jnp.stack([place.square, place.along, place.core]).astype(jnp.int32)

    def kernel(flags_ref, *refs):
        piece_refs, out_ref, held, load_sems, store_sem = refs[:4], *refs[4:]
        square, along, core = flags_ref[0], flags_ref[1], flags_ref[2]
        step_a, step_b = 1 + core, 2 - core
        spots = [
            (0, (square, square ^ step_a), core),
            (2, (square, square ^ step_b), 1 - core),
            (1, (square ^ step_b, square ^ 3), core),
            (3, (square ^ step_a, square ^ 3), 1 - core),
        ]
        loads = [
            pltpu.make_async_copy(piece_ref, held.at[at], load_sems.at[at])
            for at, piece_ref in enumerate(piece_refs)
        ]
        for load in loads:
            load.start()
        for at, quarters, side in spots:
            loads[at].wait()
            for half, quarter in enumerate(quarters):
                for order, offset in enumerate(place.offsets):
                    pltpu.make_async_copy(
                        held.at[at, half * line + order],
                        out_ref.at[quarter, along ^ offset, side],
                        store_sem,
                    ).start()
        pltpu.make_async_copy(out_ref, out_ref, store_sem).wait()

    gathered = pl.pallas_call(
        kernel,
        out_shape=jax.ShapeDtypeStruct((4, line, 2, rows, cols), pieces[0].dtype),
        grid_spec=pltpu.PrefetchScalarGridSpec(
            num_scalar_prefetch=1,
            grid=(1,),
            in_specs=[pl.BlockSpec(memory_space=pltpu.HBM)] * 4,
            out_specs=pl.BlockSpec(memory_space=pltpu.HBM),
            scratch_shapes=[
                pltpu.VMEM((4, twice, rows, cols), pieces[0].dtype),
                pltpu.SemaphoreType.DMA((4,)),
                pltpu.SemaphoreType.DMA(()),
            ],
        ),
        compiler_params=pltpu.CompilerParams(vmem_limit_bytes=(2 << 20) + 8 * twice * cols * (-(-rows // 8) * 8)),
        name="assemble",
    )(flags, *pieces)
    return gathered.reshape(8 * line * rows, cols)


def product_half(left, right):
    half = right.shape[1] // 2

    def half_of(side):
        return matmul_tn(left, lax.dynamic_slice_in_dim(right, side * half, half, 1))

    return half_of


def column_half(array):
    half = array.shape[1] // 2
    return lambda side: lax.dynamic_slice_in_dim(array, side * half, half, 1)


def scatter_halves(place, table, spots, rows):
    words, width = table.shape
    half = words // 2
    each = half // place.count
    length = rows.shape[0]
    flag = place.core.astype(jnp.int32).reshape(1)

    def kernel(spots_ref, flag_ref, table_ref, rows_ref, send_ref, keep_ref, held, load_sem, sems):
        for owner in range(place.count):
            for side in range(2):
                pltpu.make_async_copy(
                    table_ref.at[pl.ds((2 * owner + side) * each, each)],
                    held.at[pl.ds(side * half + owner * each, each)],
                    load_sem,
                ).start()
        pltpu.make_async_copy(table_ref, held, load_sem).wait()

        def step(at, unused):
            for more in range(16):
                place_at = pl.ds(spots_ref[at * 16 + more], 1)
                held[place_at, :] += rows_ref[pl.ds(at * 16 + more, 1), :]
            return unused

        lax.fori_loop(0, length // 16, step, 0)
        core = flag_ref[0]
        first = pltpu.make_async_copy(held.at[pl.ds((1 - core) * half, half)], send_ref, sems.at[0])
        second = pltpu.make_async_copy(held.at[pl.ds(core * half, half)], keep_ref, sems.at[1])
        first.start()
        second.start()
        first.wait()
        second.wait()

    return pl.pallas_call(
        kernel,
        out_shape=[jax.ShapeDtypeStruct((half, width), jnp.float32)] * 2,
        grid_spec=pltpu.PrefetchScalarGridSpec(
            num_scalar_prefetch=2,
            grid=(1,),
            in_specs=[
                pl.BlockSpec(memory_space=pltpu.HBM),
                pl.BlockSpec((length, width), lambda step, spots, flag: (0, 0)),
            ],
            out_specs=[pl.BlockSpec(memory_space=pltpu.HBM)] * 2,
            scratch_shapes=[
                pltpu.VMEM((words, width), jnp.float32),
                pltpu.SemaphoreType.DMA(()),
                pltpu.SemaphoreType.DMA((2,)),
            ],
        ),
        compiler_params=pltpu.CompilerParams(vmem_limit_bytes=48 << 20),
        name="scatter_halves",
    )(spots, flag, table, rows)


def join(held, arrived):
    return jnp.concatenate([held, arrived], 0)


class Reduction:
    def __init__(self, place, kept, across, axis=1, exact=False, short=0):
        self.place, self.axis, self.exact, self.short = place, axis, exact, short
        self.rows = [piece.shape[0] // place.count for piece in kept]
        shapes = [
            (4, place.line // 2, 2, 2 * rows, piece.shape[1]) for rows, piece in zip(self.rows, kept)
        ]
        kept = [piece.reshape(shape) for piece, shape in zip(kept, shapes)]
        across = [piece.reshape(shape) for piece, shape in zip(across, shapes)]
        if axis == 1:
            self.parts = [(own, came, own.shape[4], 0) for own, came in zip(kept, across)]
        else:
            self.parts = [
                (own, came, TILE, block)
                for own, came in zip(kept, across)
                for block in range(own.shape[4] // TILE)
            ]
            self.rows = [own.shape[3] // 2 for own, unused, cols, block in self.parts]
        self.cols = [part[2] for part in self.parts]
        if axis == 1:
            self.span = (2 * self.rows[0], sum(self.cols))
        else:
            self.span = (2 * sum(self.rows), self.cols[0])
        self.level = 0

    def where(self, at):
        if self.axis == 1:
            start = sum(self.cols[:at])
            return slice(0, self.span[0]), slice(start, start + self.cols[at])
        start = 2 * sum(self.rows[:at])
        return slice(start, start + 2 * self.rows[at]), slice(0, self.span[1])

    def lower(self, at, value):
        if self.exact and at == len(self.cols) - 1:
            last = value[..., : TILE // 2]
            rounded = last.astype(jnp.bfloat16).astype(jnp.float32)
            value = jnp.concatenate([rounded, last - rounded], -1)
        return value.astype(jnp.bfloat16)

    def lift(self, at, value):
        value = value.astype(jnp.float32)
        if self.exact and at == len(self.cols) - 1:
            rounded, rest = value[..., : TILE // 2], value[..., TILE // 2 :]
            value = jnp.concatenate([rounded + rest, jnp.zeros_like(rest)], -1)
        return value

    def cast(self, at, value, ref):
        return self.lower(at, value) if ref.dtype == jnp.bfloat16 else value

    def took(self, at, value):
        return self.lift(at, value) if value.dtype == jnp.bfloat16 else value

    def call(self, name, kernel, steps, flags, inputs, outputs):
        return pl.pallas_call(
            kernel,
            out_shape=[entry for entry, unused, index in outputs],
            grid_spec=pltpu.PrefetchScalarGridSpec(
                num_scalar_prefetch=1,
                grid=(steps,),
                in_specs=[pl.BlockSpec(block, index) for unused, block, index in inputs],
                out_specs=[pl.BlockSpec(block, index) for unused, block, index in outputs],
            ),
            compiler_params=pltpu.CompilerParams(vmem_limit_bytes=40 << 20),
            name=name,
        )(jnp.stack(flags).astype(jnp.int32), *[array for array, unused, index in inputs])

    def pieces(self, block, index):
        entries = []
        for kept, across, cols, place in self.parts:

            def at_place(step, flags, place=place):
                return index(step, flags) + (place,)

            for array in (kept, across):
                entries.append((array, block + (array.shape[3], cols), at_place))
        return entries

    def to_a(self):
        square, line = self.place.square, self.place.line
        count = len(self.cols)

        def kernel(flags_ref, *refs):
            out_ref = refs[-1]
            for at in range(count):
                rows, cols = self.where(at)
                value = refs[2 * at][0] + refs[2 * at + 1][0]
                out_ref[0, :, :, rows, cols] = self.lower(at, value)

        shape = (2, line // 2, 2) + self.span
        (result,) = self.call(
            "reduce_first",
            kernel,
            2,
            [square ^ self.place.step_a, square ^ 3],
            self.pieces((1, line // 2, 2), lambda step, flags: (flags[step], 0, 0, 0)),
            [
                (
                    jax.ShapeDtypeStruct(shape, jnp.bfloat16),
                    (1,) + shape[1:],
                    lambda step, flags: (step, 0, 0, 0, 0),
                )
            ],
        )
        return result

    def came_a(self, refs, at, index):
        rows, cols = self.where(at)
        if len(self.from_a) > 1:
            return self.lift(at, refs[at][index + (slice(None), slice(None))])
        return self.lift(at, refs[0][index + (rows, cols)])

    def to_b(self, from_a):
        self.from_a = from_a
        line, count = self.place.line, len(self.cols)

        def kernel(flags_ref, *refs):
            out_ref, firsts = refs[-1], refs[2 * count : -1]
            for at in range(count):
                rows, cols = self.where(at)
                value = refs[2 * at][0] + refs[2 * at + 1][0]
                value = value + self.came_a(firsts, at, (0, slice(None), slice(None)))
                out_ref[:, :, rows, cols] = self.lower(at, value)

        shape = (line // 2, 2) + self.span
        (result,) = self.call(
            "reduce_second",
            kernel,
            1,
            [self.place.square ^ self.place.step_b],
            self.pieces((1, line // 2, 2), lambda step, flags: (flags[0], 0, 0, 0))
            + [
                (array, (1,) + array.shape[1:], lambda step, flags: (1, 0, 0, 0, 0))
                for array in from_a
            ],
            [(jax.ShapeDtypeStruct(shape, jnp.bfloat16), shape, lambda step, flags: (0, 0, 0, 0))],
        )
        return result

    def halves(self, lines):
        self.level += 1
        kinds = (jnp.bfloat16 if self.level <= self.short else jnp.float32, jnp.float32)
        shape = (lines,) + self.span
        return [
            (jax.ShapeDtypeStruct(shape, kind), shape, lambda step, flags: (0, 0, 0))
            for kind in kinds
        ]

    def to_line(self, from_b):
        line, count = self.place.line, len(self.cols)
        mine = self.place.along % 2
        self.along = self.place.along // 2

        def kernel(flags_ref, *refs):
            firsts, second_ref = refs[2 * count : -3], refs[-3]
            for step, out_ref in enumerate(refs[-2:]):

                @pl.when(pl.program_id(0) == step)
                def _():
                    for at in range(count):
                        rows, cols = self.where(at)
                        value = refs[2 * at][0, :, 0] + refs[2 * at + 1][0, :, 0]
                        value = value + self.came_a(firsts, at, (0, slice(None), 0))
                        value = value + self.lift(at, second_ref[:, 0, rows, cols])
                        out_ref[:, rows, cols] = self.cast(at, value, out_ref)

        send, self.own = self.call(
            "reduce_third",
            kernel,
            2,
            [self.place.square, 1 - mine, mine],
            self.pieces((1, line // 2, 1), lambda step, flags: (flags[0], 0, flags[1 + step], 0))
            + [
                (
                    array,
                    (1, line // 2, 1) + array.shape[3:],
                    lambda step, flags: (0, 0, flags[1 + step], 0, 0),
                )
                for array in self.from_a
            ]
            + [
                (
                    from_b,
                    (line // 2, 1) + self.span,
                    lambda step, flags: (0, flags[1 + step], 0, 0),
                )
            ],
            self.halves(line // 2),
        )
        return send

    def next_line(self, came):
        lines, count = self.own.shape[0] // 2, len(self.cols)
        mine = self.along % 2
        self.along = self.along // 2
        entries = [
            (
                array.reshape((lines, 2) + self.span),
                (lines, 1) + self.span,
                lambda step, flags: (0, flags[step], 0, 0),
            )
            for array in (self.own, came)
        ]

        def kernel(flags_ref, own_ref, came_ref, *out_refs):
            for step, out_ref in enumerate(out_refs):

                @pl.when(pl.program_id(0) == step)
                def _():
                    for at in range(count):
                        rows, cols = self.where(at)
                        value = own_ref[:, 0, rows, cols] + self.took(at, came_ref[:, 0, rows, cols])
                        out_ref[:, rows, cols] = self.cast(at, value, out_ref)

        send, self.own = self.call(
            "reduce_line", kernel, 2, [1 - mine, mine], entries, self.halves(lines)
        )
        return send

    def to_end(self, came):
        half, count = (self.span[0] // 2, self.span[1]), len(self.cols)

        def kernel(flags_ref, own_ref, came_ref, send_ref, keep_ref, squares_ref):
            first = flags_ref[0] == 0
            if came_ref.dtype == jnp.bfloat16 and self.exact:
                pieces = [self.took(at, came_ref[(0,) + self.where(at)]) for at in range(count)]
                came = jnp.concatenate(pieces, self.axis)
            else:
                came = came_ref[0].astype(jnp.float32)
            value = own_ref[0] + came
            squared = value * value
            if self.exact:
                spot_row = lax.broadcasted_iota(jnp.int32, squared.shape, 0)
                spot_lane = lax.broadcasted_iota(jnp.int32, squared.shape, 1)
                aside = (spot_lane == 3) & (spot_row >= self.span[0] - 2 * self.rows[-1])
                squared = jnp.where(aside & first, 0.0, squared)
            squares_ref[...] = jnp.full(squares_ref.shape, jnp.sum(squared), jnp.float32)
            groups = [self.rows[0]] if self.axis == 1 else self.rows
            start = 0
            for rows in groups:
                low, high = value[2 * start : 2 * start + rows], value[2 * start + rows : 2 * start + 2 * rows]
                send_ref[start : start + rows] = jnp.where(first, high, low)
                keep_ref[start : start + rows] = jnp.where(first, low, high)
                start += rows

        whole = (1,) + self.span
        send, self.last, self.squares = self.call(
            "reduce_last",
            kernel,
            1,
            [self.place.core],
            [(array, whole, lambda step, flags: (0, 0, 0)) for array in (self.own, came)],
            [
                (jax.ShapeDtypeStruct(shape, jnp.float32), shape, lambda step, flags: (0, 0))
                for shape in (half, half, (8, TILE))
            ],
        )
        return send

    def unpack(self, array):
        results, start = [], 0
        for size in self.cols if self.axis == 1 else self.rows:
            results.append(lax.slice_in_dim(array, start, start + size, axis=self.axis))
            start += size
        return results

    def finish(self, came):
        return self.unpack(self.last), self.unpack(came)


def in_order(place, kept, came, axis):
    return jnp.where(
        place.core == 0,
        jnp.concatenate([kept, came], axis),
        jnp.concatenate([came, kept], axis),
    )


def on_device(
    token_ids,
    segment_ids,
    live,
    timesteps,
    noise,
    embedding,
    embedding_moment,
    embedding_second,
    up_weight,
    up_moment,
    up_second,
    time_weight,
    time_moment,
    time_second,
    qkv_weight,
    qkv_moment,
    qkv_second,
    out_weight,
    out_moment,
    out_second,
    fc_weight,
    fc_moment,
    fc_second,
    proj_weight,
    proj_moment,
    proj_second,
    down_weight,
    down_moment,
    down_second,
    norm_gains,
    gains_moment,
    gains_second,
):
    masters = (
        embedding,
        up_weight,
        time_weight,
        qkv_weight,
        out_weight,
        fc_weight,
        proj_weight,
        down_weight,
        norm_gains,
    )
    moments = (
        embedding_moment,
        up_moment,
        time_moment,
        qkv_moment,
        out_moment,
        fc_moment,
        proj_moment,
        down_moment,
        gains_moment,
    )
    seconds = (
        embedding_second,
        up_second,
        time_second,
        qkv_second,
        out_second,
        fc_second,
        proj_second,
        down_second,
        gains_second,
    )
    place = Place(lax.axis_size("bucket"), lax.axis_size("dp"))
    buckets = place.buckets
    step_span = STEPS_T // buckets
    tokens = token_ids[0]
    step_row = timesteps[0]
    live_float = live[0].astype(jnp.float32)
    onehot = (
        (step_row // step_span)[:, None] == jnp.arange(buckets, dtype=jnp.int32)[None, :]
    ).astype(jnp.float32)
    count_own = jnp.sum(live_float[:, None] * onehot, 0)
    count_high = jnp.floor(count_own / 32.0)
    aside = jnp.concatenate([count_high, count_own - 32.0 * count_high]).astype(jnp.bfloat16)
    low = [member.astype(jnp.bfloat16) for member in masters]
    own_rows = low[3].shape[0]
    gains_pad = jnp.concatenate(
        [
            low[8].T,
            jnp.zeros((own_rows, EMB - 3), jnp.bfloat16),
        ],
        1,
    )
    model_width = low[3].shape[1] // 3
    ff_width = low[5].shape[1]

    table = low[0][None]
    entry = jnp.concatenate([low[1].T, low[2].T, gains_pad], 1)[None]
    qkv = low[3][None]
    aside_pad = jnp.pad(aside[None, :], ((0, own_rows - 1), (0, EMB - 2 * buckets)))
    leave = jnp.concatenate([low[4].T, low[5], low[6].T, low[7], aside_pad], 1)[None]
    fraction = step_row.astype(jnp.float32) / STEPS_T
    alpha_bar = 1.0 - jnp.sqrt(fraction + 0.0001)
    keep_root = jnp.sqrt(alpha_bar)[:, None]
    seg_col = jnp.broadcast_to(segment_ids.T, (segment_ids.shape[1], TILE))
    windows = key_windows(segment_ids[0])
    down_bits = place.bits[::-1]

    for bit in down_bits[:-1]:
        table = join(table, place.swap_line(table, bit))
        entry = join(entry, place.swap_line(entry, bit))
        table, entry, windows = tie(table, entry, windows)
    table = join(table, place.swap_line(table, down_bits[-1]))
    entry = join(entry, place.swap_line(entry, down_bits[-1]))
    for bit in down_bits[:-1]:
        entry, qkv = tie(entry, qkv)
        qkv = join(qkv, place.swap_line(qkv, bit))
    table, entry, qkv = tie(table, entry, qkv)
    table_came, entry_came = place.swap_a(table), place.swap_a(entry)
    table_came, entry_came, qkv, leave, step_row = tie(
        table_came, entry_came, qkv, leave, step_row
    )
    feature_low = sinusoid(step_row, D).astype(jnp.bfloat16)
    table, entry = join(table, table_came), join(entry, entry_came)
    table_pieces = [table, place.swap_b(table), place.swap_core(table)]
    entry_pieces = [entry, place.swap_b(entry), place.swap_core(entry)]
    qkv_came = place.swap_line(qkv, down_bits[-1])
    for bit in down_bits[:-2]:
        leave = join(leave, place.swap_line(leave, bit))
    leave_came = place.swap_line(leave, down_bits[-2])
    (qkv_came,) = tie(qkv_came)
    qkv = join(qkv, qkv_came)
    *both, qkv, feature_low = tie(*table_pieces, *entry_pieces, qkv, feature_low)
    table_pieces, entry_pieces = both[:3], both[3:]
    table_pieces.append(place.swap_core(table_pieces[1]))
    entry_pieces.append(place.swap_core(entry_pieces[1]))
    qkv_came = place.swap_a(qkv)
    entry_low = assemble(place, entry_pieces)
    entry_low, qkv_came = tie(entry_low, qkv_came)
    qkv = join(qkv, qkv_came)
    entry_low, leave_came, qkv = tie(entry_low, leave_came, qkv)
    leave = join(leave, leave_came)
    leave_came = place.swap_line(leave, down_bits[-1])
    qkv_pieces = [qkv, place.swap_b(qkv), place.swap_core(qkv)]
    qkv, table_pieces[0] = tie(qkv, table_pieces[0])
    word_table = assemble(place, table_pieces)
    word_table, leave_came = tie(word_table, leave_came)
    leave = join(leave, leave_came)
    leave_came = place.swap_a(leave)
    up_low = entry_low[:, :EMB]
    time_low = entry_low[:, EMB : EMB + model_width]
    gain_rows = entry_low[:, EMB + model_width :][:, :3].T.astype(jnp.float32)

    table_size = jnp.max(jnp.sum(jnp.square(word_table.astype(jnp.float32)), 1))

    start_emb = word_table[tokens].astype(jnp.float32)
    noisy_emb = keep_root * start_emb + jnp.sqrt(1.0 - alpha_bar)[:, None] * noise[0]
    noisy_low = noisy_emb.astype(jnp.bfloat16)
    hidden_zero = matrix_product_transposed(noisy_low, up_low) + matrix_product_transposed(
        feature_low, time_low
    )
    normed, scaled_one, inverse_one = layer_normalize(hidden_zero, gain_rows[0])
    normed_one_low = normed.astype(jnp.bfloat16)
    *qkv_pieces, normed_one_low = tie(*qkv_pieces, normed_one_low)
    qkv_pieces.append(place.swap_core(qkv_pieces[1]))
    qkv_low = assemble(place, qkv_pieces)
    leave_came, qkv_low = tie(leave_came, qkv_low)
    leave = join(leave, leave_came)
    leave_pieces = [leave, place.swap_b(leave), place.swap_core(leave)]
    mixed_low = matmul(normed_one_low, qkv_low).astype(jnp.bfloat16)
    segments = (segment_ids, seg_col, windows)
    attended_low, log_sums = attention_forward(mixed_low, *segments)
    *leave_pieces, attended_low = tie(*leave_pieces, attended_low)
    leave_pieces.append(place.swap_core(leave_pieces[1]))
    leave_low = assemble(place, leave_pieces)
    out_low = leave_low[:, :model_width]
    fc_low = leave_low[:, model_width : model_width + ff_width]
    proj_low = leave_low[:, model_width + ff_width : model_width + 2 * ff_width]
    down_low = leave_low[:, model_width + 2 * ff_width : model_width + 2 * ff_width + EMB]
    shares = leave_low[:, model_width + 2 * ff_width + EMB :]
    shares = shares.reshape(place.count, own_rows, EMB)[:, 0, : 2 * buckets]
    count_sums = jnp.sum(shares.astype(jnp.float32), 0)
    counts = 32.0 * count_sums[:buckets] + count_sums[buckets:]
    token_weight = live_float * jnp.sum(onehot / counts[None, :], -1) / buckets
    hidden_one = hidden_zero + matrix_product_transposed(attended_low, out_low)
    normed, scaled_two, inverse_two = layer_normalize(hidden_one, gain_rows[1])
    normed_two_low = normed.astype(jnp.bfloat16)
    active, slope = gelu_and_slope(matmul(normed_two_low, fc_low))
    active_low, slope = tie(active.astype(jnp.bfloat16), slope)
    hidden_two = hidden_one + matrix_product_transposed(active_low, proj_low)
    normed, scaled_top, inverse_top = layer_normalize(hidden_two, gain_rows[2])
    normed_top_low = normed.astype(jnp.bfloat16)
    prediction = matmul(normed_top_low, down_low)
    pred_low = prediction.astype(jnp.bfloat16)
    size = jnp.sqrt(jnp.max(jnp.sum(jnp.square(prediction), 1)) * table_size)
    small = (size < 40.0).astype(jnp.int32).reshape(1)
    grad_table_head, grad_pred_head, log_total = head_pass(
        pred_low, word_table, token_weight[None, :], small
    )

    pred_float = pred_low.astype(jnp.float32)
    target = jnp.sum(pred_float * start_emb, -1)
    cross_loss = log_total[0] - target
    target_prob = jnp.exp(target - log_total[0])
    target_shift = lax.reduce_precision(
        token_weight * (target_prob - 1.0), 8, 7
    ) - lax.reduce_precision(token_weight * target_prob, 8, 7)
    target_shift = target_shift[:, None]
    pred_gap = prediction - start_emb
    loss_local = jnp.sum(token_weight * (jnp.mean(pred_gap * pred_gap, -1) + cross_loss))
    grad_mse = token_weight[:, None] * 2.0 * pred_gap / EMB
    grad_pred_low = (grad_mse + grad_pred_head.T + target_shift * start_emb).astype(jnp.bfloat16)
    grad_down = matmul_tn(normed_top_low, grad_pred_low)
    grad_two, grad_gain_top = norm_back(
        matrix_product_transposed(grad_pred_low, down_low), scaled_top, inverse_top, gain_rows[2]
    )

    bits = list(place.bits)
    core = place.core
    grad_two_low = grad_two.astype(jnp.bfloat16)
    proj_half = product_half(grad_two_low, active_low)
    proj_send, grad_two_low = tie(proj_half(1 - core), grad_two_low)
    proj_came = place.swap_core(proj_send)
    proj_kept = proj_half(core)
    grad_upper_low = (slope * matmul(grad_two_low, proj_low)).astype(jnp.bfloat16)
    proj_came, grad_upper_low = tie(proj_came, grad_upper_low)
    proj = Reduction(place, [proj_kept], [proj_came])
    proj_send, grad_upper_low = tie(proj.to_a(), grad_upper_low)
    proj_a = place.swap_a(proj_send)
    fc_half = product_half(normed_two_low, grad_upper_low)
    fc_send, grad_upper_low = tie(fc_half(1 - core), grad_upper_low)
    fc_came = place.swap_core(fc_send)
    fc_kept = fc_half(core)
    grad_normed_two = matrix_product_transposed(grad_upper_low, fc_low)
    back_two, grad_gain_two = norm_back(grad_normed_two, scaled_two, inverse_two, gain_rows[1])
    grad_one = grad_two + back_two
    grad_one_low = grad_one.astype(jnp.bfloat16)
    proj_a, fc_came, grad_one_low = tie(proj_a, fc_came, grad_one_low)
    fc = Reduction(place, [fc_kept], [fc_came])
    fc_send, grad_one_low = tie(fc.to_a(), grad_one_low)
    fc_a = place.swap_a(fc_send)
    out_half = product_half(grad_one_low, attended_low)
    out_send, out_kept = out_half(1 - core), out_half(core)
    grad_attended = matmul(grad_one_low, out_low).astype(jnp.bfloat16)
    lanes = lax.broadcasted_iota(jnp.int32, (model_width, 2 * TILE), 1)
    exact = jnp.where(lanes == 1, grad_gain_two[:, None], 0.0)
    exact = jnp.where(lanes == 2, grad_gain_top[:, None], exact)
    exact = jnp.where(lanes == 3, loss_local, exact)
    out_send, out_kept, exact, grad_attended = tie(out_send, out_kept, exact, grad_attended)
    out_came = place.swap_core(out_send)
    grad_mixed = attention_backward(mixed_low, grad_attended, log_sums, *segments)

    fc_a, out_came, grad_mixed = tie(fc_a, out_came, grad_mixed)
    feed = Reduction(place, [proj_kept, fc_kept], [proj_came, fc_came], short=len(bits))
    feed_send, grad_mixed = tie(feed.to_b([proj_a, fc_a]), grad_mixed)
    feed_came = place.swap_b(feed_send)
    qkv_half = product_half(normed_one_low, grad_mixed)
    qkv_send, grad_mixed = tie(qkv_half(1 - core), grad_mixed)
    qkv_came = place.swap_core(qkv_send)
    grad_normed_one = matrix_product_transposed(grad_mixed, qkv_low)
    back_one, grad_gain_one = norm_back(grad_normed_one, scaled_one, inverse_one, gain_rows[0])
    grad_zero = grad_one + back_one
    feed_came, grad_zero = tie(feed_came, grad_zero)
    feed_send, grad_zero = tie(feed.to_line(feed_came), grad_zero)
    feed_came = place.swap_line(feed_send, bits[0])
    grad_zero_low = grad_zero.astype(jnp.bfloat16)
    grad_start = matmul(grad_zero_low, up_low)
    grad_start = keep_root * grad_start - grad_mse + target_shift * pred_float
    qkv_kept, qkv_came, grad_start = tie(qkv_half(core), qkv_came, grad_start)
    mix = Reduction(place, [out_kept, qkv_kept], [out_came, qkv_came], short=1)
    mix_send, grad_start = tie(mix.to_a(), grad_start)
    mix_came = place.swap_a(mix_send)

    own_words = word_table.shape[0] // place.count // 2
    if own_words % 8 == 0:
        owner, spot = tokens // (2 * own_words), tokens % (2 * own_words)
        spot = (spot // own_words * place.count + owner) * own_words + spot % own_words
        words_send, words_kept = scatter_halves(place, grad_table_head, spot, grad_start)
    else:
        grad_table = grad_table_head.at[tokens].add(grad_start)
        split = grad_table.reshape(place.count, 2, own_words, EMB)
        words_send, words_kept = [
            lax.dynamic_index_in_dim(split, side, 1, False).reshape(-1, EMB)
            for side in (1 - core, core)
        ]
    words_send, mix_came, feed_came, grad_zero_low = tie(
        words_send, mix_came, feed_came, grad_zero_low
    )
    words_came = place.swap_core(words_send)
    feed_send, mix_send, grad_zero_low = tie(
        feed.next_line(feed_came), mix.to_b([mix_came]), grad_zero_low
    )
    feed_came, mix_came = place.swap_line(feed_send, bits[1]), place.swap_b(mix_send)
    time_half = product_half(grad_zero_low, feature_low)
    pair_half = column_half(jnp.concatenate([matmul_tn(grad_zero_low, noisy_low), grad_down], 1))
    exact_half = column_half(jnp.where(lanes == 0, grad_gain_one[:, None], exact))

    def rest_half(side):
        return time_half(side), jnp.concatenate([pair_half(side), exact_half(side)], 1)

    rest_send = tie(*rest_half(1 - core))
    rest_came = [place.swap_core(piece) for piece in rest_send]
    rest_kept = rest_half(core)
    words_came, *rest_came = tie(words_came, *rest_came)
    late = Reduction(
        place, [words_kept, *rest_kept], [words_came, *rest_came], axis=0, exact=True
    )
    late_send, mix_came = tie(late.to_a(), mix_came)
    late_came = place.swap_a(late_send)
    mix_came = place.swap_line(mix.to_line(mix_came), bits[0])
    late_came, mix_came, feed_came = tie(late_came, mix_came, feed_came)
    late_send, mix_send = tie(late.to_b([late_came]), mix.next_line(mix_came))
    late_came, mix_came = place.swap_b(late_send), place.swap_line(mix_send, bits[1])
    (late_came,) = tie(late_came)
    late_came = place.swap_line(late.to_line(late_came), bits[0])
    late_came, mix_came = tie(late_came, mix_came)
    late_came = place.swap_line(late.next_line(late_came), bits[1])
    members, arrived = (feed, mix, late), [feed_came, mix_came, late_came]
    for bit in bits[2:]:
        arrived = [
            place.swap_line(member.next_line(came), bit) for member, came in zip(members, arrived)
        ]
    ends = [
        member.finish(place.swap_core(member.to_end(came))) for member, came in zip(members, arrived)
    ]
    squares_local = feed.squares + mix.squares + late.squares
    (proj_end, fc_end), (out_end, qkv_end), (words_end, *rest_ends) = [
        list(zip(*end)) for end in ends
    ]
    time_end = [jnp.concatenate(sides[:-2], 1) for sides in zip(*rest_ends)]
    pair_end, exact_end = rest_ends[-2:]
    shard_pair = in_order(place, *pair_end, 1)
    shard_exact = jnp.where(core == 0, *exact_end)
    loss_sum = shard_exact[0, 3]
    shards = (
        in_order(place, *words_end, 0),
        shard_pair[:, :EMB],
        in_order(place, *time_end, 1),
        in_order(place, *qkv_end, 1),
        in_order(place, *out_end, 1),
        in_order(place, *fc_end, 1),
        in_order(place, *proj_end, 1),
        shard_pair[:, EMB:],
        shard_exact[:, :3].T,
    )
    squares, shards = place.total(squares_local, shards)
    squares = squares[0, 0]
    grad_norm = jnp.sqrt(squares)
    factor = CLIP_NORM / jnp.maximum(grad_norm, CLIP_NORM)
    flips = (False, True, True, False, True, False, True, False, False)

    def lay(members):
        return [member.T if flip else member for member, flip in zip(members, flips)]

    results = adam_update(factor, lay(masters), lay(moments), lay(seconds), shards)
    results = [result.T if flips[at // 3] else result for at, result in enumerate(results)]
    return (
        loss_sum,
        grad_norm,
        results[0],
        results[1],
        results[2],
        results[3],
        results[4],
        results[5],
        results[6],
        results[7],
        results[8],
        results[9],
        results[10],
        results[11],
        results[12],
        results[13],
        results[14],
        results[15],
        results[16],
        results[17],
        results[18],
        results[19],
        results[20],
        results[21],
        results[22],
        results[23],
        results[24],
        results[25],
        results[26],
    )


def solution(mesh):
    return jax.shard_map(
        on_device,
        mesh=mesh,
        in_specs=(
            P(("bucket", "dp"), None),
            P(("bucket", "dp"), None),
            P(("bucket", "dp"), None),
            P(("bucket", "dp"), None),
            P(("bucket", "dp"), None, None),
            P(("bucket", "dp"), None),
            P(("bucket", "dp"), None),
            P(("bucket", "dp"), None),
            P(None, ("bucket", "dp")),
            P(None, ("bucket", "dp")),
            P(None, ("bucket", "dp")),
            P(None, ("bucket", "dp")),
            P(None, ("bucket", "dp")),
            P(None, ("bucket", "dp")),
            P(("bucket", "dp"), None),
            P(("bucket", "dp"), None),
            P(("bucket", "dp"), None),
            P(None, ("bucket", "dp")),
            P(None, ("bucket", "dp")),
            P(None, ("bucket", "dp")),
            P(("bucket", "dp"), None),
            P(("bucket", "dp"), None),
            P(("bucket", "dp"), None),
            P(None, ("bucket", "dp")),
            P(None, ("bucket", "dp")),
            P(None, ("bucket", "dp")),
            P(("bucket", "dp"), None),
            P(("bucket", "dp"), None),
            P(("bucket", "dp"), None),
            P(None, ("bucket", "dp")),
            P(None, ("bucket", "dp")),
            P(None, ("bucket", "dp")),
        ),
        out_specs=(
            P(),
            P(),
            P(("bucket", "dp"), None),
            P(("bucket", "dp"), None),
            P(("bucket", "dp"), None),
            P(None, ("bucket", "dp")),
            P(None, ("bucket", "dp")),
            P(None, ("bucket", "dp")),
            P(None, ("bucket", "dp")),
            P(None, ("bucket", "dp")),
            P(None, ("bucket", "dp")),
            P(("bucket", "dp"), None),
            P(("bucket", "dp"), None),
            P(("bucket", "dp"), None),
            P(None, ("bucket", "dp")),
            P(None, ("bucket", "dp")),
            P(None, ("bucket", "dp")),
            P(("bucket", "dp"), None),
            P(("bucket", "dp"), None),
            P(("bucket", "dp"), None),
            P(None, ("bucket", "dp")),
            P(None, ("bucket", "dp")),
            P(None, ("bucket", "dp")),
            P(("bucket", "dp"), None),
            P(("bucket", "dp"), None),
            P(("bucket", "dp"), None),
            P(None, ("bucket", "dp")),
            P(None, ("bucket", "dp")),
            P(None, ("bucket", "dp")),
        ),
        check_vma=False,
    )
```

```python
import math

import jax
import jax.numpy as jnp
from jax import lax
from jax.experimental import pallas as pl
from jax.experimental.pallas import tpu as pltpu
from jax.sharding import PartitionSpec as P

D = 768
HEAD = 64
EMB = 128
STEPS_T = 2000
ADAM_STEP = 10


NEG_BIG = -1e30
EPS_NORM = 1e-05
BETA_ONE = 0.9
BETA_TWO = 0.95
ADAM_EPS = 1e-08
DECAY_RATE = 0.01
CLIP_NORM = 0.02
RATES = (0.05, 0.05, 0.02, 0.02, 0.02, 0.02, 0.01, 0.02, 0.3)
DECAYS = (DECAY_RATE,) * 8 + (0.0,)


def matmul(left_op, right_op):
    return jnp.dot(left_op, right_op, preferred_element_type=jnp.float32)


def matmul_tn(left_op, right_op):
    return lax.dot_general(
        left_op, right_op, (((0,), (0,)), ((), ())), preferred_element_type=jnp.float32
    )


def matrix_product_transposed(left_op, right_op):
    return lax.dot_general(
        left_op, right_op, (((1,), (1,)), ((), ())), preferred_element_type=jnp.float32
    )


def layer_normalize(hidden, gain_row):
    centre = jnp.mean(hidden, -1, keepdims=True)
    centred = hidden - centre
    spread = jnp.mean(centred * centred, -1, keepdims=True)
    scale_inv = lax.rsqrt(spread + EPS_NORM)
    normed = centred * scale_inv
    return (normed * gain_row, normed, scale_inv)


def gelu_and_slope(upper):
    root, cube = math.sqrt(2.0 / math.pi), 0.044715
    square = upper * upper
    bend = jnp.tanh(upper * (root + root * cube * square))
    half = 0.5 + 0.5 * bend
    steep = root + 3.0 * root * cube * square
    return upper * half, half + 0.5 * upper * (1.0 - bend * bend) * steep


def norm_back(grad_normed_out, normed, scale_inv, gain_row):
    grad_gain = jnp.sum(grad_normed_out * normed, 0)
    grad_scaled = grad_normed_out * gain_row
    grad_input = scale_inv * (
        grad_scaled
        - jnp.mean(grad_scaled, -1, keepdims=True)
        - normed * jnp.mean(grad_scaled * normed, -1, keepdims=True)
    )
    return (grad_input, grad_gain)


def sinusoid(step_row, model_width):
    half_width = model_width // 2
    freqs = jnp.exp(-math.log(10000.0) * jnp.arange(half_width, dtype=jnp.float32) / half_width)
    angles = step_row.astype(jnp.float32)[:, None] * freqs[None, :]
    return jnp.concatenate([jnp.sin(angles), jnp.cos(angles)], -1)


TILE = 128
LOG2E = math.log2(math.e)


def tie(*arrays):
    return lax.optimization_barrier(arrays)


def key_windows(segments):
    length = segments.shape[0]
    blocks = segments.reshape(-1, TILE)
    shared = jnp.any(blocks[:, :, None] == segments[None, None, :], 1)
    places = jnp.arange(length, dtype=jnp.int32)[None, :]
    first = jnp.min(jnp.where(shared, places, length), 1) // TILE * TILE
    last = jnp.max(jnp.where(shared, places, -1), 1) + 1
    spans = (last - first + KEYS - 1) // KEYS
    first = jnp.minimum(first, length - spans * KEYS)
    return jnp.stack([first, spans]).astype(jnp.int32)


def nt_dot(left, right):
    return lax.dot_general(
        left, right, (((1,), (1,)), ((), ())), preferred_element_type=jnp.float32
    )


def tn_dot(left, right):
    return lax.dot_general(
        left, right, (((0,), (0,)), ((), ())), preferred_element_type=jnp.float32
    )


def head_stack(pair):
    lanes = lax.broadcasted_iota(jnp.int32, pair.shape, 1)
    zero = jnp.zeros_like(pair)
    return jnp.concatenate(
        [jnp.where(lanes < HEAD, pair, zero), jnp.where(lanes >= HEAD, pair, zero)], 0
    )


def fold(array):
    return array.reshape(-1, 8, array.shape[-1])


PAIRS = D // TILE
WIDE = PAIRS * TILE
KEYS = 256
LOG_ROWS = -(-2 * PAIRS // 8) * 8


def attention_forward(mixed, seg_row, seg_col, windows):
    length, width = mixed.shape[0], mixed.shape[1] // 3
    groups = width // WIDE
    factor = HEAD ** (-0.5) * LOG2E

    def kernel(windows_ref, q_ref, k_ref, v_ref, row_ref, col_ref, o_ref, log_ref, held, out, flip):
        flip[...] = v_ref[...].T

        def step(block, unused):
            rows = pl.ds(pl.multiple_of(block * TILE, TILE), TILE)
            start, count = windows_ref[0, block], windows_ref[1, block]
            row = row_ref[:, rows]
            queries = [head_stack(q_ref[rows, pl.ds(pair * TILE, TILE)]) for pair in range(PAIRS)]

            def keys_at(at):
                return pl.ds(pl.multiple_of(start + at * KEYS, TILE), KEYS)

            def held_at(at):
                return pl.ds(pl.multiple_of(at * KEYS, KEYS), KEYS)

            def score(at, state):
                keys = keys_at(at)
                same = col_ref[keys, :] == row
                same = jnp.concatenate([same, same], 1)
                found = []
                for pair in range(PAIRS):
                    old, total = state[pair]
                    scores = nt_dot(k_ref[keys, pl.ds(pair * TILE, TILE)], queries[pair])
                    scores = jnp.where(same, scores * factor, NEG_BIG)
                    held[pair, held_at(at), :] = scores
                    scores = fold(scores)
                    new = jnp.maximum(old, jnp.max(scores, 0))
                    raised = jnp.sum(jnp.exp2(scores - new[None]), 0)
                    found.append((new, total * jnp.exp2(old - new) + raised))
                return tuple(found)

            low = jnp.full((8, 2 * TILE), NEG_BIG, jnp.float32)
            state = lax.fori_loop(0, count, score, ((low, jnp.zeros_like(low)),) * PAIRS)
            logs = []
            for peak, total in state:
                top = jnp.max(peak, 0, keepdims=True)
                total = jnp.sum(total * jnp.exp2(peak - top), 0, keepdims=True)
                logs.append(top + jnp.log2(total))
            out[...] = jnp.zeros_like(out)

            def spread(at, unused):
                for pair in range(PAIRS):
                    probs = jnp.exp2(held[pair, held_at(at), :] - logs[pair]).astype(jnp.bfloat16)
                    out[pair] += jnp.dot(
                        flip[pl.ds(pair * TILE, TILE), keys_at(at)],
                        probs,
                        preferred_element_type=jnp.float32,
                    )
                return unused

            lax.fori_loop(0, count, spread, 0)
            dims = lax.broadcasted_iota(jnp.int32, (TILE, TILE), 0)
            for pair in range(PAIRS):
                both = out[pair]
                chosen = jnp.where(dims < HEAD, both[:, :TILE], both[:, TILE:])
                o_ref[rows, pl.ds(pair * TILE, TILE)] = chosen.T.astype(jnp.bfloat16)
                log_ref[2 * pair : 2 * pair + 1, rows] = logs[pair][:, :TILE]
                log_ref[2 * pair + 1 : 2 * pair + 2, rows] = logs[pair][:, TILE:]
            return unused

        lax.fori_loop(0, length // TILE, step, 0)

    def column(place):
        return pl.BlockSpec((length, WIDE), lambda group, windows: (0, 3 * group + place))

    return pl.pallas_call(
        kernel,
        out_shape=(
            jax.ShapeDtypeStruct((length, width), jnp.bfloat16),
            jax.ShapeDtypeStruct((LOG_ROWS * groups, length), jnp.float32),
        ),
        grid_spec=pltpu.PrefetchScalarGridSpec(
            num_scalar_prefetch=1,
            grid=(groups,),
            in_specs=[
                column(0),
                column(1),
                column(2),
                pl.BlockSpec((1, length), lambda group, windows: (0, 0)),
                pl.BlockSpec((length, TILE), lambda group, windows: (0, 0)),
            ],
            out_specs=[
                pl.BlockSpec((length, WIDE), lambda group, windows: (0, group)),
                pl.BlockSpec((LOG_ROWS, length), lambda group, windows: (group, 0)),
            ],
            scratch_shapes=[
                pltpu.VMEM((PAIRS, length, 2 * TILE), jnp.float32),
                pltpu.VMEM((PAIRS, TILE, 2 * TILE), jnp.float32),
                pltpu.VMEM((WIDE, length), jnp.bfloat16),
            ],
        ),
        compiler_params=pltpu.CompilerParams(vmem_limit_bytes=28 << 20),
        name="attention_forward",
    )(windows, mixed, mixed, mixed, seg_row, seg_col)


def attention_backward(mixed, grad_attended, log_sums, seg_row, seg_col, windows):
    length = mixed.shape[0]
    score_scale = HEAD ** (-0.5)
    factor = score_scale * LOG2E

    def kernel(windows_ref, q_ref, k_ref, v_ref, do_ref, log_ref, row_ref, col_ref, *refs):
        out_ref, held, pulled, dq_flip, dq_acc, dk_acc, dv_acc, key_flip = refs
        third = pl.program_id(0)

        def step(block, unused):
            rows = pl.ds(pl.multiple_of(block * TILE, TILE), TILE)
            start, count = windows_ref[0, block], windows_ref[1, block]
            row = row_ref[:, rows]
            pairs = [pl.ds(pair * TILE, TILE) for pair in range(PAIRS)]
            queries = [head_stack(q_ref[rows, cols]) for cols in pairs]
            grads = [head_stack(do_ref[rows, cols]) for cols in pairs]
            logs = [
                jnp.concatenate(
                    [
                        log_ref[2 * pair : 2 * pair + 1, rows],
                        log_ref[2 * pair + 1 : 2 * pair + 2, rows],
                    ],
                    1,
                )
                for pair in range(PAIRS)
            ]

            def keys_at(at):
                return pl.ds(pl.multiple_of(start + at * KEYS, TILE), KEYS)

            def held_at(at):
                return pl.ds(pl.multiple_of(at * KEYS, KEYS), KEYS)

            def weigh(at, inners):
                keys = keys_at(at)
                same = col_ref[keys, :] == row
                same = jnp.concatenate([same, same], 1)
                found = []
                for pair, cols in enumerate(pairs):
                    scores = nt_dot(k_ref[keys, cols], queries[pair])
                    probs = jnp.where(same, jnp.exp2(scores * factor - logs[pair]), 0.0)
                    grad_probs = nt_dot(v_ref[keys, cols], grads[pair])
                    held[pair, held_at(at), :] = probs
                    pulled[pair, held_at(at), :] = grad_probs
                    found.append(inners[pair] + jnp.sum(fold(probs * grad_probs), 0))
                return tuple(found)

            zero = jnp.zeros((8, 2 * TILE), jnp.float32)
            inners = lax.fori_loop(0, count, weigh, (zero,) * PAIRS)
            inners = [jnp.sum(inner, 0, keepdims=True) for inner in inners]
            dq_flip[...] = jnp.zeros_like(dq_flip)

            def spread(at, unused):
                keys = keys_at(at)
                for pair, cols in enumerate(pairs):
                    probs = held[pair, held_at(at), :]
                    scores = probs * (pulled[pair, held_at(at), :] - inners[pair])
                    scores_low = scores.astype(jnp.bfloat16)
                    dv_acc[keys, cols] += jnp.dot(
                        probs.astype(jnp.bfloat16), grads[pair], preferred_element_type=jnp.float32
                    )
                    dk_acc[keys, cols] += jnp.dot(
                        scores_low, queries[pair], preferred_element_type=jnp.float32
                    )
                    dq_flip[pair] += jnp.dot(
                        key_flip[cols, keys], scores_low, preferred_element_type=jnp.float32
                    )
                return unused

            lax.fori_loop(0, count, spread, 0)
            dims = lax.broadcasted_iota(jnp.int32, (TILE, TILE), 0)
            for pair, cols in enumerate(pairs):
                both = dq_flip[pair]
                dq_acc[rows, cols] = jnp.where(dims < HEAD, both[:, :TILE], both[:, TILE:]).T
            return unused

        @pl.when(third == 0)
        def _():
            dk_acc[...] = jnp.zeros_like(dk_acc)
            dv_acc[...] = jnp.zeros_like(dv_acc)
            key_flip[...] = k_ref[...].T
            lax.fori_loop(0, length // TILE, step, 0)
            out_ref[...] = (dq_acc[...] * score_scale).astype(jnp.bfloat16)

        @pl.when(third == 1)
        def _():
            out_ref[...] = (dk_acc[...] * score_scale).astype(jnp.bfloat16)

        @pl.when(third == 2)
        def _():
            out_ref[...] = dv_acc[...].astype(jnp.bfloat16)

    def column(place):
        return pl.BlockSpec(
            (length, WIDE), lambda third, windows: (0, place), pipeline_mode=pl.Buffered(1)
        )

    return pl.pallas_call(
        kernel,
        out_shape=jax.ShapeDtypeStruct(mixed.shape, jnp.bfloat16),
        grid_spec=pltpu.PrefetchScalarGridSpec(
            num_scalar_prefetch=1,
            grid=(3,),
            in_specs=[
                column(0),
                column(1),
                column(2),
                column(0),
                pl.BlockSpec((LOG_ROWS, length), lambda third, windows: (0, 0)),
                pl.BlockSpec((1, length), lambda third, windows: (0, 0)),
                pl.BlockSpec((length, TILE), lambda third, windows: (0, 0)),
            ],
            out_specs=pl.BlockSpec((length, WIDE), lambda third, windows: (0, third)),
            scratch_shapes=[pltpu.VMEM((PAIRS, length, 2 * TILE), jnp.float32)] * 2
            + [pltpu.VMEM((PAIRS, TILE, 2 * TILE), jnp.float32)]
            + [pltpu.VMEM((length, WIDE), jnp.float32)] * 3
            + [pltpu.VMEM((WIDE, length), jnp.bfloat16)],
        ),
        compiler_params=pltpu.CompilerParams(vmem_limit_bytes=38 << 20),
        name="attention_backward",
    )(windows, mixed, mixed, mixed, grad_attended, log_sums, seg_row, seg_col)


def head_pass(pred_low, word_table, token_weight, small):
    length, width = pred_low.shape
    words = word_table.shape[0]
    tile, across = 1024, 256

    def kernel(
        small_ref, pred_ref, table_ref, weight_ref, grad_table_ref, grad_pred_ref, log_ref, peak, total, grads
    ):
        phase, step = pl.program_id(0), pl.program_id(1)
        blocks = [
            (pl.ds(row, TILE), pl.ds(col, across))
            for col in range(0, length, across)
            for row in range(0, tile, TILE)
        ]

        @pl.when((phase == 0) & (step == 0))
        def _():
            peak[...] = jnp.full_like(peak, jnp.where(small_ref[0] == 1, 0.0, -1e30))
            total[...] = jnp.zeros_like(total)
            grad_pred_ref[...] = jnp.zeros_like(grad_pred_ref)

        @pl.when((phase == 0) & (small_ref[0] == 1))
        def _():
            for rows, cols in blocks:
                logits = fold(nt_dot(table_ref[rows, :], pred_ref[cols, :]) * LOG2E)
                total[:, cols] += jnp.sum(jnp.exp2(logits), 0)

        @pl.when((phase == 0) & (small_ref[0] == 0))
        def _():
            for rows, cols in blocks:
                logits = fold(nt_dot(table_ref[rows, :], pred_ref[cols, :]) * LOG2E)
                old = peak[:, cols]
                new = jnp.maximum(old, jnp.max(logits, 0))
                raised = jnp.sum(jnp.exp2(logits - new[None]), 0)
                total[:, cols] = total[:, cols] * jnp.exp2(old - new) + raised
                peak[:, cols] = new

        @pl.when((phase == 1) & (step == 0))
        def _():
            top = jnp.max(peak[...], 0, keepdims=True)
            sums = jnp.sum(total[...] * jnp.exp2(peak[...] - top), 0, keepdims=True)
            logs = top + jnp.log2(sums)
            log_ref[...] = logs / LOG2E
            weight = weight_ref[...]
            down = jnp.where(weight > 0.0, jnp.log2(weight), -1e30)
            peak[...] = jnp.broadcast_to(logs - down, peak.shape)

        @pl.when(phase == 1)
        def _():
            for rows, cols in blocks:
                logits = nt_dot(table_ref[rows, :], pred_ref[cols, :])
                lowered = fold(logits * LOG2E) - peak[:, cols][None]
                grads[rows, cols] = (
                    jnp.exp2(lowered).reshape(TILE, across).astype(jnp.bfloat16)
                )
            grad_table_ref[...] = jnp.dot(
                grads[...], pred_ref[...], preferred_element_type=jnp.float32
            )
            grad_pred_ref[...] += tn_dot(table_ref[...], grads[...])

    def whole(shape):
        return pl.BlockSpec(shape, lambda phase, step, small: (0, 0))

    return pl.pallas_call(
        kernel,
        out_shape=(
            jax.ShapeDtypeStruct((words, width), jnp.float32),
            jax.ShapeDtypeStruct((width, length), jnp.float32),
            jax.ShapeDtypeStruct((1, length), jnp.float32),
        ),
        grid_spec=pltpu.PrefetchScalarGridSpec(
            num_scalar_prefetch=1,
            grid=(2, words // tile),
            in_specs=[
                whole((length, width)),
                pl.BlockSpec((tile, width), lambda phase, step, small: (step, 0)),
                whole((1, length)),
            ],
            out_specs=[
                pl.BlockSpec((tile, width), lambda phase, step, small: (phase * step, 0)),
                whole((width, length)),
                whole((1, length)),
            ],
            scratch_shapes=[pltpu.VMEM((8, length), jnp.float32)] * 2
            + [pltpu.VMEM((tile, length), jnp.bfloat16)],
        ),
        compiler_params=pltpu.CompilerParams(vmem_limit_bytes=60 << 20),
        name="head_pass",
    )(small, pred_low, word_table, token_weight)


def adam_rule(master, moment, second, grad, rate, decay):
    moment_new = BETA_ONE * moment + (1.0 - BETA_ONE) * grad
    second_new = BETA_TWO * second + (1.0 - BETA_TWO) * grad * grad
    moment_hat = moment_new / (1.0 - BETA_ONE**ADAM_STEP)
    second_hat = second_new / (1.0 - BETA_TWO**ADAM_STEP)
    master_new = master - rate * (moment_hat / (jnp.sqrt(second_hat) + ADAM_EPS) + decay * master)
    return [moment_new, second_new, master_new]


def adam_update(factor, masters, moments, seconds, grads):
    count = len(masters) - 1
    shapes = [member.shape for member in masters[:count]]

    def kernel(factor_ref, *refs):
        small, refs = refs[:4], refs[4:]
        sources, targets = refs[: 4 * count], refs[4 * count : 7 * count]
        small_out, refs = refs[7 * count : 7 * count + 3], refs[7 * count + 3 :]
        held, load_sems, store_sems = refs[:count], refs[count], refs[count + 1]
        loads = []
        for at in range(count):
            for kind in range(4):
                loads.append(
                    pltpu.make_async_copy(
                        sources[kind * count + at], held[at].at[kind], load_sems.at[at, kind]
                    )
                )
                loads[-1].start()
        scale = factor_ref[0]
        values = [ref[...] for ref in small]
        values[3] = scale * values[3]
        for kind, value in enumerate(adam_rule(*values, RATES[count], DECAYS[count])):
            small_out[kind][...] = value
        stores = []
        for at in range(count):
            for kind in range(4):
                loads[4 * at + kind].wait()
            values = [held[at][kind] for kind in range(4)]
            values[3] = scale * values[3]
            for kind, value in enumerate(adam_rule(*values, RATES[at], DECAYS[at])):
                held[at][4 + kind] = value
                stores.append(
                    pltpu.make_async_copy(
                        held[at].at[4 + kind], targets[3 * at + kind], store_sems.at[at, kind]
                    )
                )
                stores[-1].start()
        for store in stores:
            store.wait()

    kinds = (masters, moments, seconds, grads)
    return pl.pallas_call(
        kernel,
        out_shape=[
            jax.ShapeDtypeStruct(member.shape, jnp.float32) for member in masters for kind in range(3)
        ],
        in_specs=[pl.BlockSpec(memory_space=pltpu.SMEM)]
        + [pl.BlockSpec(memory_space=pltpu.VMEM)] * 4
        + [pl.BlockSpec(memory_space=pltpu.HBM)] * (4 * count),
        out_specs=[pl.BlockSpec(memory_space=pltpu.HBM)] * (3 * count)
        + [pl.BlockSpec(memory_space=pltpu.VMEM)] * 3,
        scratch_shapes=[pltpu.VMEM((7,) + shape, jnp.float32) for shape in shapes]
        + [pltpu.SemaphoreType.DMA((count, 4)), pltpu.SemaphoreType.DMA((count, 3))],
        compiler_params=pltpu.CompilerParams(vmem_limit_bytes=60 << 20),
        name="adam_update",
    )(
        factor.reshape(1),
        *[members[count] for members in kinds],
        *[member for members in kinds for member in members[:count]],
    )


AXES = ("bucket", "dp")


class Place:
    def __init__(self, buckets, columns):
        self.buckets, self.columns = buckets, columns
        self.count = buckets * columns
        self.line = columns // 2
        self.bits = [1 << place for place in range(1, columns.bit_length() - 1)]
        self.offsets = [0]
        for bit in reversed(self.bits):
            self.offsets += [offset ^ (bit >> 1) for offset in self.offsets]
        self.square = lax.axis_index("bucket")
        along = lax.axis_index("dp")
        self.core = along % 2
        self.along = along // 2
        self.flat = self.square * columns + along
        self.step_a = 1 + self.core
        self.step_b = 2 - self.core

    def swap(self, array, pick):
        pairs = [(member, member ^ pick(member)) for member in range(self.count)]
        return lax.ppermute(array, AXES, pairs)

    def swap_core(self, array):
        return self.swap(array, lambda member: 1)

    def swap_a(self, array):
        return self.swap(array, lambda member: self.columns * (1 + member % 2))

    def swap_b(self, array):
        return self.swap(array, lambda member: self.columns * (2 - member % 2))

    def swap_line(self, array, bit):
        return self.swap(array, lambda member: bit)

    def total(self, array, beside):
        array = array + self.swap_core(array)
        spans = [self.columns, 2 * self.columns] + self.bits
        for at in range(0, len(spans), 2):
            near, *more = spans[at : at + 2]
            parts = [self.swap_line(array, near)]
            for far in more:
                parts += [self.swap_line(array, far), self.swap_line(array, near ^ far)]
            array = array + sum(parts)
            if at == 0:
                array, *beside = tie(array, *beside)
        return array, beside


def assemble(place, pieces):
    twice, rows, cols = pieces[0].shape
    line = twice // 2
    flags = jnp.stack([place.square, place.along, place.core]).astype(jnp.int32)

    def kernel(flags_ref, *refs):
        piece_refs, out_ref, held, load_sems, store_sem = refs[:4], *refs[4:]
        square, along, core = flags_ref[0], flags_ref[1], flags_ref[2]
        step_a, step_b = 1 + core, 2 - core
        spots = [
            (0, (square, square ^ step_a), core),
            (2, (square, square ^ step_b), 1 - core),
            (1, (square ^ step_b, square ^ 3), core),
            (3, (square ^ step_a, square ^ 3), 1 - core),
        ]
        loads = [
            pltpu.make_async_copy(piece_ref, held.at[at], load_sems.at[at])
            for at, piece_ref in enumerate(piece_refs)
        ]
        for load in loads:
            load.start()
        for at, quarters, side in spots:
            loads[at].wait()
            for half, quarter in enumerate(quarters):
                for order, offset in enumerate(place.offsets):
                    pltpu.make_async_copy(
                        held.at[at, half * line + order],
                        out_ref.at[quarter, along ^ offset, side],
                        store_sem,
                    ).start()
        pltpu.make_async_copy(out_ref, out_ref, store_sem).wait()

    gathered = pl.pallas_call(
        kernel,
        out_shape=jax.ShapeDtypeStruct((4, line, 2, rows, cols), pieces[0].dtype),
        grid_spec=pltpu.PrefetchScalarGridSpec(
            num_scalar_prefetch=1,
            grid=(1,),
            in_specs=[pl.BlockSpec(memory_space=pltpu.HBM)] * 4,
            out_specs=pl.BlockSpec(memory_space=pltpu.HBM),
            scratch_shapes=[
                pltpu.VMEM((4, twice, rows, cols), pieces[0].dtype),
                pltpu.SemaphoreType.DMA((4,)),
                pltpu.SemaphoreType.DMA(()),
            ],
        ),
        compiler_params=pltpu.CompilerParams(vmem_limit_bytes=(2 << 20) + 8 * twice * cols * (-(-rows // 8) * 8)),
        name="assemble",
    )(flags, *pieces)
    return gathered.reshape(8 * line * rows, cols)


def product_half(left, right):
    half = right.shape[1] // 2

    def half_of(side):
        return matmul_tn(left, lax.dynamic_slice_in_dim(right, side * half, half, 1))

    return half_of


def column_half(array):
    half = array.shape[1] // 2
    return lambda side: lax.dynamic_slice_in_dim(array, side * half, half, 1)


def scatter_halves(place, table, spots, rows):
    words, width = table.shape
    half = words // 2
    each = half // place.count
    length = rows.shape[0]
    flag = place.core.astype(jnp.int32).reshape(1)

    def kernel(spots_ref, flag_ref, table_ref, rows_ref, send_ref, keep_ref, held, load_sem, sems):
        for owner in range(place.count):
            for side in range(2):
                pltpu.make_async_copy(
                    table_ref.at[pl.ds((2 * owner + side) * each, each)],
                    held.at[pl.ds(side * half + owner * each, each)],
                    load_sem,
                ).start()
        pltpu.make_async_copy(table_ref, held, load_sem).wait()

        def step(at, unused):
            for more in range(16):
                place_at = pl.ds(spots_ref[at * 16 + more], 1)
                held[place_at, :] += rows_ref[pl.ds(at * 16 + more, 1), :]
            return unused

        lax.fori_loop(0, length // 16, step, 0)
        core = flag_ref[0]
        first = pltpu.make_async_copy(held.at[pl.ds((1 - core) * half, half)], send_ref, sems.at[0])
        second = pltpu.make_async_copy(held.at[pl.ds(core * half, half)], keep_ref, sems.at[1])
        first.start()
        second.start()
        first.wait()
        second.wait()

    return pl.pallas_call(
        kernel,
        out_shape=[jax.ShapeDtypeStruct((half, width), jnp.float32)] * 2,
        grid_spec=pltpu.PrefetchScalarGridSpec(
            num_scalar_prefetch=2,
            grid=(1,),
            in_specs=[
                pl.BlockSpec(memory_space=pltpu.HBM),
                pl.BlockSpec((length, width), lambda step, spots, flag: (0, 0)),
            ],
            out_specs=[pl.BlockSpec(memory_space=pltpu.HBM)] * 2,
            scratch_shapes=[
                pltpu.VMEM((words, width), jnp.float32),
                pltpu.SemaphoreType.DMA(()),
                pltpu.SemaphoreType.DMA((2,)),
            ],
        ),
        compiler_params=pltpu.CompilerParams(vmem_limit_bytes=48 << 20),
        name="scatter_halves",
    )(spots, flag, table, rows)


def join(held, arrived):
    return jnp.concatenate([held, arrived], 0)


class Reduction:
    def __init__(self, place, kept, across, axis=1, exact=False, short=0):
        self.place, self.axis, self.exact, self.short = place, axis, exact, short
        self.rows = [piece.shape[0] // place.count for piece in kept]
        shapes = [
            (4, place.line // 2, 2, 2 * rows, piece.shape[1]) for rows, piece in zip(self.rows, kept)
        ]
        kept = [piece.reshape(shape) for piece, shape in zip(kept, shapes)]
        across = [piece.reshape(shape) for piece, shape in zip(across, shapes)]
        if axis == 1:
            self.parts = [(own, came, own.shape[4], 0) for own, came in zip(kept, across)]
        else:
            self.parts = [
                (own, came, TILE, block)
                for own, came in zip(kept, across)
                for block in range(own.shape[4] // TILE)
            ]
            self.rows = [own.shape[3] // 2 for own, unused, cols, block in self.parts]
        self.cols = [part[2] for part in self.parts]
        if axis == 1:
            self.span = (2 * self.rows[0], sum(self.cols))
        else:
            self.span = (2 * sum(self.rows), self.cols[0])
        self.level = 0

    def where(self, at):
        if self.axis == 1:
            start = sum(self.cols[:at])
            return slice(0, self.span[0]), slice(start, start + self.cols[at])
        start = 2 * sum(self.rows[:at])
        return slice(start, start + 2 * self.rows[at]), slice(0, self.span[1])

    def lower(self, at, value):
        if self.exact and at == len(self.cols) - 1:
            last = value[..., : TILE // 2]
            rounded = last.astype(jnp.bfloat16).astype(jnp.float32)
            value = jnp.concatenate([rounded, last - rounded], -1)
        return value.astype(jnp.bfloat16)

    def lift(self, at, value):
        value = value.astype(jnp.float32)
        if self.exact and at == len(self.cols) - 1:
            rounded, rest = value[..., : TILE // 2], value[..., TILE // 2 :]
            value = jnp.concatenate([rounded + rest, jnp.zeros_like(rest)], -1)
        return value

    def cast(self, at, value, ref):
        return self.lower(at, value) if ref.dtype == jnp.bfloat16 else value

    def took(self, at, value):
        return self.lift(at, value) if value.dtype == jnp.bfloat16 else value

    def call(self, name, kernel, steps, flags, inputs, outputs):
        return pl.pallas_call(
            kernel,
            out_shape=[entry for entry, unused, index in outputs],
            grid_spec=pltpu.PrefetchScalarGridSpec(
                num_scalar_prefetch=1,
                grid=(steps,),
                in_specs=[pl.BlockSpec(block, index) for unused, block, index in inputs],
                out_specs=[pl.BlockSpec(block, index) for unused, block, index in outputs],
            ),
            compiler_params=pltpu.CompilerParams(vmem_limit_bytes=40 << 20),
            name=name,
        )(jnp.stack(flags).astype(jnp.int32), *[array for array, unused, index in inputs])

    def pieces(self, block, index):
        entries = []
        for kept, across, cols, place in self.parts:

            def at_place(step, flags, place=place):
                return index(step, flags) + (place,)

            for array in (kept, across):
                entries.append((array, block + (array.shape[3], cols), at_place))
        return entries

    def to_a(self):
        square, line = self.place.square, self.place.line
        count = len(self.cols)

        def kernel(flags_ref, *refs):
            out_ref = refs[-1]
            for at in range(count):
                rows, cols = self.where(at)
                value = refs[2 * at][0] + refs[2 * at + 1][0]
                out_ref[0, :, :, rows, cols] = self.lower(at, value)

        shape = (2, line // 2, 2) + self.span
        (result,) = self.call(
            "reduce_first",
            kernel,
            2,
            [square ^ self.place.step_a, square ^ 3],
            self.pieces((1, line // 2, 2), lambda step, flags: (flags[step], 0, 0, 0)),
            [
                (
                    jax.ShapeDtypeStruct(shape, jnp.bfloat16),
                    (1,) + shape[1:],
                    lambda step, flags: (step, 0, 0, 0, 0),
                )
            ],
        )
        return result

    def came_a(self, refs, at, index):
        rows, cols = self.where(at)
        if len(self.from_a) > 1:
            return self.lift(at, refs[at][index + (slice(None), slice(None))])
        return self.lift(at, refs[0][index + (rows, cols)])

    def to_b(self, from_a):
        self.from_a = from_a
        line, count = self.place.line, len(self.cols)

        def kernel(flags_ref, *refs):
            out_ref, firsts = refs[-1], refs[2 * count : -1]
            for at in range(count):
                rows, cols = self.where(at)
                value = refs[2 * at][0] + refs[2 * at + 1][0]
                value = value + self.came_a(firsts, at, (0, slice(None), slice(None)))
                out_ref[:, :, rows, cols] = self.lower(at, value)

        shape = (line // 2, 2) + self.span
        (result,) = self.call(
            "reduce_second",
            kernel,
            1,
            [self.place.square ^ self.place.step_b],
            self.pieces((1, line // 2, 2), lambda step, flags: (flags[0], 0, 0, 0))
            + [
                (array, (1,) + array.shape[1:], lambda step, flags: (1, 0, 0, 0, 0))
                for array in from_a
            ],
            [(jax.ShapeDtypeStruct(shape, jnp.bfloat16), shape, lambda step, flags: (0, 0, 0, 0))],
        )
        return result

    def halves(self, lines):
        self.level += 1
        kinds = (jnp.bfloat16 if self.level <= self.short else jnp.float32, jnp.float32)
        shape = (lines,) + self.span
        return [
            (jax.ShapeDtypeStruct(shape, kind), shape, lambda step, flags: (0, 0, 0))
            for kind in kinds
        ]

    def to_line(self, from_b):
        line, count = self.place.line, len(self.cols)
        mine = self.place.along % 2
        self.along = self.place.along // 2

        def kernel(flags_ref, *refs):
            firsts, second_ref = refs[2 * count : -3], refs[-3]
            for step, out_ref in enumerate(refs[-2:]):

                @pl.when(pl.program_id(0) == step)
                def _():
                    for at in range(count):
                        rows, cols = self.where(at)
                        value = refs[2 * at][0, :, 0] + refs[2 * at + 1][0, :, 0]
                        value = value + self.came_a(firsts, at, (0, slice(None), 0))
                        value = value + self.lift(at, second_ref[:, 0, rows, cols])
                        out_ref[:, rows, cols] = self.cast(at, value, out_ref)

        send, self.own = self.call(
            "reduce_third",
            kernel,
            2,
            [self.place.square, 1 - mine, mine],
            self.pieces((1, line // 2, 1), lambda step, flags: (flags[0], 0, flags[1 + step], 0))
            + [
                (
                    array,
                    (1, line // 2, 1) + array.shape[3:],
                    lambda step, flags: (0, 0, flags[1 + step], 0, 0),
                )
                for array in self.from_a
            ]
            + [
                (
                    from_b,
                    (line // 2, 1) + self.span,
                    lambda step, flags: (0, flags[1 + step], 0, 0),
                )
            ],
            self.halves(line // 2),
        )
        return send

    def next_line(self, came):
        lines, count = self.own.shape[0] // 2, len(self.cols)
        mine = self.along % 2
        self.along = self.along // 2
        entries = [
            (
                array.reshape((lines, 2) + self.span),
                (lines, 1) + self.span,
                lambda step, flags: (0, flags[step], 0, 0),
            )
            for array in (self.own, came)
        ]

        def kernel(flags_ref, own_ref, came_ref, *out_refs):
            for step, out_ref in enumerate(out_refs):

                @pl.when(pl.program_id(0) == step)
                def _():
                    for at in range(count):
                        rows, cols = self.where(at)
                        value = own_ref[:, 0, rows, cols] + self.took(at, came_ref[:, 0, rows, cols])
                        out_ref[:, rows, cols] = self.cast(at, value, out_ref)

        send, self.own = self.call(
            "reduce_line", kernel, 2, [1 - mine, mine], entries, self.halves(lines)
        )
        return send

    def to_end(self, came):
        half, count = (self.span[0] // 2, self.span[1]), len(self.cols)

        def kernel(flags_ref, own_ref, came_ref, send_ref, keep_ref, squares_ref):
            first = flags_ref[0] == 0
            if came_ref.dtype == jnp.bfloat16 and self.exact:
                pieces = [self.took(at, came_ref[(0,) + self.where(at)]) for at in range(count)]
                came = jnp.concatenate(pieces, self.axis)
            else:
                came = came_ref[0].astype(jnp.float32)
            value = own_ref[0] + came
            squared = value * value
            if self.exact:
                spot_row = lax.broadcasted_iota(jnp.int32, squared.shape, 0)
                spot_lane = lax.broadcasted_iota(jnp.int32, squared.shape, 1)
                aside = (spot_lane == 3) & (spot_row >= self.span[0] - 2 * self.rows[-1])
                squared = jnp.where(aside & first, 0.0, squared)
            squares_ref[...] = jnp.full(squares_ref.shape, jnp.sum(squared), jnp.float32)
            groups = [self.rows[0]] if self.axis == 1 else self.rows
            start = 0
            for rows in groups:
                low, high = value[2 * start : 2 * start + rows], value[2 * start + rows : 2 * start + 2 * rows]
                send_ref[start : start + rows] = jnp.where(first, high, low)
                keep_ref[start : start + rows] = jnp.where(first, low, high)
                start += rows

        whole = (1,) + self.span
        send, self.last, self.squares = self.call(
            "reduce_last",
            kernel,
            1,
            [self.place.core],
            [(array, whole, lambda step, flags: (0, 0, 0)) for array in (self.own, came)],
            [
                (jax.ShapeDtypeStruct(shape, jnp.float32), shape, lambda step, flags: (0, 0))
                for shape in (half, half, (8, TILE))
            ],
        )
        return send

    def unpack(self, array):
        results, start = [], 0
        for size in self.cols if self.axis == 1 else self.rows:
            results.append(lax.slice_in_dim(array, start, start + size, axis=self.axis))
            start += size
        return results

    def finish(self, came):
        return self.unpack(self.last), self.unpack(came)


def in_order(place, kept, came, axis):
    return jnp.where(
        place.core == 0,
        jnp.concatenate([kept, came], axis),
        jnp.concatenate([came, kept], axis),
    )


def on_device(
    token_ids,
    segment_ids,
    live,
    timesteps,
    noise,
    embedding,
    embedding_moment,
    embedding_second,
    up_weight,
    up_moment,
    up_second,
    time_weight,
    time_moment,
    time_second,
    qkv_weight,
    qkv_moment,
    qkv_second,
    out_weight,
    out_moment,
    out_second,
    fc_weight,
    fc_moment,
    fc_second,
    proj_weight,
    proj_moment,
    proj_second,
    down_weight,
    down_moment,
    down_second,
    norm_gains,
    gains_moment,
    gains_second,
):
    masters = (
        embedding,
        up_weight,
        time_weight,
        qkv_weight,
        out_weight,
        fc_weight,
        proj_weight,
        down_weight,
        norm_gains,
    )
    moments = (
        embedding_moment,
        up_moment,
        time_moment,
        qkv_moment,
        out_moment,
        fc_moment,
        proj_moment,
        down_moment,
        gains_moment,
    )
    seconds = (
        embedding_second,
        up_second,
        time_second,
        qkv_second,
        out_second,
        fc_second,
        proj_second,
        down_second,
        gains_second,
    )
    place = Place(lax.axis_size("bucket"), lax.axis_size("dp"))
    buckets = place.buckets
    step_span = STEPS_T // buckets
    tokens = token_ids[0]
    step_row = timesteps[0]
    live_float = live[0].astype(jnp.float32)
    onehot = (
        (step_row // step_span)[:, None] == jnp.arange(buckets, dtype=jnp.int32)[None, :]
    ).astype(jnp.float32)
    count_own = jnp.sum(live_float[:, None] * onehot, 0)
    count_high = jnp.floor(count_own / 32.0)
    aside = jnp.concatenate([count_high, count_own - 32.0 * count_high]).astype(jnp.bfloat16)
    low = [member.astype(jnp.bfloat16) for member in masters]
    own_rows = low[3].shape[0]
    gains_pad = jnp.concatenate(
        [
            low[8].T,
            jnp.zeros((own_rows, EMB - 3), jnp.bfloat16),
        ],
        1,
    )
    model_width = low[3].shape[1] // 3
    ff_width = low[5].shape[1]

    table = low[0][None]
    entry = jnp.concatenate([low[1].T, low[2].T, gains_pad], 1)[None]
    qkv = low[3][None]
    aside_pad = jnp.pad(aside[None, :], ((0, own_rows - 1), (0, EMB - 2 * buckets)))
    leave = jnp.concatenate([low[4].T, low[5], low[6].T, low[7], aside_pad], 1)[None]
    fraction = step_row.astype(jnp.float32) / STEPS_T
    alpha_bar = 1.0 - jnp.sqrt(fraction + 0.0001)
    keep_root = jnp.sqrt(alpha_bar)[:, None]
    seg_col = jnp.broadcast_to(segment_ids.T, (segment_ids.shape[1], TILE))
    windows = key_windows(segment_ids[0])
    down_bits = place.bits[::-1]

    for bit in down_bits[:-1]:
        table = join(table, place.swap_line(table, bit))
        entry = join(entry, place.swap_line(entry, bit))
        table, entry, windows = tie(table, entry, windows)
    table = join(table, place.swap_line(table, down_bits[-1]))
    entry = join(entry, place.swap_line(entry, down_bits[-1]))
    for bit in down_bits[:-1]:
        entry, qkv = tie(entry, qkv)
        qkv = join(qkv, place.swap_line(qkv, bit))
    table, entry, qkv = tie(table, entry, qkv)
    table_came, entry_came = place.swap_a(table), place.swap_a(entry)
    table_came, entry_came, qkv, leave, step_row = tie(
        table_came, entry_came, qkv, leave, step_row
    )
    feature_low = sinusoid(step_row, D).astype(jnp.bfloat16)
    table, entry = join(table, table_came), join(entry, entry_came)
    table_pieces = [table, place.swap_b(table), place.swap_core(table)]
    entry_pieces = [entry, place.swap_b(entry), place.swap_core(entry)]
    qkv_came = place.swap_line(qkv, down_bits[-1])
    for bit in down_bits[:-2]:
        leave = join(leave, place.swap_line(leave, bit))
    leave_came = place.swap_line(leave, down_bits[-2])
    (qkv_came,) = tie(qkv_came)
    qkv = join(qkv, qkv_came)
    *both, qkv, feature_low = tie(*table_pieces, *entry_pieces, qkv, feature_low)
    table_pieces, entry_pieces = both[:3], both[3:]
    table_pieces.append(place.swap_core(table_pieces[1]))
    entry_pieces.append(place.swap_core(entry_pieces[1]))
    qkv_came = place.swap_a(qkv)
    entry_low = assemble(place, entry_pieces)
    entry_low, qkv_came = tie(entry_low, qkv_came)
    qkv = join(qkv, qkv_came)
    entry_low, leave_came, qkv = tie(entry_low, leave_came, qkv)
    leave = join(leave, leave_came)
    leave_came = place.swap_line(leave, down_bits[-1])
    qkv_pieces = [qkv, place.swap_b(qkv), place.swap_core(qkv)]
    qkv, table_pieces[0] = tie(qkv, table_pieces[0])
    word_table = assemble(place, table_pieces)
    word_table, leave_came = tie(word_table, leave_came)
    leave = join(leave, leave_came)
    leave_came = place.swap_a(leave)
    up_low = entry_low[:, :EMB]
    time_low = entry_low[:, EMB : EMB + model_width]
    gain_rows = entry_low[:, EMB + model_width :][:, :3].T.astype(jnp.float32)

    table_size = jnp.max(jnp.sum(jnp.square(word_table.astype(jnp.float32)), 1))

    start_emb = word_table[tokens].astype(jnp.float32)
    noisy_emb = keep_root * start_emb + jnp.sqrt(1.0 - alpha_bar)[:, None] * noise[0]
    noisy_low = noisy_emb.astype(jnp.bfloat16)
    hidden_zero = matrix_product_transposed(noisy_low, up_low) + matrix_product_transposed(
        feature_low, time_low
    )
    normed, scaled_one, inverse_one = layer_normalize(hidden_zero, gain_rows[0])
    normed_one_low = normed.astype(jnp.bfloat16)
    *qkv_pieces, normed_one_low = tie(*qkv_pieces, normed_one_low)
    qkv_pieces.append(place.swap_core(qkv_pieces[1]))
    qkv_low = assemble(place, qkv_pieces)
    leave_came, qkv_low = tie(leave_came, qkv_low)
    leave = join(leave, leave_came)
    leave_pieces = [leave, place.swap_b(leave), place.swap_core(leave)]
    mixed_low = matmul(normed_one_low, qkv_low).astype(jnp.bfloat16)
    segments = (segment_ids, seg_col, windows)
    attended_low, log_sums = attention_forward(mixed_low, *segments)
    *leave_pieces, attended_low = tie(*leave_pieces, attended_low)
    leave_pieces.append(place.swap_core(leave_pieces[1]))
    leave_low = assemble(place, leave_pieces)
    out_low = leave_low[:, :model_width]
    fc_low = leave_low[:, model_width : model_width + ff_width]
    proj_low = leave_low[:, model_width + ff_width : model_width + 2 * ff_width]
    down_low = leave_low[:, model_width + 2 * ff_width : model_width + 2 * ff_width + EMB]
    shares = leave_low[:, model_width + 2 * ff_width + EMB :]
    shares = shares.reshape(place.count, own_rows, EMB)[:, 0, : 2 * buckets]
    count_sums = jnp.sum(shares.astype(jnp.float32), 0)
    counts = 32.0 * count_sums[:buckets] + count_sums[buckets:]
    token_weight = live_float * jnp.sum(onehot / counts[None, :], -1) / buckets
    hidden_one = hidden_zero + matrix_product_transposed(attended_low, out_low)
    normed, scaled_two, inverse_two = layer_normalize(hidden_one, gain_rows[1])
    normed_two_low = normed.astype(jnp.bfloat16)
    active, slope = gelu_and_slope(matmul(normed_two_low, fc_low))
    active_low, slope = tie(active.astype(jnp.bfloat16), slope)
    hidden_two = hidden_one + matrix_product_transposed(active_low, proj_low)
    normed, scaled_top, inverse_top = layer_normalize(hidden_two, gain_rows[2])
    normed_top_low = normed.astype(jnp.bfloat16)
    prediction = matmul(normed_top_low, down_low)
    pred_low = prediction.astype(jnp.bfloat16)
    size = jnp.sqrt(jnp.max(jnp.sum(jnp.square(prediction), 1)) * table_size)
    small = (size < 40.0).astype(jnp.int32).reshape(1)
    grad_table_head, grad_pred_head, log_total = head_pass(
        pred_low, word_table, token_weight[None, :], small
    )

    pred_float = pred_low.astype(jnp.float32)
    target = jnp.sum(pred_float * start_emb, -1)
    cross_loss = log_total[0] - target
    target_prob = jnp.exp(target - log_total[0])
    target_shift = lax.reduce_precision(
        token_weight * (target_prob - 1.0), 8, 7
    ) - lax.reduce_precision(token_weight * target_prob, 8, 7)
    target_shift = target_shift[:, None]
    pred_gap = prediction - start_emb
    loss_local = jnp.sum(token_weight * (jnp.mean(pred_gap * pred_gap, -1) + cross_loss))
    grad_mse = token_weight[:, None] * 2.0 * pred_gap / EMB
    grad_pred_low = (grad_mse + grad_pred_head.T + target_shift * start_emb).astype(jnp.bfloat16)
    grad_down = matmul_tn(normed_top_low, grad_pred_low)
    grad_two, grad_gain_top = norm_back(
        matrix_product_transposed(grad_pred_low, down_low), scaled_top, inverse_top, gain_rows[2]
    )

    bits = list(place.bits)
    core = place.core
    grad_two_low = grad_two.astype(jnp.bfloat16)
    proj_half = product_half(grad_two_low, active_low)
    proj_send, grad_two_low = tie(proj_half(1 - core), grad_two_low)
    proj_came = place.swap_core(proj_send)
    proj_kept = proj_half(core)
    grad_upper_low = (slope * matmul(grad_two_low, proj_low)).astype(jnp.bfloat16)
    proj_came, grad_upper_low = tie(proj_came, grad_upper_low)
    proj = Reduction(place, [proj_kept], [proj_came])
    proj_send, grad_upper_low = tie(proj.to_a(), grad_upper_low)
    proj_a = place.swap_a(proj_send)
    fc_half = product_half(normed_two_low, grad_upper_low)
    fc_send, grad_upper_low = tie(fc_half(1 - core), grad_upper_low)
    fc_came = place.swap_core(fc_send)
    fc_kept = fc_half(core)
    grad_normed_two = matrix_product_transposed(grad_upper_low, fc_low)
    back_two, grad_gain_two = norm_back(grad_normed_two, scaled_two, inverse_two, gain_rows[1])
    grad_one = grad_two + back_two
    grad_one_low = grad_one.astype(jnp.bfloat16)
    proj_a, fc_came, grad_one_low = tie(proj_a, fc_came, grad_one_low)
    fc = Reduction(place, [fc_kept], [fc_came])
    fc_send, grad_one_low = tie(fc.to_a(), grad_one_low)
    fc_a = place.swap_a(fc_send)
    out_half = product_half(grad_one_low, attended_low)
    out_send, out_kept = out_half(1 - core), out_half(core)
    grad_attended = matmul(grad_one_low, out_low).astype(jnp.bfloat16)
    lanes = lax.broadcasted_iota(jnp.int32, (model_width, TILE), 1)
    exact = jnp.where(lanes == 1, grad_gain_two[:, None], 0.0)
    exact = jnp.where(lanes == 2, grad_gain_top[:, None], exact)
    exact = jnp.where(lanes == 3, loss_local, exact)
    out_send, out_kept, exact, grad_attended = tie(out_send, out_kept, exact, grad_attended)
    out_came = place.swap_core(out_send)
    grad_mixed = attention_backward(mixed_low, grad_attended, log_sums, *segments)

    fc_a, out_came, grad_mixed = tie(fc_a, out_came, grad_mixed)
    feed = Reduction(place, [proj_kept, fc_kept], [proj_came, fc_came], short=len(bits))
    feed_send, grad_mixed = tie(feed.to_b([proj_a, fc_a]), grad_mixed)
    feed_came = place.swap_b(feed_send)
    qkv_half = product_half(normed_one_low, grad_mixed)
    qkv_send, grad_mixed = tie(qkv_half(1 - core), grad_mixed)
    qkv_came = place.swap_core(qkv_send)
    grad_normed_one = matrix_product_transposed(grad_mixed, qkv_low)
    back_one, grad_gain_one = norm_back(grad_normed_one, scaled_one, inverse_one, gain_rows[0])
    grad_zero = grad_one + back_one
    feed_came, grad_zero = tie(feed_came, grad_zero)
    feed_send, grad_zero = tie(feed.to_line(feed_came), grad_zero)
    feed_came = place.swap_line(feed_send, bits[0])
    grad_zero_low = grad_zero.astype(jnp.bfloat16)
    grad_start = matmul(grad_zero_low, up_low)
    grad_start = keep_root * grad_start - grad_mse + target_shift * pred_float
    qkv_kept, qkv_came, grad_start = tie(qkv_half(core), qkv_came, grad_start)
    mix = Reduction(place, [out_kept, qkv_kept], [out_came, qkv_came], short=1)
    mix_send, grad_start = tie(mix.to_a(), grad_start)
    mix_came = place.swap_a(mix_send)

    own_words = word_table.shape[0] // place.count // 2
    if own_words % 8 == 0:
        owner, spot = tokens // (2 * own_words), tokens % (2 * own_words)
        spot = (spot // own_words * place.count + owner) * own_words + spot % own_words
        words_send, words_kept = scatter_halves(place, grad_table_head, spot, grad_start)
    else:
        grad_table = grad_table_head.at[tokens].add(grad_start)
        split = grad_table.reshape(place.count, 2, own_words, EMB)
        words_send, words_kept = [
            lax.dynamic_index_in_dim(split, side, 1, False).reshape(-1, EMB)
            for side in (1 - core, core)
        ]
    words_send, mix_came, feed_came, grad_zero_low = tie(
        words_send, mix_came, feed_came, grad_zero_low
    )
    words_came = place.swap_core(words_send)
    feed_send, mix_send, grad_zero_low = tie(
        feed.next_line(feed_came), mix.to_b([mix_came]), grad_zero_low
    )
    feed_came, mix_came = place.swap_line(feed_send, bits[1]), place.swap_b(mix_send)
    time_half = product_half(grad_zero_low, feature_low)
    grad_up = matmul_tn(grad_zero_low, noisy_low)
    exact = jnp.where(lanes == 0, grad_gain_one[:, None], exact)

    def rest_half(side):
        first = side == 0
        return time_half(side), jnp.where(first, grad_up, grad_down), jnp.where(first, exact, 0.0)

    rest_send = tie(*rest_half(1 - core))
    rest_came = [place.swap_core(piece) for piece in rest_send]
    rest_kept = rest_half(core)
    words_came, *rest_came = tie(words_came, *rest_came)
    late = Reduction(
        place, [words_kept, *rest_kept], [words_came, *rest_came], axis=0, exact=True
    )
    late_send, mix_came = tie(late.to_a(), mix_came)
    late_came = place.swap_a(late_send)
    mix_came = place.swap_line(mix.to_line(mix_came), bits[0])
    late_came, mix_came, feed_came = tie(late_came, mix_came, feed_came)
    late_send, mix_send = tie(late.to_b([late_came]), mix.next_line(mix_came))
    late_came, mix_came = place.swap_b(late_send), place.swap_line(mix_send, bits[1])
    (late_came,) = tie(late_came)
    late_came = place.swap_line(late.to_line(late_came), bits[0])
    late_came, mix_came = tie(late_came, mix_came)
    late_came = place.swap_line(late.next_line(late_came), bits[1])
    members, arrived = (feed, mix, late), [feed_came, mix_came, late_came]
    for bit in bits[2:]:
        arrived = [
            place.swap_line(member.next_line(came), bit) for member, came in zip(members, arrived)
        ]
    ends = [
        member.finish(place.swap_core(member.to_end(came))) for member, came in zip(members, arrived)
    ]
    squares_local = feed.squares + mix.squares + late.squares
    (proj_end, fc_end), (out_end, qkv_end), (words_end, *rest_ends) = [
        list(zip(*end)) for end in ends
    ]
    time_end = [jnp.concatenate(sides[:-2], 1) for sides in zip(*rest_ends)]
    pair_end, exact_end = rest_ends[-2:]
    shard_pair = in_order(place, *pair_end, 1)
    shard_exact = jnp.where(core == 0, *exact_end)
    loss_sum = shard_exact[0, 3]
    shards = (
        in_order(place, *words_end, 0),
        shard_pair[:, :EMB],
        in_order(place, *time_end, 1),
        in_order(place, *qkv_end, 1),
        in_order(place, *out_end, 1),
        in_order(place, *fc_end, 1),
        in_order(place, *proj_end, 1),
        shard_pair[:, EMB:],
        shard_exact[:, :3].T,
    )
    squares, shards = place.total(squares_local, shards)
    squares = squares[0, 0]
    grad_norm = jnp.sqrt(squares)
    factor = CLIP_NORM / jnp.maximum(grad_norm, CLIP_NORM)
    flips = (False, True, True, False, True, False, True, False, False)

    def lay(members):
        return [member.T if flip else member for member, flip in zip(members, flips)]

    results = adam_update(factor, lay(masters), lay(moments), lay(seconds), shards)
    results = [result.T if flips[at // 3] else result for at, result in enumerate(results)]
    return (
        loss_sum,
        grad_norm,
        results[0],
        results[1],
        results[2],
        results[3],
        results[4],
        results[5],
        results[6],
        results[7],
        results[8],
        results[9],
        results[10],
        results[11],
        results[12],
        results[13],
        results[14],
        results[15],
        results[16],
        results[17],
        results[18],
        results[19],
        results[20],
        results[21],
        results[22],
        results[23],
        results[24],
        results[25],
        results[26],
    )


def solution(mesh):
    return jax.shard_map(
        on_device,
        mesh=mesh,
        in_specs=(
            P(("bucket", "dp"), None),
            P(("bucket", "dp"), None),
            P(("bucket", "dp"), None),
            P(("bucket", "dp"), None),
            P(("bucket", "dp"), None, None),
            P(("bucket", "dp"), None),
            P(("bucket", "dp"), None),
            P(("bucket", "dp"), None),
            P(None, ("bucket", "dp")),
            P(None, ("bucket", "dp")),
            P(None, ("bucket", "dp")),
            P(None, ("bucket", "dp")),
            P(None, ("bucket", "dp")),
            P(None, ("bucket", "dp")),
            P(("bucket", "dp"), None),
            P(("bucket", "dp"), None),
            P(("bucket", "dp"), None),
            P(None, ("bucket", "dp")),
            P(None, ("bucket", "dp")),
            P(None, ("bucket", "dp")),
            P(("bucket", "dp"), None),
            P(("bucket", "dp"), None),
            P(("bucket", "dp"), None),
            P(None, ("bucket", "dp")),
            P(None, ("bucket", "dp")),
            P(None, ("bucket", "dp")),
            P(("bucket", "dp"), None),
            P(("bucket", "dp"), None),
            P(("bucket", "dp"), None),
            P(None, ("bucket", "dp")),
            P(None, ("bucket", "dp")),
            P(None, ("bucket", "dp")),
        ),
        out_specs=(
            P(),
            P(),
            P(("bucket", "dp"), None),
            P(("bucket", "dp"), None),
            P(("bucket", "dp"), None),
            P(None, ("bucket", "dp")),
            P(None, ("bucket", "dp")),
            P(None, ("bucket", "dp")),
            P(None, ("bucket", "dp")),
            P(None, ("bucket", "dp")),
            P(None, ("bucket", "dp")),
            P(("bucket", "dp"), None),
            P(("bucket", "dp"), None),
            P(("bucket", "dp"), None),
            P(None, ("bucket", "dp")),
            P(None, ("bucket", "dp")),
            P(None, ("bucket", "dp")),
            P(("bucket", "dp"), None),
            P(("bucket", "dp"), None),
            P(("bucket", "dp"), None),
            P(None, ("bucket", "dp")),
            P(None, ("bucket", "dp")),
            P(None, ("bucket", "dp")),
            P(("bucket", "dp"), None),
            P(("bucket", "dp"), None),
            P(("bucket", "dp"), None),
            P(None, ("bucket", "dp")),
            P(None, ("bucket", "dp")),
            P(None, ("bucket", "dp")),
        ),
        check_vma=False,
    )
```
